32 devices in a mesh: group: 2 (over y), seq: 4 (over z), rep: 4 (over x, core).
Axes of the slice: x: 2, y: 2, z: 4, core: 2. Of those that a mesh axis runs over, the one named last changes fastest.
Arguments:
- queries: bfloat16 [8, 1024, 1024], P(('group', 'rep'), 'seq'), parts along dimension 0, may hold values from -6 to 6
- keys: bfloat16 [8, 1024, 1024], P(('group', 'rep'), 'seq'), parts along dimension 0, may hold values from -6 to 6
- values: bfloat16 [8, 1024, 1024], P(('group', 'rep'), 'seq'), parts along dimension 0, may hold values from -6 to 6
- stream: bfloat16 [8, 1024, 1024], P(('group', 'rep'), 'seq'), parts along dimension 0, may hold values from -6 to 6
- attn_gain: float32 [1024], replicated, may hold values from 0.5 to 1.5
- moe_gain: float32 [1024], replicated, may hold values from 0.5 to 1.5
- expert_ids: int32 [8, 1024, 2], P(('group', 'rep'), 'seq'), parts along dimension 0, may hold values from 0 to 3, all different within a row; in each aligned block of 256 rows (0 to 255, 256 to 511, ..., all dimensions but the last counted through in order) at most 192 rows name the same one
- gate_weights: float32 [8, 1024, 2], P(('group', 'rep'), 'seq'), parts along dimension 0, may hold values from 0.1 to 1
- w_gate: bfloat16 [4, 1024, 512], P('seq'), may hold values from -0.1875 to 0.1875
- w_up: bfloat16 [4, 1024, 512], P('seq'), may hold values from -0.1875 to 0.1875
- w_down: bfloat16 [4, 512, 1024], P('seq'), may hold values from -0.25 to 0.25
Outputs:
- mixed: bfloat16 [8, 1024, 1024], P(('group', 'rep'), 'seq'), parts along dimension 0
The draws below stay inside these ranges and needn't reach their ends.
There are 2 independent parts, one for each index of `group`. The reference program is written for one: setup_inputs(seed, part) draws one part's arguments, and reference() takes and returns one part's arrays. A program takes and returns all parts, laid end to end along the dimension named above; an argument that names none is the same for every part. Nothing has to cross between parts.
Inputs may be any that keep to these rules, and one draw needn't show every extreme that they name: `expert_ids`: each position names two different experts; within each aligned block of 256 positions (the rows of one device) no expert is named more than 192 times, a bound that some block reaches.
All inputs are finite; a program needn't handle non-finite values.
Results may differ from the reference program's by a relative error of at most 0.0085.
Values may be sent and summed in bfloat16 or wider, within the bound.
A program may use at most 64 MiB of HBM per device.

```python
import math
import jax
import jax.numpy as jnp
import numpy as np
from jax import lax

H = 8
DH = 128
HID = 512
LEN_DEV = 256
D = 1024
EXPERTS = 4
SEQS = 4
LEN = 1024
CAP = 192
N_SEQ = 4


def block_levels(rng, shape, shards, low, largest):
    loudness, own = 1.0, jax.random.fold_in(rng, 6)
    for position, shards_of in shards:
        heights = jnp.exp(jax.random.uniform(jax.random.fold_in(own, position), (shards_of,), jnp.float32, low / len(shards), largest / len(shards)))
        loudness = loudness * jnp.repeat(heights, shape[position] // shards_of).reshape([-1 if axis == position else 1 for axis in range(len(shape))])
    return loudness


def shared_out(key, own, number, rows, number_of, top, most, lean):
    order = jax.random.permutation(key, number_of)
    packed, usual = portions_of(number_of, rows * top, most, lean, True), portions_of(number_of, rows * top, most, lean, False)
    places = jnp.arange(number_of)

    def named(tallies, turn):
        used = int((tallies > 0).sum())
        fixed = max(1, used // 4)
        shifted = fixed + (places - fixed + turn * (used - fixed)) % max(1, number_of - fixed)
        return jnp.zeros((number_of,), jnp.int32).at[order[jnp.where(places < fixed, places, shifted)]].set(jnp.asarray(tallies, jnp.int32))

    tallies = jnp.where(number % 4 == 0, named(packed, number // 4), named(usual, number - number // 4 - 1))
    mixed = jax.random.permutation(jax.random.fold_in(own, 3), number_of)
    giver, sink = mixed[0:number_of // 2 * 2:2], mixed[1:number_of // 2 * 2:2]
    slack = jnp.minimum(tallies[giver] - 1, most - tallies[sink]) // 2
    slack = jnp.where((giver == order[0]) | (sink == order[0]) | (tallies[sink] == 0), 0, jnp.maximum(slack, 0))
    shifted = jax.random.randint(jax.random.fold_in(own, 4), (number_of // 2,), 0, 1 << 20) % (slack + 1)
    tallies = tallies.at[giver].add(-shifted).at[sink].add(shifted)
    members = jnp.searchsorted(jnp.cumsum(tallies), jnp.arange(rows * top), side="right").astype(jnp.int32)
    table = members.reshape(top, rows).T
    table = table[jax.random.permutation(jax.random.fold_in(own, 1), rows)]
    turn = jax.random.randint(jax.random.fold_in(own, 2), (rows, 1), 0, top)
    return jnp.take_along_axis(table, (jnp.arange(top)[None, :] + turn) % top, axis=1)


def portions_of(count, total, limit, skew, full):
    loads = [(1 << 20) // math.isqrt(rank ** skew) + 1 for rank in range(1, count + 1)]
    largest = limit if full else min(limit, max(-(-total // count), total * loads[0] // sum(loads)))
    least = 1 if total - largest >= count - 1 else 0
    holding, surplus = [largest] + [least] * (count - 1), total - largest - least * (count - 1)
    while surplus > 0:
        free = [i for i in range(1, count) if holding[i] < largest] or [i for i in range(1, count) if holding[i] < limit]
        pool, left = sum([loads[i] for i in free]), surplus
        for i in free:
            extra = min(limit - holding[i], max(1, left * loads[i] // pool), surplus)
            holding[i] = holding[i] + extra
            surplus = surplus - extra
    return np.array(holding)


def gaussian(stream_key, dims, deviation, bound, cuts=(), kind=jnp.bfloat16):
    factor_of = block_levels(stream_key, dims, cuts, -0.22, 0.18) if cuts else 1.0
    drawn = jax.random.normal(stream_key, dims, jnp.float32) * deviation * factor_of
    return jnp.minimum(jnp.maximum(drawn, -bound), bound).astype(kind)


def setup_inputs(seed: int = 0, part: int = 0) -> dict:
    key_of = jax.random.split(jax.random.key(seed), 12)
    own_keys = jax.random.split(jax.random.fold_in(key_of[11], part), 12)
    queries = gaussian(own_keys[0], (SEQS, LEN, D), 1.0, 6.0, ((0, 4), (1, 4)))
    keys = gaussian(own_keys[1], (SEQS, LEN, D), 1.0, 6.0, ((0, 4), (1, 4)))
    values = gaussian(own_keys[2], (SEQS, LEN, D), 1.0, 6.0, ((0, 4), (1, 4)))
    stream = gaussian(own_keys[3], (SEQS, LEN, D), 1.0, 6.0, ((0, 4), (1, 4)))
    attn_gain = jnp.clip(1.0 + 0.1 * jax.random.normal(key_of[4], (D,), jnp.float32), 0.5, 1.5)
    moe_gain = jnp.clip(1.0 + 0.1 * jax.random.normal(key_of[5], (D,), jnp.float32), 0.5, 1.5)
    expert_ids_keys = jax.random.split(jax.random.fold_in(own_keys[6], 1), SEQS * LEN // LEN_DEV)
    expert_ids_turns = jax.random.permutation(jax.random.fold_in(own_keys[6], 3), SEQS * LEN // LEN_DEV)
    expert_ids = jax.vmap(lambda own, number: shared_out(jax.random.fold_in(own_keys[6], 2), own, number, LEN_DEV, EXPERTS, 2, CAP, 2))(expert_ids_keys, expert_ids_turns).reshape((SEQS, LEN, 2))
    gate_weights = jnp.clip(0.1 + 0.9 * jax.random.uniform(own_keys[7], (SEQS, LEN, 2), jnp.float32) ** block_levels(own_keys[7], (SEQS, LEN, 2), ((0, 4), (1, 4)), -0.2, 0.2), 0.1, 1.0)
    w_gate = gaussian(key_of[8], (EXPERTS, D, HID), D ** -0.5, 0.1875, ((0, 4),))
    w_up = gaussian(key_of[9], (EXPERTS, D, HID), D ** -0.5, 0.1875, ((0, 4),))
    w_down = gaussian(key_of[10], (EXPERTS, HID, D), HID ** -0.5, 0.25, ((0, 4),))
    return dict(queries=queries, keys=keys, values=values, stream=stream, attn_gain=attn_gain, moe_gain=moe_gain, expert_ids=expert_ids, gate_weights=gate_weights, w_gate=w_gate, w_up=w_up, w_down=w_down)


def attend_sequence(query_seq, key_seq, value_seq):
    query_blocks = query_seq.reshape(N_SEQ, LEN_DEV, H, DH)
    key_blocks = key_seq.reshape(N_SEQ, LEN_DEV, H, DH)
    value_blocks = value_seq.reshape(N_SEQ, LEN_DEV, H, DH)
    causal = jnp.arange(LEN_DEV)[:, None] >= jnp.arange(LEN_DEV)[None, :]

    def block_step(carried, pieces):
        query_block, key_block, value_block = pieces
        query_wide = query_block.astype(jnp.float32)
        key_wide = key_block.astype(jnp.float32)
        value_wide = value_block.astype(jnp.float32)
        scores = jnp.einsum('thd,shd->hts', query_wide, key_wide)
        masked = jnp.where(causal[None], scores, jnp.zeros((), jnp.float32))
        weights = lax.optimization_barrier(masked.astype(jnp.bfloat16)).astype(jnp.float32)
        intra = jnp.einsum('hts,shd->thd', weights, value_wide)
        prefix_low = lax.optimization_barrier(carried.astype(jnp.bfloat16)).astype(jnp.float32)
        inter = jnp.einsum('thd,hde->the', query_wide, prefix_low)
        local = jnp.einsum('shd,she->hde', key_wide, value_wide)
        return (carried + local, intra + inter)
    start = jnp.zeros((H, DH, DH), jnp.float32)
    _, attended = lax.scan(block_step, start, (query_blocks, key_blocks, value_blocks))
    return attended.reshape(LEN, H, DH)

def reference(queries, keys, values, stream, attn_gain, moe_gain, expert_ids, gate_weights, w_gate, w_up, w_down):

    def one_sequence(triple):
        return attend_sequence(triple[0], triple[1], triple[2])
    attended = lax.map(one_sequence, (queries, keys, values))
    normed = attended * lax.rsqrt(lax.optimization_barrier(jnp.mean(attended * attended, axis=-1, keepdims=True)) + 1e-06)
    hidden = (stream.astype(jnp.float32) + normed.reshape(SEQS, LEN, D) * attn_gain).astype(jnp.bfloat16)
    hidden_wide = hidden.astype(jnp.float32)
    moe_in = (hidden_wide * lax.rsqrt(lax.optimization_barrier(jnp.mean(hidden_wide * hidden_wide, axis=-1, keepdims=True)) + 1e-06) * moe_gain).astype(jnp.bfloat16)
    choice_ids = expert_ids.reshape(SEQS, N_SEQ, LEN_DEV * 2).astype(jnp.int32)
    onehot = (choice_ids[..., None] == jnp.arange(EXPERTS, dtype=jnp.int32)).astype(jnp.int32)
    slot_rank = lax.optimization_barrier(jnp.sum(jnp.cumsum(onehot, axis=2) * onehot, axis=-1)) - 1
    seq_index = jnp.arange(SEQS, dtype=jnp.int32)[:, None, None]
    block_index = jnp.arange(N_SEQ, dtype=jnp.int32)[None, :, None]
    slot_key = ((choice_ids * SEQS + seq_index) * N_SEQ + block_index) * CAP + slot_rank
    slot_table = jnp.full((EXPERTS * SEQS * N_SEQ * CAP,), -1, jnp.int32)
    slot_table = slot_table.at[slot_key.reshape(-1)].set(jnp.arange(SEQS * LEN * 2, dtype=jnp.int32))
    slot_table = slot_table.reshape(EXPERTS, SEQS * N_SEQ * CAP)
    flat_in = moe_in.reshape(SEQS * LEN, D)
    gates_flat = gate_weights.reshape(-1)

    def expert_step(total, pieces):
        index_row, gate_mat, up_mat, down_mat = pieces
        valid = index_row >= 0
        safe_index = jnp.where(valid, index_row, 0)
        token_index = (safe_index // 2).astype(jnp.int32)
        rows_in = jnp.where(valid[:, None], flat_in[token_index], jnp.zeros((), jnp.bfloat16))
        gate = jnp.dot(rows_in, gate_mat, preferred_element_type=jnp.float32)
        upper = jnp.dot(rows_in, up_mat, preferred_element_type=jnp.float32)
        active = (jax.nn.silu(gate) * upper).astype(jnp.bfloat16)
        produced = jnp.dot(active, down_mat, preferred_element_type=jnp.float32).astype(jnp.bfloat16)
        scale_row = jnp.where(valid, gates_flat[safe_index], jnp.zeros((), jnp.float32))
        return (total.at[token_index].add(scale_row[:, None] * produced.astype(jnp.float32)), None)
    moe_total, _ = lax.scan(expert_step, jnp.zeros((SEQS * LEN, D), jnp.float32), (slot_table, w_gate, w_up, w_down))
    mixed = hidden_wide.reshape(SEQS * LEN, D) + moe_total
    return mixed.astype(jnp.bfloat16).reshape(SEQS, LEN, D)
```

```python
import functools

import jax
import jax.numpy as jnp
from jax import lax
from jax.experimental import pallas as pl
from jax.experimental.pallas import tpu as pltpu
from jax.sharding import PartitionSpec as P

H = 8
DH = 128
MESH = pl.DeviceIdType.MESH
GATHER_LIMIT = 24 << 20


def fused_kernel(
    n,
    q_hbm,
    k_hbm,
    v_hbm,
    s_hbm,
    attn_gain_hbm,
    moe_gain_hbm,
    ids_hbm,
    gw_hbm,
    wg_hbm,
    wu_hbm,
    wd_hbm,
    out_ref,
    qb,
    kb,
    vb,
    sb,
    attn_gain_ref,
    moe_gain_ref,
    ids,
    gw,
    wg,
    wu,
    wd,
    local,
    prefix,
    passed,
    attended,
    hidden,
    moe_in,
    total,
    load_sem,
    z_sem,
    x_sem,
    y_sem,
    fwd_sem,
    sib_sem,
    recv_sem,
    state_send,
    state_recv,
):
    g, z, r = lax.axis_index("group"), lax.axis_index("seq"), lax.axis_index("rep")
    x, c = r // 2, r % 2
    r_x, r_s = 2 * (1 - x) + c, 2 * x + (1 - c)
    mine, at_x, at_y, at_d = g * 4 + r, g * 4 + r_x, (1 - g) * 4 + r, (1 - g) * 4 + r_x
    to_x, to_y, to_s = {"rep": r_x}, {"group": 1 - g}, {"rep": r_s}
    rows = qb.shape[0]
    pieces = 8
    hbm = (wg_hbm, wu_hbm, wd_hbm)
    held = (wg, wu, wd)
    has_up, has_down = z < n - 1, z > 0
    inside = has_up & has_down

    def span(t, piece):
        size = held[t].shape[1] // pieces
        return pl.ds(pl.multiple_of(piece * size, size), size)

    def send(t, e, piece, sem, to, source=None):
        dst = held[t].at[e, span(t, piece), :]
        return pltpu.make_async_remote_copy(
            src_ref=dst if source is None else source,
            dst_ref=dst,
            send_sem=sem,
            recv_sem=recv_sem.at[piece, e, t],
            device_id=to,
            device_id_type=MESH,
        )

    def arrive(t, e, piece):
        send(t, e, piece, recv_sem.at[piece, e, t], to_s).wait_recv()

    def expert(s):
        if s == 0:
            return z
        near = jnp.minimum(z, n - 1 - z)
        offset = (s + 1) // 2
        both = jnp.where(s % 2 == 1, z - offset, z + offset)
        only = jnp.where(z < n - 1 - z, s, n - 1 - s)
        return jnp.where(s <= 2 * near, both, only)

    steps = [(expert(s), t) for s in range(1, n) for t in range(3)]

    barrier = pltpu.get_barrier_semaphore()
    for to in (to_x, to_y, to_s):
        pl.semaphore_signal(barrier, inc=1, device_id=to, device_id_type=MESH)

    @pl.when(has_up)
    def _():
        pl.semaphore_signal(barrier, inc=1, device_id={"seq": z + 1}, device_id_type=MESH)

    @pl.when(has_down)
    def _():
        pl.semaphore_signal(barrier, inc=1, device_id={"seq": z - 1}, device_id_type=MESH)

    loads = [
        pltpu.make_async_copy(src, dst, load_sem.at[i])
        for i, (src, dst) in enumerate(
            [
                (k_hbm.at[0], kb),
                (v_hbm.at[0], vb),
                (q_hbm.at[0], qb),
                (s_hbm.at[0], sb),
                (attn_gain_hbm, attn_gain_ref),
                (moe_gain_hbm, moe_gain_ref),
                (ids_hbm.at[0], ids),
                (gw_hbm.at[0], gw),
                (wg_hbm.at[0], wg.at[z]),
                (wu_hbm.at[0], wu.at[z]),
                (wd_hbm.at[0], wd.at[z]),
            ]
        )
    ]
    for load in loads[:4]:
        load.start()
    pl.semaphore_wait(barrier, 3 + (z < n - 1).astype(jnp.int32) + (z > 0).astype(jnp.int32))

    def own_up(t):
        return send(t, z, mine, z_sem.at[0, t], {"seq": z + 1}, hbm[t].at[0, span(t, mine), :])

    def own_down(t):
        return send(t, z, mine, z_sem.at[1, t], {"seq": z - 1}, hbm[t].at[0, span(t, mine), :])

    for t in range(3):

        @pl.when(has_up)
        def _():
            own_up(t).start()

        @pl.when(has_down)
        def _():
            own_down(t).start()

    for load in loads[4:]:
        load.start()

    def further(i, up):
        e, t = steps[i]
        return send(t, e, mine, z_sem.at[2 + i // 3, t], {"seq": z + 1 if up else z - 1})

    def goes_up(i):
        return (steps[i][0] < z) & has_up

    def goes_down(i):
        return (steps[i][0] > z) & has_down

    def across(i):
        e, t = steps[i]
        a, b = i // 3, t
        return (
            send(t, e, mine, x_sem.at[a, b], to_x),
            send(t, e, mine, y_sem.at[a, b], to_y),
            send(t, e, mine, sib_sem.at[0, a, b], to_s),
        )

    def relays(i):
        e, t = steps[i]
        a, b = i // 3, t
        return (
            lambda: send(t, e, at_x, fwd_sem.at[a, b], to_y),
            lambda: send(t, e, at_y, fwd_sem.at[a, b], to_x),
            lambda: send(t, e, at_x, sib_sem.at[1, a, b], to_s),
            lambda: send(t, e, at_y, sib_sem.at[2, a, b], to_s),
            lambda: send(t, e, at_d, sib_sem.at[3, a, b], to_s),
        )

    def take(i):
        e, t = steps[i]
        arrive(t, e, mine)

        @pl.when(goes_up(i))
        def _():
            further(i, True).start()

        @pl.when(goes_down(i))
        def _():
            further(i, False).start()

    def stage_z(i):
        if i < 3:
            take(i)
        else:

            @pl.when(~inside)
            def _():
                take(i)

        if i + 3 < len(steps):

            @pl.when(inside)
            def _():
                take(i + 3)

        for copy in across(i):
            copy.start()

    def stage_xy(i):
        e, t = steps[i]
        on_y, on_x, sib_x, sib_y, _ = relays(i)
        arrive(t, e, at_x)

        @pl.when((c + i) % 2 == 0)
        def _():
            on_y().start()

        sib_x().start()
        arrive(t, e, at_y)

        @pl.when((c + i) % 2 == 1)
        def _():
            on_x().start()

        sib_y().start()

    def stage_d(i):
        e, t = steps[i]
        arrive(t, e, at_d)
        relays(i)[4]().start()

    def stage_sib(i):
        e, t = steps[i]
        for g_of in range(2):
            for x_of in range(2):
                arrive(t, e, g_of * 4 + 2 * x_of + (1 - c))

    def state_copy(part, to):
        size = H // 4
        heads = pl.ds(part * size, size)
        return pltpu.make_async_remote_copy(
            src_ref=passed.at[heads],
            dst_ref=prefix.at[heads],
            send_sem=state_send.at[part],
            recv_sem=state_recv.at[part],
            device_id=to,
            device_id_type=MESH,
        )

    def state_first():
        prefix[...] = jnp.zeros_like(prefix)
        passed[...] = local[...].astype(passed.dtype)
        for part in range(4):
            state_copy(part, {"seq": z + 1}).start()

    def state_next():
        for part in range(4):
            state_copy(part, to_s).wait_recv()

            @pl.when(has_up)
            def _():
                heads = pl.ds(part * (H // 4), H // 4)
                passed[heads] = (prefix[heads].astype(jnp.float32) + local[heads]).astype(
                    passed.dtype
                )
                state_copy(part, {"seq": z + 1}).start()

    def head(h):
        return pl.ds(pl.multiple_of(h * DH, DH), DH)

    loads[0].wait()
    loads[1].wait()

    def local_state(h, carry):
        local[h] = lax.dot_general(
            kb[:, head(h)],
            vb[:, head(h)],
            (((0,), (0,)), ((), ())),
            preferred_element_type=jnp.float32,
        )
        return carry

    lax.fori_loop(0, H, local_state, 0)

    @pl.when(z == 0)
    def _():
        state_first()

    loads[2].wait()
    causal = lax.broadcasted_iota(jnp.int32, (rows, rows), 0) >= lax.broadcasted_iota(
        jnp.int32, (rows, rows), 1
    )

    def intra(h, carry):
        scores = lax.dot_general(
            qb[:, head(h)],
            kb[:, head(h)],
            (((1,), (1,)), ((), ())),
            preferred_element_type=jnp.float32,
        )
        weights = jnp.where(causal, scores, 0.0).astype(jnp.bfloat16)
        attended[:, head(h)] = jnp.dot(
            weights, vb[:, head(h)], preferred_element_type=jnp.float32
        )
        return carry


    def finish():
        for load in loads[3:]:
            load.wait()

        def inter(h, square):
            both = attended[:, head(h)] + jnp.dot(
                qb[:, head(h)], prefix[h], preferred_element_type=jnp.float32
            )
            scale = lax.rsqrt(jnp.mean(both * both, axis=-1, keepdims=True) + 1e-06)
            wide = sb[:, head(h)].astype(jnp.float32) + both * scale * attn_gain_ref[:, head(h)]
            rounded = wide.astype(jnp.bfloat16)
            hidden[:, head(h)] = rounded
            wide = rounded.astype(jnp.float32)
            return square + jnp.sum(wide * wide, axis=-1, keepdims=True)

        square = lax.fori_loop(0, H, inter, jnp.zeros((rows, 1), jnp.float32))
        scale = lax.rsqrt(square / (H * DH) + 1e-06)

        def norm(h, carry):
            wide = hidden[:, head(h)].astype(jnp.float32)
            moe_in[:, head(h)] = (wide * scale * moe_gain_ref[:, head(h)]).astype(jnp.bfloat16)
            return carry

        lax.fori_loop(0, H, norm, 0)

    def activate(e):
        inputs = moe_in[...]
        gate = jnp.dot(inputs, wg[e], preferred_element_type=jnp.float32)
        upper = jnp.dot(inputs, wu[e], preferred_element_type=jnp.float32)
        return (gate / (1.0 + jnp.exp(-gate)) * upper).astype(jnp.bfloat16)

    def weigh(e, active):
        made = jnp.dot(active, wd[e], preferred_element_type=jnp.float32)
        made = made.astype(jnp.bfloat16).astype(jnp.float32)
        chosen = jnp.sum(jnp.where(ids[...] == e, gw[...], 0.0), axis=0, keepdims=True)
        return made * jnp.broadcast_to(chosen, (8, rows)).T[:, :1]

    last = len(steps)
    events = [(3 + 2 * i, stage_z, i) for i in range(last)]
    events += [(5 + 3 * i, stage_xy, i) for i in range(last)]
    events += [(15 + 3 * i, stage_d, i) for i in range(last)]

    def take_state(hop):
        @pl.when(z == hop)
        def _():
            state_next()

    def run_own(_):
        total[...] = weigh(z, activate(z))

    def run_expert(s):
        for t in range(3):
            stage_sib(3 * (s - 1) + t)
        total[...] += weigh(expert(s), activate(expert(s)))

    events += [(2, lambda _: lax.fori_loop(0, H // 2, intra, 0), 0)]
    events += [(5, lambda _: lax.fori_loop(H // 2, H, intra, 0), 0)]
    events += [(2 + 6 * hop, take_state, hop) for hop in range(1, n)]
    events += [(6 * n - 4, lambda _: finish(), 0), (6 * n - 1, run_own, 0)]
    events += [(max(9 * s + 21, 6 * n - 1 + 3 * s), run_expert, s) for s in range(1, n - 1)]
    for _, stage, i in sorted(events, key=lambda event: event[0]):
        stage(i)

    stage_sib(last - 3)
    stage_sib(last - 2)
    active = activate(expert(n - 1))
    stage_sib(last - 1)
    out_ref[0] = (
        hidden[...].astype(jnp.float32) + (total[...] + weigh(expert(n - 1), active))
    ).astype(out_ref.dtype)

    for t in range(3):

        @pl.when(has_up)
        def _():
            own_up(t).wait_send()

        @pl.when(has_down)
        def _():
            own_down(t).wait_send()

    for i in range(last):

        @pl.when(goes_up(i))
        def _():
            further(i, True).wait_send()

        @pl.when(goes_down(i))
        def _():
            further(i, False).wait_send()

        for copy in across(i):
            copy.wait_send()
        on_y, on_x, *sibs = relays(i)

        @pl.when((c + i) % 2 == 0)
        def _():
            on_y().wait_send()

        @pl.when((c + i) % 2 == 1)
        def _():
            on_x().wait_send()

        for copy in sibs:
            copy().wait_send()

    @pl.when(has_up)
    def _():
        for part in range(4):
            state_copy(part, {"seq": z + 1}).wait_send()


def gathered_weights(
    n,
    queries,
    keys,
    values,
    stream,
    attn_gain,
    moe_gain,
    expert_ids,
    gate_weights,
    w_gate,
    w_up,
    w_down,
):
    rows, width = queries.shape[1:]
    units = w_gate.shape[2]
    half = jnp.bfloat16
    anywhere = pl.BlockSpec(memory_space=pl.ANY)
    vmem = pl.BlockSpec(memory_space=pltpu.VMEM)
    dma = pltpu.SemaphoreType.DMA
    return pl.pallas_call(
        functools.partial(fused_kernel, n),
        out_shape=jax.ShapeDtypeStruct((1, rows, width), half),
        in_specs=[anywhere] * 11,
        out_specs=vmem,
        scratch_shapes=[
            pltpu.VMEM((rows, width), half),
            pltpu.VMEM((rows, width), half),
            pltpu.VMEM((rows, width), half),
            pltpu.VMEM((rows, width), half),
            pltpu.VMEM((1, width), jnp.float32),
            pltpu.VMEM((1, width), jnp.float32),
            pltpu.VMEM((2, rows), jnp.int32),
            pltpu.VMEM((2, rows), jnp.float32),
            pltpu.VMEM((n, width, units), half),
            pltpu.VMEM((n, width, units), half),
            pltpu.VMEM((n, units, width), half),
            pltpu.VMEM((H, DH, DH), jnp.float32),
            pltpu.VMEM((H, DH, DH), half),
            pltpu.VMEM((H, DH, DH), half),
            pltpu.VMEM((rows, width), jnp.float32),
            pltpu.VMEM((rows, width), half),
            pltpu.VMEM((rows, width), half),
            pltpu.VMEM((rows, width), jnp.float32),
            dma((11,)),
            dma((n + 1, 3)),
            dma((n - 1, 3)),
            dma((n - 1, 3)),
            dma((n - 1, 3)),
            dma((4, n - 1, 3)),
            dma((8, n, 3)),
            dma((4,)),
            dma((4,)),
        ],
        compiler_params=pltpu.CompilerParams(
            collective_id=0, has_side_effects=True, vmem_limit_bytes=63 << 20
        ),
    )(
        queries,
        keys,
        values,
        stream,
        attn_gain[None],
        moe_gain[None],
        jnp.swapaxes(expert_ids, 1, 2),
        jnp.swapaxes(gate_weights, 1, 2),
        w_gate,
        w_up,
        w_down,
    )


def prefix_2(value, axis, join, neutral):
    count, mine = (lax.axis_size(axis), lax.axis_index(axis))
    pieces = lax.all_gather(value, axis)
    total = jnp.full_like(value, 0) + jnp.asarray(neutral, value.dtype)

    def lap(position, total):
        longer = join(total, pieces[position])
        return jnp.where(position < mine, longer, total)

    return lax.fori_loop(0, count - 1, lap, total)


def add_states(earlier, later):
    return earlier + later


def per_device(
    queries,
    keys,
    values,
    stream,
    attn_gain,
    moe_gain,
    expert_ids,
    gate_weights,
    w_gate,
    w_up,
    w_down,
):
    row_count = queries.shape[1]
    width = queries.shape[2]
    query_heads = queries[0].reshape(row_count, H, DH)
    key_heads = keys[0].reshape(row_count, H, DH)
    value_heads = values[0].reshape(row_count, H, DH)
    own_state = jnp.einsum(
        "shd,she->hde", key_heads, value_heads, preferred_element_type=jnp.float32
    )
    scores = jnp.einsum("thd,shd->hts", query_heads, key_heads, preferred_element_type=jnp.float32)
    causal = jnp.arange(row_count)[:, None] >= jnp.arange(row_count)[None, :]
    weights = jnp.where(causal[None], scores, jnp.zeros((), jnp.float32)).astype(jnp.bfloat16)
    intra = jnp.einsum("hts,shd->thd", weights, value_heads, preferred_element_type=jnp.float32)
    prefix = prefix_2(own_state, "seq", add_states, jnp.zeros_like(own_state))
    inter = jnp.einsum(
        "thd,hde->the", query_heads, prefix.astype(jnp.bfloat16), preferred_element_type=jnp.float32
    )
    attended = intra + inter
    normed = attended * lax.rsqrt(jnp.mean(attended * attended, axis=-1, keepdims=True) + 1e-06)
    hidden = (stream[0].astype(jnp.float32) + normed.reshape(row_count, width) * attn_gain).astype(
        jnp.bfloat16
    )
    hidden_wide = hidden.astype(jnp.float32)
    moe_in = (
        hidden_wide
        * lax.rsqrt(jnp.mean(hidden_wide * hidden_wide, axis=-1, keepdims=True) + 1e-06)
        * moe_gain
    ).astype(jnp.bfloat16)
    dest_count = lax.axis_size("seq")
    capacity = 3 * row_count // dest_count
    choice_ids = expert_ids[0].reshape(-1)
    place = jnp.arange(2 * row_count, dtype=jnp.int32)
    earlier = (choice_ids[:, None] == choice_ids[None, :]) & (place[:, None] > place[None, :])
    slot_rank = jnp.sum(earlier.astype(jnp.int32), axis=1)
    slot_index = choice_ids * capacity + slot_rank
    token_index = jnp.arange(2 * row_count, dtype=jnp.int32) // 2
    outgoing = (
        jnp.zeros((dest_count * capacity, width), jnp.bfloat16)
        .at[slot_index]
        .set(moe_in[token_index])
    )
    outgoing = outgoing.reshape(dest_count, capacity, width)
    received = lax.all_to_all(outgoing, "seq", split_axis=0, concat_axis=0, tiled=True)
    flat_rows = received.reshape(-1, width)
    gate = jnp.dot(flat_rows, w_gate[0], preferred_element_type=jnp.float32)
    upper = jnp.dot(flat_rows, w_up[0], preferred_element_type=jnp.float32)
    active = (jax.nn.silu(gate) * upper).astype(jnp.bfloat16)
    produced = jnp.dot(active, w_down[0], preferred_element_type=jnp.float32).astype(jnp.bfloat16)
    returned = lax.all_to_all(
        produced.reshape(received.shape), "seq", split_axis=0, concat_axis=0, tiled=True
    )
    picked = returned.reshape(-1, width)[slot_index].astype(jnp.float32)
    weighted = (gate_weights[0].reshape(-1)[:, None] * picked).reshape(row_count, 2, width)
    mixed = hidden_wide + (weighted[:, 0] + weighted[:, 1])
    return mixed.astype(jnp.bfloat16)[None]


def solution(mesh):
    placed = (
        P(("group", "rep"), "seq", None),
        P(("group", "rep"), "seq", None),
        P(("group", "rep"), "seq", None),
        P(("group", "rep"), "seq", None),
        P(),
        P(),
        P(("group", "rep"), "seq", None),
        P(("group", "rep"), "seq", None),
        P("seq", None, None),
        P("seq", None, None),
        P("seq", None, None),
    )
    ways = dict(mesh.shape)

    def plan(*args):
        n = ways["seq"]
        held = n * sum(w.size // w.shape[0] * w.dtype.itemsize for w in args[-3:])
        if ways["group"] == 2 and ways["rep"] == 4 and n > 1 and held <= GATHER_LIMIT:
            return gathered_weights(n, *args)
        return per_device(*args)

    return jax.shard_map(
        plan,
        mesh=mesh,
        in_specs=placed,
        out_specs=P(("group", "rep"), "seq", None),
        check_vma=False,
    )
```

```python
import functools

import jax
import jax.numpy as jnp
from jax import lax
from jax.experimental import pallas as pl
from jax.experimental.pallas import tpu as pltpu
from jax.sharding import PartitionSpec as P

H = 8
DH = 128
MESH = pl.DeviceIdType.MESH
GATHER_LIMIT = 24 << 20


M, X, Y, D, NATIVE, STATE, FIRST, LOCAL, INTRA, FINISH, COMPACT, OWN, ACT, DOWN, SERVE, SERVED = range(16)
PROGRAMS = (
    (
        (NATIVE, M, 0, 0, 1), (NATIVE, M, 0, 1, 1), (LOCAL,), (FIRST,), (NATIVE, M, 1, 0, 1), (NATIVE, M, 1, 1, 1),
        (NATIVE, M, 2, 0, 1), (NATIVE, M, 2, 1, 1), (INTRA, 0), (INTRA, 1), (FINISH,), (COMPACT,), (OWN,),
        (M, 2, 0, 0), (M, 2, 0, 1), (M, 2, 1, 0), (X, 2, 0, 0), (Y, 2, 0, 0), (M, 2, 1, 1), (X, 2, 0, 1),
        (Y, 2, 0, 1), (M, 3, 0, 0), (X, 2, 1, 0), (Y, 2, 1, 0), (M, 3, 0, 1), (X, 2, 1, 1), (D, 2, 0, 0),
        (D, 2, 0, 1), (Y, 2, 1, 1), (M, 3, 1, 0), (X, 3, 0, 0), (Y, 3, 0, 0), (M, 3, 1, 1), (X, 3, 0, 1),
        (D, 2, 1, 0), (M, 3, 2, 0), (D, 2, 1, 1), (Y, 3, 0, 1), (M, 3, 2, 1), (NATIVE, D, 0, 0, 1), (ACT, 2),
        (X, 3, 1, 0), (Y, 3, 1, 0), (M, 2, 2, 0), (NATIVE, D, 0, 1, 1), (X, 3, 1, 1), (D, 3, 0, 0), (M, 2, 2, 1),
        (NATIVE, D, 1, 0, 1), (X, 3, 2, 0), (Y, 3, 1, 1), (NATIVE, D, 1, 1, 1), (D, 3, 0, 1), (Y, 3, 2, 0),
        (NATIVE, D, 2, 0, 1), (X, 3, 2, 1), (Y, 3, 2, 1), (NATIVE, D, 2, 1, 1), (X, 2, 2, 0), (D, 3, 1, 0),
        (X, 2, 2, 1), (Y, 2, 2, 0), (D, 3, 1, 1), (Y, 2, 2, 1), (SERVED,), (ACT, 3), (D, 3, 2, 1), (D, 3, 2, 0),
        (D, 2, 2, 0), (DOWN, 3), (D, 2, 2, 1), (DOWN, 2),
    ),
    (
        (NATIVE, M, 0, 0, 2), (NATIVE, M, 0, 1, 2), (LOCAL,), (INTRA, 0), (NATIVE, M, 1, 0, 2), (INTRA, 1),
        (NATIVE, M, 1, 1, 2), (M, 2, 0, 0), (M, 0, 0, 0), (M, 2, 0, 1), (M, 0, 0, 1), (STATE, 0), (M, 2, 1, 0),
        (STATE, 1), (X, 2, 0, 0), (Y, 2, 0, 0), (M, 2, 1, 1), (STATE, 2), (X, 0, 0, 0), (Y, 0, 0, 0), (M, 3, 0, 0),
        (STATE, 3), (X, 2, 0, 1), (Y, 2, 0, 1), (M, 3, 0, 1), (FINISH,), (X, 0, 0, 1), (Y, 0, 0, 1), (M, 0, 1, 0),
        (M, 3, 1, 0), (X, 2, 1, 0), (Y, 2, 1, 0), (M, 0, 1, 1), (M, 3, 1, 1), (OWN,), (X, 2, 1, 1), (Y, 2, 1, 1),
        (M, 0, 2, 0), (M, 3, 2, 0), (X, 3, 0, 0), (Y, 3, 0, 0), (M, 0, 2, 1), (M, 3, 2, 1), (X, 3, 0, 1),
        (Y, 3, 0, 1), (M, 2, 2, 0), (X, 0, 1, 0), (Y, 0, 1, 0), (NATIVE, M, 2, 0, 2), (M, 2, 2, 1), (X, 3, 1, 0),
        (Y, 3, 1, 0), (NATIVE, M, 2, 1, 2), (SERVE, 0), (X, 0, 1, 1), (Y, 0, 1, 1), (NATIVE, D, 0, 0, 2), (SERVE, 1),
        (D, 2, 0, 0), (X, 3, 1, 1), (Y, 3, 1, 1), (NATIVE, D, 0, 1, 2), (D, 2, 0, 1), (X, 0, 2, 0), (Y, 0, 2, 0),
        (NATIVE, D, 1, 0, 2), (SERVE, 2), (D, 2, 1, 0), (X, 3, 2, 0), (Y, 3, 2, 0), (NATIVE, D, 1, 1, 2),
        (D, 0, 0, 0), (D, 2, 1, 1), (X, 0, 2, 1), (D, 3, 0, 0), (NATIVE, D, 2, 0, 2), (ACT, 2), (D, 0, 0, 1),
        (D, 2, 2, 0), (X, 3, 2, 1), (Y, 0, 2, 1), (NATIVE, D, 2, 1, 2), (D, 0, 1, 0), (D, 2, 2, 1), (D, 3, 0, 1),
        (Y, 3, 2, 1), (D, 0, 1, 1), (X, 2, 2, 0), (Y, 2, 2, 0), (ACT, 0), (D, 0, 2, 0), (X, 2, 2, 1), (Y, 2, 2, 1),
        (D, 0, 2, 1), (DOWN, 2), (D, 3, 1, 1), (D, 3, 1, 0), (DOWN, 0), (D, 3, 2, 1), (D, 3, 2, 0), (ACT, 3),
        (DOWN, 3),
    ),
    (
        (NATIVE, M, 0, 0, 1), (NATIVE, M, 0, 1, 1), (LOCAL,), (INTRA, 0), (NATIVE, M, 1, 0, 1), (INTRA, 1),
        (NATIVE, M, 1, 1, 1), (M, 1, 0, 0), (M, 3, 0, 0), (M, 1, 0, 1), (M, 3, 0, 1), (M, 1, 1, 0), (M, 3, 1, 0),
        (X, 1, 0, 0), (Y, 1, 0, 0), (M, 1, 1, 1), (M, 3, 1, 1), (X, 3, 0, 0), (Y, 3, 0, 0), (M, 3, 2, 0),
        (M, 0, 0, 0), (X, 1, 0, 1), (Y, 1, 0, 1), (M, 3, 2, 1), (M, 0, 0, 1), (STATE, 0), (X, 3, 0, 1), (Y, 3, 0, 1),
        (D, 3, 0, 0), (STATE, 1), (X, 1, 1, 0), (Y, 1, 1, 0), (NATIVE, M, 2, 0, 1), (D, 3, 0, 1), (STATE, 2),
        (X, 3, 1, 0), (Y, 3, 1, 0), (NATIVE, M, 2, 1, 1), (D, 3, 1, 0), (STATE, 3), (X, 1, 1, 1), (Y, 1, 1, 1),
        (D, 3, 1, 1), (FINISH,), (X, 3, 1, 1), (Y, 3, 1, 1), (D, 3, 2, 0), (M, 0, 1, 0), (X, 3, 2, 0), (Y, 3, 2, 0),
        (NATIVE, D, 0, 0, 1), (NATIVE, D, 0, 1, 1), (OWN,), (D, 3, 2, 1), (M, 0, 1, 1), (X, 0, 0, 0), (Y, 0, 0, 0),
        (M, 0, 2, 0), (NATIVE, D, 1, 0, 1), (ACT, 3), (X, 3, 2, 1), (Y, 3, 2, 1), (NATIVE, D, 1, 1, 1), (M, 0, 2, 1),
        (X, 0, 0, 1), (Y, 0, 0, 1), (NATIVE, D, 2, 0, 1), (DOWN, 3), (M, 1, 2, 0), (X, 0, 1, 0), (Y, 0, 1, 0),
        (NATIVE, D, 2, 1, 1), (M, 1, 2, 1), (X, 0, 1, 1), (Y, 0, 1, 1), (D, 1, 0, 0), (X, 0, 2, 0), (D, 0, 0, 0),
        (SERVE, 0), (D, 1, 0, 1), (X, 0, 2, 1), (Y, 0, 2, 0), (D, 1, 1, 0), (D, 0, 0, 1), (Y, 0, 2, 1), (SERVE, 1),
        (D, 1, 1, 1), (X, 1, 2, 0), (Y, 1, 2, 0), (D, 1, 2, 0), (ACT, 1), (X, 1, 2, 1), (D, 0, 1, 0), (SERVE, 2),
        (D, 1, 2, 1), (D, 0, 1, 1), (Y, 1, 2, 1), (ACT, 0), (D, 0, 2, 1), (D, 0, 2, 0), (DOWN, 1), (DOWN, 0),
    ),
    (
        (NATIVE, M, 0, 0, 2), (NATIVE, M, 0, 1, 2), (NATIVE, M, 1, 0, 2), (NATIVE, M, 1, 1, 2), (NATIVE, M, 2, 0, 2),
        (NATIVE, M, 2, 1, 2), (LOCAL,), (INTRA, 0), (INTRA, 1), (M, 1, 0, 0), (NATIVE, D, 0, 0, 2), (M, 1, 0, 1),
        (NATIVE, D, 0, 1, 2), (M, 1, 1, 0), (NATIVE, D, 1, 0, 2), (X, 1, 0, 0), (Y, 1, 0, 0), (M, 1, 1, 1),
        (NATIVE, D, 1, 1, 2), (X, 1, 0, 1), (Y, 1, 0, 1), (M, 0, 0, 0), (NATIVE, D, 2, 0, 2), (X, 1, 1, 0),
        (Y, 1, 1, 0), (M, 0, 0, 1), (NATIVE, D, 2, 1, 2), (X, 1, 1, 1), (D, 1, 0, 0), (STATE, 0), (D, 1, 0, 1),
        (Y, 1, 1, 1), (STATE, 1), (X, 0, 0, 0), (Y, 0, 0, 0), (STATE, 2), (X, 0, 0, 1), (D, 1, 1, 0), (STATE, 3),
        (FINISH,), (D, 1, 1, 1), (Y, 0, 0, 1), (D, 0, 0, 0), (M, 0, 1, 0), (COMPACT,), (OWN,), (M, 0, 1, 1), (ACT, 1),
        (M, 0, 2, 0), (D, 0, 0, 1), (Y, 0, 1, 0), (M, 0, 2, 1), (X, 0, 1, 0), (Y, 0, 1, 1), (M, 1, 2, 0),
        (X, 0, 1, 1), (Y, 0, 2, 0), (M, 1, 2, 1), (X, 0, 2, 0), (Y, 0, 2, 1), (X, 0, 2, 1), (D, 0, 1, 0),
        (D, 0, 1, 1), (Y, 1, 2, 0), (ACT, 0), (X, 1, 2, 0), (Y, 1, 2, 1), (X, 1, 2, 1), (D, 0, 2, 0), (D, 0, 2, 1),
        (D, 1, 2, 0), (DOWN, 0), (D, 1, 2, 1), (SERVED,), (DOWN, 1),
    ),
)


def fused_kernel(
    n,
    q_hbm,
    k_hbm,
    v_hbm,
    s_hbm,
    attn_gain_hbm,
    moe_gain_hbm,
    ids_hbm,
    gw_hbm,
    wg_hbm,
    wu_hbm,
    wd_hbm,
    out_ref,
    qb,
    kb,
    vb,
    sb,
    attn_gain_ref,
    moe_gain_ref,
    ids,
    gw,
    wg,
    wu,
    wd,
    local,
    prefix,
    passed,
    attended,
    hidden,
    moe_in,
    total,
    active,
    pick,
    rows_out,
    rows_in,
    load_sem,
    send_sem,
    piece_sem,
    sib_sem,
    state_send,
    state_recv,
    row_send,
    row_recv,
):
    g, z, r = lax.axis_index("group"), lax.axis_index("seq"), lax.axis_index("rep")
    x, c = r // 2, r % 2
    r_x, r_s = 2 * (1 - x) + c, 2 * x + (1 - c)
    piece_of = {
        M: g * 4 + r,
        X: g * 4 + r_x,
        Y: (1 - g) * 4 + r,
        D: (1 - g) * 4 + r_x,
    }
    to_x, to_y, to_s = {"rep": r_x}, {"group": 1 - g}, {"rep": r_s}
    rows = qb.shape[0]
    cap = rows_in.shape[0]
    group = cap // 3
    hbm = (wg_hbm, wu_hbm, wd_hbm)
    held = (wg, wu, wd)

    def span(t, piece, half):
        size = held[t].shape[1] // 16
        return pl.ds(pl.multiple_of(piece * 2 * size + half * size, size), size)

    barrier = pltpu.get_barrier_semaphore()
    for to in (to_x, to_y, to_s):
        pl.semaphore_signal(barrier, inc=1, device_id=to, device_id_type=MESH)

    @pl.when(z < n - 1)
    def _():
        pl.semaphore_signal(barrier, inc=1, device_id={"seq": z + 1}, device_id_type=MESH)

    @pl.when(z > 0)
    def _():
        pl.semaphore_signal(barrier, inc=1, device_id={"seq": z - 1}, device_id_type=MESH)

    loads = [
        pltpu.make_async_copy(src, dst, load_sem.at[i])
        for i, (src, dst) in enumerate(
            [
                (k_hbm.at[0], kb),
                (v_hbm.at[0], vb),
                (q_hbm.at[0], qb),
                (s_hbm.at[0], sb),
                (attn_gain_hbm, attn_gain_ref),
                (moe_gain_hbm, moe_gain_ref),
                (ids_hbm.at[0], ids),
                (gw_hbm.at[0], gw),
                (wg_hbm.at[0], wg.at[z]),
                (wu_hbm.at[0], wu.at[z]),
                (wd_hbm.at[0], wd.at[z]),
            ]
        )
    ]
    for load in loads[:4]:
        load.start()
    pl.semaphore_wait(barrier, 3 + (z < n - 1).astype(jnp.int32) + (z > 0).astype(jnp.int32))

    def head(h):
        return pl.ds(pl.multiple_of(h * DH, DH), DH)

    def local_state():
        loads[0].wait()
        loads[1].wait()

        def one(h, carry):
            local[h] = lax.dot_general(
                kb[:, head(h)],
                vb[:, head(h)],
                (((0,), (0,)), ((), ())),
                preferred_element_type=jnp.float32,
            )
            return carry

        lax.fori_loop(0, H, one, 0)

    def intra(part):
        if part == 0:
            loads[2].wait()
        causal = lax.broadcasted_iota(jnp.int32, (rows, rows), 0) >= lax.broadcasted_iota(
            jnp.int32, (rows, rows), 1
        )

        def one(h, carry):
            scores = lax.dot_general(
                qb[:, head(h)],
                kb[:, head(h)],
                (((1,), (1,)), ((), ())),
                preferred_element_type=jnp.float32,
            )
            weights = jnp.where(causal, scores, 0.0).astype(jnp.bfloat16)
            attended[:, head(h)] = jnp.dot(
                weights, vb[:, head(h)], preferred_element_type=jnp.float32
            )
            return carry

        lax.fori_loop(part * H // 2, (part + 1) * H // 2, one, 0)

    def finish():
        for load in loads[3:8]:
            load.wait()

        def inter(h, square):
            both = attended[:, head(h)] + jnp.dot(
                qb[:, head(h)], prefix[h], preferred_element_type=jnp.float32
            )
            scale = lax.rsqrt(jnp.mean(both * both, axis=-1, keepdims=True) + 1e-06)
            wide = sb[:, head(h)].astype(jnp.float32) + both * scale * attn_gain_ref[:, head(h)]
            rounded = wide.astype(jnp.bfloat16)
            hidden[:, head(h)] = rounded
            wide = rounded.astype(jnp.float32)
            return square + jnp.sum(wide * wide, axis=-1, keepdims=True)

        square = lax.fori_loop(0, H, inter, jnp.zeros((rows, 1), jnp.float32))
        scale = lax.rsqrt(square / (H * DH) + 1e-06)

        def norm(h, carry):
            wide = hidden[:, head(h)].astype(jnp.float32)
            moe_in[:, head(h)] = (wide * scale * moe_gain_ref[:, head(h)]).astype(jnp.bfloat16)
            return carry

        lax.fori_loop(0, H, norm, 0)

    def activate(inputs, e):
        gate = jnp.dot(inputs, wg[e], preferred_element_type=jnp.float32)
        upper = jnp.dot(inputs, wu[e], preferred_element_type=jnp.float32)
        return (gate / (1.0 + jnp.exp(-gate)) * upper).astype(jnp.bfloat16)

    def down(acts, e):
        return jnp.dot(acts, wd[e], preferred_element_type=jnp.float32).astype(jnp.bfloat16)

    def weigh(made, e):
        chosen = jnp.sum(jnp.where(ids[...] == e, gw[...], 0.0), axis=0, keepdims=True)
        return made.astype(jnp.float32) * jnp.broadcast_to(chosen, (8, rows)).T[:, :1]

    def program(at):
        end = at in (0, n - 1)
        near = 1 if at == 0 else at - 1 if at == n - 1 else n - 1 - at
        outer = None if end else (0 if at < n - 1 - at else n - 1)
        sent = {}

        def push(sem, copy):
            sent[sem] = sent.get(sem, 0) + 1
            copy.start()

        def piece(kind, landed, e, t, half, sem, to, source=None):
            where = span(t, piece_of[kind], half)
            dst = held[t].at[e, where, :]
            return pltpu.make_async_remote_copy(
                src_ref=dst if source is None else source.at[0, where, :],
                dst_ref=dst,
                send_sem=send_sem.at[sem],
                recv_sem=landed,
                device_id=to,
                device_id_type=MESH,
            )

        def landing(kind, e, t, half):
            return piece_sem.at[kind, e, t, half]

        def doubled(e, t):
            return not end and abs(e - at) == 1

        def native(kind, t, half, to):
            landed = landing(kind, at, t, half)
            sem = 0 if to > at else 1
            push(sem, piece(kind, landed, at, t, half, sem, {"seq": to}, hbm[t]))

        def pass_on(kind, e, t, half):
            piece(kind, landing(kind, e, t, half), e, t, half, 0, to_x).wait_recv()
            if kind == M:
                if not end:
                    to = near if e == outer else outer
                    sem = 0 if to > at else 1
                    push(sem, piece(M, landing(M, e, t, half), e, t, half, sem, {"seq": to}))
                push(2, piece(M, landing(X, e, t, half), e, t, half, 2, to_x))
                push(3, piece(M, landing(Y, e, t, half), e, t, half, 3, to_y))
            if kind == X and half == 0 and not doubled(e, t):
                push(3, piece(X, landing(D, e, t, half), e, t, half, 3, to_y))
            if kind == Y and half == 1 and not doubled(e, t):
                push(2, piece(Y, landing(D, e, t, half), e, t, half, 2, to_x))
            sem = 4 + kind
            push(sem, piece(kind, sib_sem.at[e, t], e, t, half, sem, to_s))

        def from_sibling(e, t):
            half = held[t].at[e, pl.ds(0, held[t].shape[1] // 2), :]
            pltpu.make_async_copy(half, half, sib_sem.at[e, t]).wait()

        def state_copy(part):
            heads = pl.ds(part * (H // 4), H // 4)
            return pltpu.make_async_remote_copy(
                src_ref=passed.at[heads],
                dst_ref=prefix.at[heads],
                send_sem=state_send.at[part],
                recv_sem=state_recv.at[part],
                device_id={"seq": at + 1 if at < n - 1 else at - 1},
                device_id_type=MESH,
            )

        def first_state():
            prefix[...] = jnp.zeros_like(prefix)
            passed[...] = local[...].astype(passed.dtype)
            for part in range(4):
                state_copy(part).start()

        def next_state(part):
            state_copy(part).wait_recv()
            if at < n - 1:
                heads = pl.ds(part * (H // 4), H // 4)
                passed[heads] = (prefix[heads].astype(jnp.float32) + local[heads]).astype(
                    passed.dtype
                )
                state_copy(part).start()

        def row_copy(part):
            some = pl.ds(part * group, group)
            return pltpu.make_async_remote_copy(
                src_ref=rows_out.at[some],
                dst_ref=rows_in.at[some],
                send_sem=row_send.at[part],
                recv_sem=row_recv.at[part],
                device_id={"seq": near if end else outer},
                device_id_type=MESH,
            )

        def compact():
            named = jnp.max((ids[...] == near).astype(jnp.float32), axis=0, keepdims=True)
            earlier = lax.broadcasted_iota(jnp.int32, (rows, rows), 0) < lax.broadcasted_iota(
                jnp.int32, (rows, rows), 1
            )
            place = jnp.dot(
                jnp.broadcast_to(named, (8, rows)).astype(jnp.bfloat16),
                earlier.astype(jnp.bfloat16),
                preferred_element_type=jnp.float32,
            )[:1]
            slots = lax.broadcasted_iota(jnp.int32, (cap, rows), 0).astype(jnp.float32)
            pick[...] = jnp.where(slots == place, named, 0.0).astype(jnp.bfloat16)
            rows_out[...] = jnp.dot(
                pick[...], moe_in[...], preferred_element_type=jnp.float32
            ).astype(jnp.bfloat16)
            for part in range(3):
                row_copy(part).start()

        def serve(part):
            row_copy(part).wait_recv()
            some = pl.ds(part * group, group)
            rows_out[some] = down(activate(rows_in[some], at), at)
            row_copy(part).start()

        def served():
            for part in range(3):
                row_copy(part).wait_recv()
            made = lax.dot_general(
                pick[...],
                rows_in[...],
                (((0,), (0,)), ((), ())),
                preferred_element_type=jnp.float32,
            )
            return weigh(made, near)

        def own():
            for load in loads[8:]:
                load.wait()
            total[...] = weigh(down(activate(moe_in[...], at), at), at)

        def act(e):
            from_sibling(e, 0)
            from_sibling(e, 1)
            active[e] = activate(moe_in[...], e)

        def expert_out(e):
            from_sibling(e, 2)
            return weigh(down(active[e], e), e)

        def settle():
            for sem, count in sent.items():
                some = wg.at[:, pl.ds(0, wg.shape[1] // 64 * count), :]
                pltpu.make_async_copy(some, some, send_sem.at[sem]).wait()
            if at < n - 1:
                for part in range(4):
                    state_copy(part).wait_send()
            for part in range(3):
                row_copy(part).wait_send()

        items = PROGRAMS[at]
        started = False
        for index, item in enumerate(items):
            name, *rest = item
            if name <= D:
                pass_on(name, *rest)
            elif name == NATIVE:
                native(*rest)
            elif name == STATE:
                next_state(*rest)
            elif name == FIRST:
                first_state()
            elif name == LOCAL:
                local_state()
            elif name == INTRA:
                intra(*rest)
            elif name == FINISH:
                finish()
            elif name == COMPACT:
                compact()
            elif name == SERVE:
                serve(*rest)
            elif name == OWN:
                own()
            elif name == ACT:
                act(*rest)
            else:
                last = index == len(items) - 1
                if last:
                    settle()
                added = total[...] + (served() if name == SERVED else expert_out(*rest))
                if last:
                    out_ref[0] = (hidden[...].astype(jnp.float32) + added).astype(out_ref.dtype)
                else:
                    total[...] = added
            if name == LOCAL and not started:
                started = True
                for load in loads[4:]:
                    load.start()

    for at in range(n):

        @pl.when(z == at)
        def _():
            program(at)


def gathered_weights(
    n,
    queries,
    keys,
    values,
    stream,
    attn_gain,
    moe_gain,
    expert_ids,
    gate_weights,
    w_gate,
    w_up,
    w_down,
):
    rows, width = queries.shape[1:]
    units = w_gate.shape[2]
    cap = 3 * rows // n
    half = jnp.bfloat16
    anywhere = pl.BlockSpec(memory_space=pl.ANY)
    vmem = pl.BlockSpec(memory_space=pltpu.VMEM)
    dma = pltpu.SemaphoreType.DMA
    return pl.pallas_call(
        functools.partial(fused_kernel, n),
        out_shape=jax.ShapeDtypeStruct((1, rows, width), half),
        in_specs=[anywhere] * 11,
        out_specs=vmem,
        scratch_shapes=[
            pltpu.VMEM((rows, width), half),
            pltpu.VMEM((rows, width), half),
            pltpu.VMEM((rows, width), half),
            pltpu.VMEM((rows, width), half),
            pltpu.VMEM((1, width), jnp.float32),
            pltpu.VMEM((1, width), jnp.float32),
            pltpu.VMEM((2, rows), jnp.int32),
            pltpu.VMEM((2, rows), jnp.float32),
            pltpu.VMEM((n, width, units), half),
            pltpu.VMEM((n, width, units), half),
            pltpu.VMEM((n, units, width), half),
            pltpu.VMEM((H, DH, DH), jnp.float32),
            pltpu.VMEM((H, DH, DH), half),
            pltpu.VMEM((H, DH, DH), half),
            pltpu.VMEM((rows, width), jnp.float32),
            pltpu.VMEM((rows, width), half),
            pltpu.VMEM((rows, width), half),
            pltpu.VMEM((rows, width), jnp.float32),
            pltpu.VMEM((n, rows, units), half),
            pltpu.VMEM((cap, rows), half),
            pltpu.VMEM((cap, width), half),
            pltpu.VMEM((cap, width), half),
            dma((11,)),
            dma((8,)),
            dma((4, n, 3, 2)),
            dma((n, 3)),
            dma((4,)),
            dma((4,)),
            dma((3,)),
            dma((3,)),
        ],
        compiler_params=pltpu.CompilerParams(
            collective_id=0, has_side_effects=True, vmem_limit_bytes=63 << 20
        ),
    )(
        queries,
        keys,
        values,
        stream,
        attn_gain[None],
        moe_gain[None],
        jnp.swapaxes(expert_ids, 1, 2),
        jnp.swapaxes(gate_weights, 1, 2),
        w_gate,
        w_up,
        w_down,
    )


def prefix_2(value, axis, join, neutral):
    count, mine = (lax.axis_size(axis), lax.axis_index(axis))
    pieces = lax.all_gather(value, axis)
    total = jnp.full_like(value, 0) + jnp.asarray(neutral, value.dtype)

    def lap(position, total):
        longer = join(total, pieces[position])
        return jnp.where(position < mine, longer, total)

    return lax.fori_loop(0, count - 1, lap, total)


def add_states(earlier, later):
    return earlier + later


def per_device(
    queries,
    keys,
    values,
    stream,
    attn_gain,
    moe_gain,
    expert_ids,
    gate_weights,
    w_gate,
    w_up,
    w_down,
):
    row_count = queries.shape[1]
    width = queries.shape[2]
    query_heads = queries[0].reshape(row_count, H, DH)
    key_heads = keys[0].reshape(row_count, H, DH)
    value_heads = values[0].reshape(row_count, H, DH)
    own_state = jnp.einsum(
        "shd,she->hde", key_heads, value_heads, preferred_element_type=jnp.float32
    )
    scores = jnp.einsum("thd,shd->hts", query_heads, key_heads, preferred_element_type=jnp.float32)
    causal = jnp.arange(row_count)[:, None] >= jnp.arange(row_count)[None, :]
    weights = jnp.where(causal[None], scores, jnp.zeros((), jnp.float32)).astype(jnp.bfloat16)
    intra = jnp.einsum("hts,shd->thd", weights, value_heads, preferred_element_type=jnp.float32)
    prefix = prefix_2(own_state, "seq", add_states, jnp.zeros_like(own_state))
    inter = jnp.einsum(
        "thd,hde->the", query_heads, prefix.astype(jnp.bfloat16), preferred_element_type=jnp.float32
    )
    attended = intra + inter
    normed = attended * lax.rsqrt(jnp.mean(attended * attended, axis=-1, keepdims=True) + 1e-06)
    hidden = (stream[0].astype(jnp.float32) + normed.reshape(row_count, width) * attn_gain).astype(
        jnp.bfloat16
    )
    hidden_wide = hidden.astype(jnp.float32)
    moe_in = (
        hidden_wide
        * lax.rsqrt(jnp.mean(hidden_wide * hidden_wide, axis=-1, keepdims=True) + 1e-06)
        * moe_gain
    ).astype(jnp.bfloat16)
    dest_count = lax.axis_size("seq")
    capacity = 3 * row_count // dest_count
    choice_ids = expert_ids[0].reshape(-1)
    place = jnp.arange(2 * row_count, dtype=jnp.int32)
    earlier = (choice_ids[:, None] == choice_ids[None, :]) & (place[:, None] > place[None, :])
    slot_rank = jnp.sum(earlier.astype(jnp.int32), axis=1)
    slot_index = choice_ids * capacity + slot_rank
    token_index = jnp.arange(2 * row_count, dtype=jnp.int32) // 2
    outgoing = (
        jnp.zeros((dest_count * capacity, width), jnp.bfloat16)
        .at[slot_index]
        .set(moe_in[token_index])
    )
    outgoing = outgoing.reshape(dest_count, capacity, width)
    received = lax.all_to_all(outgoing, "seq", split_axis=0, concat_axis=0, tiled=True)
    flat_rows = received.reshape(-1, width)
    gate = jnp.dot(flat_rows, w_gate[0], preferred_element_type=jnp.float32)
    upper = jnp.dot(flat_rows, w_up[0], preferred_element_type=jnp.float32)
    active = (jax.nn.silu(gate) * upper).astype(jnp.bfloat16)
    produced = jnp.dot(active, w_down[0], preferred_element_type=jnp.float32).astype(jnp.bfloat16)
    returned = lax.all_to_all(
        produced.reshape(received.shape), "seq", split_axis=0, concat_axis=0, tiled=True
    )
    picked = returned.reshape(-1, width)[slot_index].astype(jnp.float32)
    weighted = (gate_weights[0].reshape(-1)[:, None] * picked).reshape(row_count, 2, width)
    mixed = hidden_wide + (weighted[:, 0] + weighted[:, 1])
    return mixed.astype(jnp.bfloat16)[None]


def solution(mesh):
    placed = (
        P(("group", "rep"), "seq", None),
        P(("group", "rep"), "seq", None),
        P(("group", "rep"), "seq", None),
        P(("group", "rep"), "seq", None),
        P(),
        P(),
        P(("group", "rep"), "seq", None),
        P(("group", "rep"), "seq", None),
        P("seq", None, None),
        P("seq", None, None),
        P("seq", None, None),
    )
    ways = dict(mesh.shape)

    def plan(*args):
        n = ways["seq"]
        held = n * sum(w.size // w.shape[0] * w.dtype.itemsize for w in args[-3:])
        whole = args[-1].shape[1] % 256 == 0 and args[0].shape[1] % 64 == 0
        if ways["group"] == 2 and ways["rep"] == 4 and n == len(PROGRAMS) and whole and held <= GATHER_LIMIT:
            return gathered_weights(n, *args)
        return per_device(*args)

    return jax.shard_map(
        plan,
        mesh=mesh,
        in_specs=placed,
        out_specs=P(("group", "rep"), "seq", None),
        check_vma=False,
    )
```

```python
import functools

import jax
import jax.numpy as jnp
from jax import lax
from jax.experimental import pallas as pl
from jax.experimental.pallas import tpu as pltpu
from jax.sharding import PartitionSpec as P

H = 8
DH = 128
MESH = pl.DeviceIdType.MESH
GATHER_LIMIT = 24 << 20


M, X, Y, D, NATIVE, STATE, FIRST, LOCAL, INTRA, FINISH, COMPACT, OWN, ACT, DOWN, SERVE, SERVED = range(16)
PROGRAMS = (
    (
        (NATIVE, M, 0, 0, 1), (NATIVE, M, 0, 1, 1), (LOCAL,), (FIRST,), (NATIVE, M, 1, 0, 1), (NATIVE, M, 1, 1, 1),
        (NATIVE, M, 2, 0, 1), (NATIVE, M, 2, 1, 1), (INTRA, 0), (INTRA, 1), (FINISH,), (COMPACT,), (OWN,),
        (M, 2, 0, 0), (M, 2, 0, 1), (X, 2, 0, 0), (Y, 2, 0, 0), (M, 3, 0, 0), (X, 2, 0, 1), (Y, 2, 0, 1),
        (M, 3, 0, 1), (M, 3, 1, 0), (D, 2, 0, 0), (X, 3, 0, 0), (Y, 3, 0, 0), (M, 2, 1, 0), (D, 2, 0, 1),
        (Y, 3, 0, 1), (X, 3, 0, 1), (M, 2, 1, 1), (Y, 3, 1, 0), (X, 3, 1, 0), (M, 3, 1, 1), (D, 3, 0, 0),
        (X, 2, 1, 0), (M, 3, 2, 0), (NATIVE, D, 0, 0, 1), (Y, 2, 1, 0), (D, 3, 0, 1), (M, 3, 2, 1),
        (NATIVE, D, 0, 1, 1), (Y, 2, 1, 1), (X, 2, 1, 1), (M, 2, 2, 0), (NATIVE, D, 1, 0, 1), (D, 3, 1, 0),
        (X, 3, 1, 1), (M, 2, 2, 1), (NATIVE, D, 1, 1, 1), (Y, 3, 1, 1), (X, 3, 2, 0), (NATIVE, D, 2, 0, 1),
        (D, 2, 1, 0), (X, 3, 2, 1), (NATIVE, D, 2, 1, 1), (Y, 3, 2, 0), (D, 2, 1, 1), (ACT, 2), (Y, 3, 2, 1),
        (X, 2, 2, 0), (Y, 2, 2, 0), (X, 2, 2, 1), (Y, 2, 2, 1), (D, 3, 1, 1), (SERVED,), (ACT, 3), (D, 3, 2, 0),
        (D, 3, 2, 1), (D, 2, 2, 0), (DOWN, 3), (D, 2, 2, 1), (DOWN, 2),
    ),
    (
        (NATIVE, M, 0, 0, 2), (NATIVE, M, 0, 1, 2), (NATIVE, M, 1, 0, 2), (LOCAL,), (INTRA, 0), (INTRA, 1),
        (NATIVE, M, 1, 1, 2), (NATIVE, M, 2, 0, 2), (M, 2, 0, 0), (M, 0, 0, 0), (M, 2, 0, 1), (M, 0, 0, 1),
        (STATE, 0), (X, 2, 0, 0), (Y, 2, 0, 0), (M, 3, 0, 0), (STATE, 1), (X, 0, 0, 0), (Y, 0, 0, 0), (M, 3, 0, 1),
        (STATE, 2), (X, 2, 0, 1), (Y, 2, 0, 1), (M, 3, 1, 0), (STATE, 3), (FINISH,), (X, 0, 0, 1), (Y, 0, 0, 1),
        (M, 2, 1, 0), (OWN,), (M, 0, 1, 0), (X, 3, 0, 0), (Y, 3, 0, 0), (M, 2, 1, 1), (M, 0, 1, 1), (X, 3, 0, 1),
        (Y, 3, 0, 1), (M, 3, 1, 1), (M, 0, 2, 0), (X, 3, 1, 0), (Y, 3, 1, 0), (M, 3, 2, 0), (M, 0, 2, 1),
        (X, 2, 1, 0), (Y, 2, 1, 0), (M, 3, 2, 1), (X, 0, 1, 0), (Y, 0, 1, 0), (M, 2, 2, 0), (NATIVE, M, 2, 1, 2),
        (X, 2, 1, 1), (D, 3, 0, 0), (M, 2, 2, 1), (SERVE, 0), (X, 0, 1, 1), (Y, 2, 1, 1), (NATIVE, D, 0, 0, 2),
        (NATIVE, D, 0, 1, 2), (SERVE, 1), (D, 3, 0, 1), (Y, 0, 1, 1), (NATIVE, D, 1, 0, 2), (X, 3, 1, 1),
        (Y, 3, 1, 1), (NATIVE, D, 1, 1, 2), (SERVE, 2), (D, 2, 0, 0), (X, 0, 2, 0), (Y, 0, 2, 0),
        (NATIVE, D, 2, 0, 2), (D, 0, 0, 0), (D, 2, 0, 1), (X, 3, 2, 0), (D, 3, 1, 0), (NATIVE, D, 2, 1, 2),
        (D, 0, 0, 1), (D, 2, 1, 0), (X, 0, 2, 1), (Y, 3, 2, 0), (D, 0, 1, 0), (D, 2, 1, 1), (X, 3, 2, 1),
        (Y, 0, 2, 1), (ACT, 2), (D, 0, 1, 1), (D, 2, 2, 0), (X, 2, 2, 0), (Y, 3, 2, 1), (D, 0, 2, 0), (D, 2, 2, 1),
        (ACT, 0), (X, 2, 2, 1), (Y, 2, 2, 0), (D, 0, 2, 1), (D, 3, 1, 1), (Y, 2, 2, 1), (DOWN, 0), (ACT, 3),
        (D, 3, 2, 1), (D, 3, 2, 0), (DOWN, 2), (DOWN, 3),
    ),
    (
        (NATIVE, M, 0, 0, 1), (NATIVE, M, 0, 1, 1), (LOCAL,), (INTRA, 0), (INTRA, 1), (M, 1, 0, 0), (M, 3, 0, 0),
        (M, 1, 0, 1), (M, 3, 0, 1), (M, 1, 1, 0), (M, 3, 1, 0), (X, 1, 0, 0), (Y, 1, 0, 0), (NATIVE, M, 1, 0, 1),
        (NATIVE, M, 1, 1, 1), (M, 1, 1, 1), (M, 3, 1, 1), (X, 3, 0, 0), (Y, 3, 0, 0), (M, 1, 2, 0), (M, 3, 2, 0),
        (X, 1, 0, 1), (Y, 1, 0, 1), (M, 3, 2, 1), (M, 0, 0, 0), (X, 3, 0, 1), (Y, 3, 0, 1), (D, 3, 0, 0),
        (M, 0, 0, 1), (NATIVE, M, 2, 0, 1), (X, 1, 1, 0), (Y, 1, 1, 0), (STATE, 0), (D, 3, 0, 1),
        (NATIVE, M, 2, 1, 1), (X, 3, 1, 0), (Y, 3, 1, 0), (STATE, 1), (D, 3, 1, 0), (X, 1, 1, 1), (Y, 1, 1, 1),
        (STATE, 2), (D, 3, 1, 1), (X, 3, 1, 1), (Y, 3, 1, 1), (STATE, 3), (D, 3, 2, 0), (FINISH,), (X, 1, 2, 0),
        (Y, 1, 2, 0), (OWN,), (D, 3, 2, 1), (M, 0, 1, 0), (X, 3, 2, 0), (Y, 3, 2, 0), (M, 0, 1, 1), (ACT, 3),
        (X, 3, 2, 1), (Y, 3, 2, 1), (NATIVE, D, 0, 0, 1), (NATIVE, D, 0, 1, 1), (NATIVE, D, 1, 0, 1), (M, 0, 2, 0),
        (X, 0, 0, 0), (Y, 0, 0, 0), (DOWN, 3), (M, 0, 2, 1), (NATIVE, D, 1, 1, 1), (X, 0, 0, 1), (Y, 0, 0, 1),
        (NATIVE, D, 2, 0, 1), (M, 1, 2, 1), (X, 0, 1, 0), (Y, 0, 1, 0), (NATIVE, D, 2, 1, 1), (D, 1, 0, 0),
        (X, 0, 1, 1), (Y, 0, 1, 1), (D, 1, 0, 1), (SERVE, 0), (X, 0, 2, 0), (Y, 0, 2, 0), (D, 1, 1, 0), (X, 0, 2, 1),
        (D, 0, 0, 0), (D, 1, 1, 1), (SERVE, 1), (D, 0, 0, 1), (Y, 0, 2, 1), (ACT, 1), (D, 1, 2, 0), (X, 1, 2, 1),
        (Y, 1, 2, 1), (D, 1, 2, 1), (SERVE, 2), (D, 0, 1, 1), (D, 0, 1, 0), (DOWN, 1), (D, 0, 2, 1), (D, 0, 2, 0),
        (ACT, 0), (DOWN, 0),
    ),
    (
        (NATIVE, M, 0, 0, 2), (NATIVE, M, 0, 1, 2), (NATIVE, M, 1, 0, 2), (NATIVE, M, 1, 1, 2), (NATIVE, M, 2, 0, 2),
        (NATIVE, M, 2, 1, 2), (LOCAL,), (INTRA, 0), (INTRA, 1), (NATIVE, D, 0, 0, 2), (M, 1, 0, 0),
        (NATIVE, D, 0, 1, 2), (M, 1, 0, 1), (NATIVE, D, 1, 0, 2), (M, 1, 1, 0), (NATIVE, D, 1, 1, 2), (X, 1, 0, 0),
        (Y, 1, 0, 0), (M, 1, 1, 1), (NATIVE, D, 2, 0, 2), (X, 1, 0, 1), (Y, 1, 0, 1), (M, 1, 2, 0),
        (NATIVE, D, 2, 1, 2), (X, 1, 1, 0), (Y, 1, 1, 0), (M, 0, 0, 0), (X, 1, 1, 1), (D, 1, 0, 0), (M, 0, 0, 1),
        (D, 1, 0, 1), (Y, 1, 1, 1), (STATE, 0), (X, 1, 2, 0), (Y, 1, 2, 0), (STATE, 1), (X, 0, 0, 0), (D, 1, 1, 0),
        (STATE, 2), (X, 0, 0, 1), (Y, 0, 0, 0), (STATE, 3), (FINISH,), (D, 1, 1, 1), (Y, 0, 0, 1), (COMPACT,),
        (D, 1, 2, 0), (OWN,), (M, 0, 1, 0), (D, 0, 0, 0), (ACT, 1), (M, 0, 1, 1), (D, 0, 0, 1), (M, 0, 2, 0),
        (X, 0, 1, 0), (Y, 0, 1, 0), (M, 0, 2, 1), (X, 0, 1, 1), (Y, 0, 1, 1), (M, 1, 2, 1), (X, 0, 2, 0),
        (Y, 0, 2, 0), (X, 0, 2, 1), (D, 0, 1, 0), (D, 0, 1, 1), (Y, 0, 2, 1), (ACT, 0), (X, 1, 2, 1), (Y, 1, 2, 1),
        (D, 0, 2, 0), (D, 0, 2, 1), (DOWN, 0), (D, 1, 2, 1), (SERVED,), (DOWN, 1),
    ),
)


def fused_kernel(
    n,
    q_hbm,
    k_hbm,
    v_hbm,
    s_hbm,
    attn_gain_hbm,
    moe_gain_hbm,
    ids_hbm,
    gw_hbm,
    wg_hbm,
    wu_hbm,
    wd_hbm,
    out_ref,
    qb,
    kb,
    vb,
    sb,
    attn_gain_ref,
    moe_gain_ref,
    ids,
    gw,
    wg,
    wu,
    wd,
    local,
    prefix,
    passed,
    attended,
    hidden,
    moe_in,
    total,
    active,
    pick,
    rows_out,
    rows_in,
    load_sem,
    send_sem,
    piece_sem,
    sib_sem,
    state_send,
    state_recv,
    row_send,
    row_recv,
):
    g, z, r = lax.axis_index("group"), lax.axis_index("seq"), lax.axis_index("rep")
    x, c = r // 2, r % 2
    r_x, r_s = 2 * (1 - x) + c, 2 * x + (1 - c)
    piece_of = {
        M: g * 4 + r,
        X: g * 4 + r_x,
        Y: (1 - g) * 4 + r,
        D: (1 - g) * 4 + r_x,
    }
    to_x, to_y, to_s = {"rep": r_x}, {"group": 1 - g}, {"rep": r_s}
    rows = qb.shape[0]
    cap = rows_in.shape[0]
    group = cap // 3
    hbm = (wg_hbm, wu_hbm, wd_hbm)
    held = (wg, wu, wd)

    def span(t, piece, half):
        size = held[t].shape[1] // 16
        return pl.ds(pl.multiple_of(piece * 2 * size + half * size, size), size)

    barrier = pltpu.get_barrier_semaphore()
    for to in (to_x, to_y, to_s):
        pl.semaphore_signal(barrier, inc=1, device_id=to, device_id_type=MESH)

    @pl.when(z < n - 1)
    def _():
        pl.semaphore_signal(barrier, inc=1, device_id={"seq": z + 1}, device_id_type=MESH)

    @pl.when(z > 0)
    def _():
        pl.semaphore_signal(barrier, inc=1, device_id={"seq": z - 1}, device_id_type=MESH)

    loads = [
        pltpu.make_async_copy(src, dst, load_sem.at[i])
        for i, (src, dst) in enumerate(
            [
                (k_hbm.at[0], kb),
                (v_hbm.at[0], vb),
                (q_hbm.at[0], qb),
                (s_hbm.at[0], sb),
                (attn_gain_hbm, attn_gain_ref),
                (moe_gain_hbm, moe_gain_ref),
                (ids_hbm.at[0], ids),
                (gw_hbm.at[0], gw),
                (wg_hbm.at[0], wg.at[z]),
                (wu_hbm.at[0], wu.at[z]),
                (wd_hbm.at[0], wd.at[z]),
            ]
        )
    ]
    for load in loads[:4]:
        load.start()
    pl.semaphore_wait(barrier, 3 + (z < n - 1).astype(jnp.int32) + (z > 0).astype(jnp.int32))

    def head(h):
        return pl.ds(h * DH, DH)

    def local_state():
        loads[0].wait()
        loads[1].wait()
        for h in range(H):
            local[h] = lax.dot_general(
                kb[:, head(h)],
                vb[:, head(h)],
                (((0,), (0,)), ((), ())),
                preferred_element_type=jnp.float32,
            )

    def intra(part):
        if part == 0:
            loads[2].wait()
        causal = lax.broadcasted_iota(jnp.int32, (rows, rows), 0) >= lax.broadcasted_iota(
            jnp.int32, (rows, rows), 1
        )
        for h in range(part * H // 2, (part + 1) * H // 2):
            scores = lax.dot_general(
                qb[:, head(h)],
                kb[:, head(h)],
                (((1,), (1,)), ((), ())),
                preferred_element_type=jnp.float32,
            )
            weights = jnp.where(causal, scores, 0.0).astype(jnp.bfloat16)
            attended[:, head(h)] = jnp.dot(
                weights, vb[:, head(h)], preferred_element_type=jnp.float32
            )

    def finish():
        for load in loads[3:8]:
            load.wait()
        square = jnp.zeros((rows, DH), jnp.float32)
        for h in range(H):
            both = attended[:, head(h)] + jnp.dot(
                qb[:, head(h)], prefix[h], preferred_element_type=jnp.float32
            )
            scale = lax.rsqrt(jnp.mean(both * both, axis=-1, keepdims=True) + 1e-06)
            wide = sb[:, head(h)].astype(jnp.float32) + both * scale * attn_gain_ref[:, head(h)]
            rounded = wide.astype(jnp.bfloat16)
            hidden[:, head(h)] = rounded
            wide = rounded.astype(jnp.float32)
            square = square + wide * wide
        scale = lax.rsqrt(jnp.sum(square, axis=-1, keepdims=True) / (H * DH) + 1e-06)
        for h in range(H):
            wide = hidden[:, head(h)].astype(jnp.float32)
            moe_in[:, head(h)] = (wide * scale * moe_gain_ref[:, head(h)]).astype(jnp.bfloat16)

    def activate(inputs, e):
        gate = jnp.dot(inputs, wg[e], preferred_element_type=jnp.float32)
        upper = jnp.dot(inputs, wu[e], preferred_element_type=jnp.float32)
        return (gate / (1.0 + jnp.exp(-gate)) * upper).astype(jnp.bfloat16)

    def down(acts, e):
        return jnp.dot(acts, wd[e], preferred_element_type=jnp.float32).astype(jnp.bfloat16)

    def weigh(made, e):
        chosen = jnp.sum(jnp.where(ids[...] == e, gw[...], 0.0), axis=0, keepdims=True)
        return made.astype(jnp.float32) * jnp.broadcast_to(chosen, (8, rows)).T[:, :1]

    def program(at):
        end = at in (0, n - 1)
        near = 1 if at == 0 else at - 1 if at == n - 1 else n - 1 - at
        outer = None if end else (0 if at < n - 1 - at else n - 1)
        sent = {}

        def push(sem, copy):
            sent[sem] = sent.get(sem, 0) + 1
            copy.start()

        def piece(kind, landed, e, t, half, sem, to, source=None):
            where = span(t, piece_of[kind], half)
            dst = held[t].at[e, where, :]
            return pltpu.make_async_remote_copy(
                src_ref=dst if source is None else source.at[0, where, :],
                dst_ref=dst,
                send_sem=send_sem.at[sem],
                recv_sem=landed,
                device_id=to,
                device_id_type=MESH,
            )

        def landing(kind, e, t, half):
            return piece_sem.at[kind, e, t, half]

        def doubled(e, t):
            return not end and abs(e - at) == 1

        def native(kind, t, half, to):
            landed = landing(kind, at, t, half)
            sem = 0 if to > at else 1
            push(sem, piece(kind, landed, at, t, half, sem, {"seq": to}, hbm[t]))

        def pass_on(kind, e, t, half):
            piece(kind, landing(kind, e, t, half), e, t, half, 0, to_x).wait_recv()
            if kind == M:
                if not end:
                    to = near if e == outer else outer
                    sem = 0 if to > at else 1
                    push(sem, piece(M, landing(M, e, t, half), e, t, half, sem, {"seq": to}))
                push(2, piece(M, landing(X, e, t, half), e, t, half, 2, to_x))
                push(3, piece(M, landing(Y, e, t, half), e, t, half, 3, to_y))
            if kind == X and half == 0 and not doubled(e, t):
                push(3, piece(X, landing(D, e, t, half), e, t, half, 3, to_y))
            if kind == Y and half == 1 and not doubled(e, t):
                push(2, piece(Y, landing(D, e, t, half), e, t, half, 2, to_x))
            sem = 4 + kind
            push(sem, piece(kind, sib_sem.at[e, t], e, t, half, sem, to_s))

        def from_sibling(e, t):
            half = held[t].at[e, pl.ds(0, held[t].shape[1] // 2), :]
            pltpu.make_async_copy(half, half, sib_sem.at[e, t]).wait()

        def state_copy(part):
            heads = pl.ds(part * (H // 4), H // 4)
            return pltpu.make_async_remote_copy(
                src_ref=passed.at[heads],
                dst_ref=prefix.at[heads],
                send_sem=state_send.at[part],
                recv_sem=state_recv.at[part],
                device_id={"seq": at + 1 if at < n - 1 else at - 1},
                device_id_type=MESH,
            )

        def first_state():
            prefix[...] = jnp.zeros_like(prefix)
            passed[...] = local[...].astype(passed.dtype)
            for part in range(4):
                state_copy(part).start()

        def next_state(part):
            state_copy(part).wait_recv()
            if at < n - 1:
                heads = pl.ds(part * (H // 4), H // 4)
                passed[heads] = (prefix[heads].astype(jnp.float32) + local[heads]).astype(
                    passed.dtype
                )
                state_copy(part).start()

        def row_copy(part):
            some = pl.ds(part * group, group)
            return pltpu.make_async_remote_copy(
                src_ref=rows_out.at[some],
                dst_ref=rows_in.at[some],
                send_sem=row_send.at[part],
                recv_sem=row_recv.at[part],
                device_id={"seq": near if end else outer},
                device_id_type=MESH,
            )

        def compact():
            named = jnp.max((ids[...] == near).astype(jnp.float32), axis=0, keepdims=True)
            earlier = lax.broadcasted_iota(jnp.int32, (rows, rows), 0) < lax.broadcasted_iota(
                jnp.int32, (rows, rows), 1
            )
            place = jnp.dot(
                jnp.broadcast_to(named, (8, rows)).astype(jnp.bfloat16),
                earlier.astype(jnp.bfloat16),
                preferred_element_type=jnp.float32,
            )[:1]
            slots = lax.broadcasted_iota(jnp.int32, (cap, rows), 0).astype(jnp.float32)
            pick[...] = jnp.where(slots == place, named, 0.0).astype(jnp.bfloat16)
            rows_out[...] = jnp.dot(
                pick[...], moe_in[...], preferred_element_type=jnp.float32
            ).astype(jnp.bfloat16)
            for part in range(3):
                row_copy(part).start()

        def serve(part):
            row_copy(part).wait_recv()
            some = pl.ds(part * group, group)
            rows_out[some] = down(activate(rows_in[some], at), at)
            row_copy(part).start()

        def served():
            for part in range(3):
                row_copy(part).wait_recv()
            made = lax.dot_general(
                pick[...],
                rows_in[...],
                (((0,), (0,)), ((), ())),
                preferred_element_type=jnp.float32,
            )
            return weigh(made, near)

        def own():
            for load in loads[8:]:
                load.wait()
            total[...] = weigh(down(activate(moe_in[...], at), at), at)

        def act(e):
            from_sibling(e, 0)
            from_sibling(e, 1)
            active[e] = activate(moe_in[...], e)

        def expert_out(e):
            from_sibling(e, 2)
            return weigh(down(active[e], e), e)

        def settle():
            for sem, count in sent.items():
                some = wg.at[:, pl.ds(0, wg.shape[1] // 64 * count), :]
                pltpu.make_async_copy(some, some, send_sem.at[sem]).wait()
            if at < n - 1:
                for part in range(4):
                    state_copy(part).wait_send()
            for part in range(3):
                row_copy(part).wait_send()

        items = PROGRAMS[at]
        started = False
        for index, item in enumerate(items):
            name, *rest = item
            if name <= D:
                pass_on(name, *rest)
            elif name == NATIVE:
                native(*rest)
            elif name == STATE:
                next_state(*rest)
            elif name == FIRST:
                first_state()
            elif name == LOCAL:
                local_state()
            elif name == INTRA:
                intra(*rest)
            elif name == FINISH:
                finish()
            elif name == COMPACT:
                compact()
            elif name == SERVE:
                serve(*rest)
            elif name == OWN:
                own()
            elif name == ACT:
                act(*rest)
            else:
                last = index == len(items) - 1
                if last:
                    settle()
                added = total[...] + (served() if name == SERVED else expert_out(*rest))
                if last:
                    out_ref[0] = (hidden[...].astype(jnp.float32) + added).astype(out_ref.dtype)
                else:
                    total[...] = added
            if name == LOCAL and not started:
                started = True
                for load in loads[4:]:
                    load.start()

    for at in range(n):

        @pl.when(z == at)
        def _():
            program(at)


def gathered_weights(
    n,
    queries,
    keys,
    values,
    stream,
    attn_gain,
    moe_gain,
    expert_ids,
    gate_weights,
    w_gate,
    w_up,
    w_down,
):
    rows, width = queries.shape[1:]
    units = w_gate.shape[2]
    cap = 3 * rows // n
    half = jnp.bfloat16
    anywhere = pl.BlockSpec(memory_space=pl.ANY)
    vmem = pl.BlockSpec(memory_space=pltpu.VMEM)
    dma = pltpu.SemaphoreType.DMA
    return pl.pallas_call(
        functools.partial(fused_kernel, n),
        out_shape=pltpu.VMEM((1, rows, width), half),
        in_specs=[anywhere] * 11,
        out_specs=vmem,
        scratch_shapes=[
            pltpu.VMEM((rows, width), half),
            pltpu.VMEM((rows, width), half),
            pltpu.VMEM((rows, width), half),
            pltpu.VMEM((rows, width), half),
            pltpu.VMEM((1, width), jnp.float32),
            pltpu.VMEM((1, width), jnp.float32),
            pltpu.VMEM((2, rows), jnp.int32),
            pltpu.VMEM((2, rows), jnp.float32),
            pltpu.VMEM((n, width, units), half),
            pltpu.VMEM((n, width, units), half),
            pltpu.VMEM((n, units, width), half),
            pltpu.VMEM((H, DH, DH), jnp.float32),
            pltpu.VMEM((H, DH, DH), half),
            pltpu.VMEM((H, DH, DH), half),
            pltpu.VMEM((rows, width), jnp.float32),
            pltpu.VMEM((rows, width), half),
            pltpu.VMEM((rows, width), half),
            pltpu.VMEM((rows, width), jnp.float32),
            pltpu.VMEM((n, rows, units), half),
            pltpu.VMEM((cap, rows), half),
            pltpu.VMEM((cap, width), half),
            pltpu.VMEM((cap, width), half),
            dma((11,)),
            dma((8,)),
            dma((4, n, 3, 2)),
            dma((n, 3)),
            dma((4,)),
            dma((4,)),
            dma((3,)),
            dma((3,)),
        ],
        compiler_params=pltpu.CompilerParams(
            collective_id=0, has_side_effects=True, vmem_limit_bytes=(64 << 20) - (600 << 10)
        ),
    )(
        queries,
        keys,
        values,
        stream,
        attn_gain[None],
        moe_gain[None],
        jnp.swapaxes(expert_ids, 1, 2),
        jnp.swapaxes(gate_weights, 1, 2),
        w_gate,
        w_up,
        w_down,
    )


def prefix_2(value, axis, join, neutral):
    count, mine = (lax.axis_size(axis), lax.axis_index(axis))
    pieces = lax.all_gather(value, axis)
    total = jnp.full_like(value, 0) + jnp.asarray(neutral, value.dtype)

    def lap(position, total):
        longer = join(total, pieces[position])
        return jnp.where(position < mine, longer, total)

    return lax.fori_loop(0, count - 1, lap, total)


def add_states(earlier, later):
    return earlier + later


def per_device(
    queries,
    keys,
    values,
    stream,
    attn_gain,
    moe_gain,
    expert_ids,
    gate_weights,
    w_gate,
    w_up,
    w_down,
):
    row_count = queries.shape[1]
    width = queries.shape[2]
    query_heads = queries[0].reshape(row_count, H, DH)
    key_heads = keys[0].reshape(row_count, H, DH)
    value_heads = values[0].reshape(row_count, H, DH)
    own_state = jnp.einsum(
        "shd,she->hde", key_heads, value_heads, preferred_element_type=jnp.float32
    )
    scores = jnp.einsum("thd,shd->hts", query_heads, key_heads, preferred_element_type=jnp.float32)
    causal = jnp.arange(row_count)[:, None] >= jnp.arange(row_count)[None, :]
    weights = jnp.where(causal[None], scores, jnp.zeros((), jnp.float32)).astype(jnp.bfloat16)
    intra = jnp.einsum("hts,shd->thd", weights, value_heads, preferred_element_type=jnp.float32)
    prefix = prefix_2(own_state, "seq", add_states, jnp.zeros_like(own_state))
    inter = jnp.einsum(
        "thd,hde->the", query_heads, prefix.astype(jnp.bfloat16), preferred_element_type=jnp.float32
    )
    attended = intra + inter
    normed = attended * lax.rsqrt(jnp.mean(attended * attended, axis=-1, keepdims=True) + 1e-06)
    hidden = (stream[0].astype(jnp.float32) + normed.reshape(row_count, width) * attn_gain).astype(
        jnp.bfloat16
    )
    hidden_wide = hidden.astype(jnp.float32)
    moe_in = (
        hidden_wide
        * lax.rsqrt(jnp.mean(hidden_wide * hidden_wide, axis=-1, keepdims=True) + 1e-06)
        * moe_gain
    ).astype(jnp.bfloat16)
    dest_count = lax.axis_size("seq")
    capacity = 3 * row_count // dest_count
    choice_ids = expert_ids[0].reshape(-1)
    place = jnp.arange(2 * row_count, dtype=jnp.int32)
    earlier = (choice_ids[:, None] == choice_ids[None, :]) & (place[:, None] > place[None, :])
    slot_rank = jnp.sum(earlier.astype(jnp.int32), axis=1)
    slot_index = choice_ids * capacity + slot_rank
    token_index = jnp.arange(2 * row_count, dtype=jnp.int32) // 2
    outgoing = (
        jnp.zeros((dest_count * capacity, width), jnp.bfloat16)
        .at[slot_index]
        .set(moe_in[token_index])
    )
    outgoing = outgoing.reshape(dest_count, capacity, width)
    received = lax.all_to_all(outgoing, "seq", split_axis=0, concat_axis=0, tiled=True)
    flat_rows = received.reshape(-1, width)
    gate = jnp.dot(flat_rows, w_gate[0], preferred_element_type=jnp.float32)
    upper = jnp.dot(flat_rows, w_up[0], preferred_element_type=jnp.float32)
    active = (jax.nn.silu(gate) * upper).astype(jnp.bfloat16)
    produced = jnp.dot(active, w_down[0], preferred_element_type=jnp.float32).astype(jnp.bfloat16)
    returned = lax.all_to_all(
        produced.reshape(received.shape), "seq", split_axis=0, concat_axis=0, tiled=True
    )
    picked = returned.reshape(-1, width)[slot_index].astype(jnp.float32)
    weighted = (gate_weights[0].reshape(-1)[:, None] * picked).reshape(row_count, 2, width)
    mixed = hidden_wide + (weighted[:, 0] + weighted[:, 1])
    return mixed.astype(jnp.bfloat16)[None]


def solution(mesh):
    placed = (
        P(("group", "rep"), "seq", None),
        P(("group", "rep"), "seq", None),
        P(("group", "rep"), "seq", None),
        P(("group", "rep"), "seq", None),
        P(),
        P(),
        P(("group", "rep"), "seq", None),
        P(("group", "rep"), "seq", None),
        P("seq", None, None),
        P("seq", None, None),
        P("seq", None, None),
    )
    ways = dict(mesh.shape)

    def plan(*args):
        n = ways["seq"]
        held = n * sum(w.size // w.shape[0] * w.dtype.itemsize for w in args[-3:])
        whole = args[-1].shape[1] % 256 == 0 and args[0].shape[1] % 64 == 0
        if ways["group"] == 2 and ways["rep"] == 4 and n == len(PROGRAMS) and whole and held <= GATHER_LIMIT:
            return gathered_weights(n, *args)
        return per_device(*args)

    return jax.shard_map(
        plan,
        mesh=mesh,
        in_specs=placed,
        out_specs=P(("group", "rep"), "seq", None),
        check_vma=False,
    )
```

```python
import functools

import jax
import jax.numpy as jnp
from jax import lax
from jax.experimental import pallas as pl
from jax.experimental.pallas import tpu as pltpu
from jax.sharding import PartitionSpec as P

H = 8
DH = 128
MESH = pl.DeviceIdType.MESH
GATHER_LIMIT = 24 << 20


DOUBLED = ((0, 1, 2), (1, 2), (1,))
M, X, Y, D, NATIVE, STATE, FIRST, LOCAL, INTRA, FINISH, COMPACT, OWN, ACT, DOWN, SERVE, SERVED = range(16)
PROGRAMS = (
    (
        (NATIVE, M, 0, 0, 1), (NATIVE, M, 0, 1, 1), (LOCAL,), (FIRST,), (NATIVE, M, 1, 0, 1), (NATIVE, M, 1, 1, 1),
        (NATIVE, M, 2, 0, 1), (NATIVE, M, 2, 1, 1), (INTRA, 0), (INTRA, 1), (FINISH,), (COMPACT,), (OWN,),
        (M, 2, 0, 0), (M, 2, 0, 1), (M, 2, 1, 0), (X, 2, 0, 0), (Y, 2, 0, 0), (M, 2, 1, 1), (X, 2, 0, 1),
        (Y, 2, 0, 1), (M, 3, 0, 0), (X, 2, 1, 0), (Y, 2, 1, 0), (M, 3, 0, 1), (X, 2, 1, 1), (D, 2, 0, 0),
        (D, 2, 0, 1), (Y, 2, 1, 1), (M, 3, 1, 0), (X, 3, 0, 0), (Y, 3, 0, 0), (M, 3, 1, 1), (X, 3, 0, 1),
        (D, 2, 1, 0), (M, 3, 2, 0), (D, 2, 1, 1), (Y, 3, 0, 1), (M, 3, 2, 1), (X, 3, 1, 0), (Y, 3, 1, 0),
        (NATIVE, D, 0, 0, 1), (M, 2, 2, 0), (X, 3, 1, 1), (D, 3, 0, 0), (NATIVE, D, 0, 1, 1), (M, 2, 2, 1),
        (X, 3, 2, 0), (Y, 3, 1, 1), (NATIVE, D, 1, 0, 1), (D, 3, 0, 1), (Y, 3, 2, 0), (ACT, 2), (NATIVE, D, 1, 1, 1),
        (X, 3, 2, 1), (Y, 3, 2, 1), (NATIVE, D, 2, 0, 1), (X, 2, 2, 0), (D, 3, 1, 0), (NATIVE, D, 2, 1, 1),
        (X, 2, 2, 1), (Y, 2, 2, 0), (D, 3, 1, 1), (Y, 2, 2, 1), (SERVED,), (D, 3, 2, 1), (D, 3, 2, 0), (ACT, 3),
        (DOWN, 3), (D, 2, 2, 0), (D, 2, 2, 1), (DOWN, 2),
    ),
    (
        (NATIVE, M, 0, 0, 2), (LOCAL,), (NATIVE, M, 0, 1, 2), (INTRA, 0), (INTRA, 1), (NATIVE, M, 1, 0, 2),
        (NATIVE, M, 1, 1, 2), (M, 2, 0, 0), (M, 0, 0, 0), (M, 2, 0, 1), (M, 0, 0, 1), (STATE, 0), (M, 2, 1, 0),
        (X, 2, 0, 0), (Y, 2, 0, 0), (STATE, 1), (M, 2, 1, 1), (X, 0, 0, 0), (Y, 0, 0, 0), (STATE, 2), (M, 3, 0, 0),
        (X, 2, 0, 1), (Y, 2, 0, 1), (STATE, 3), (M, 3, 0, 1), (FINISH,), (X, 0, 0, 1), (Y, 0, 0, 1), (OWN,),
        (M, 0, 1, 0), (Y, 2, 1, 0), (M, 0, 1, 1), (M, 3, 1, 0), (M, 3, 1, 1), (X, 2, 1, 0), (X, 2, 1, 1),
        (D, 2, 0, 0), (M, 0, 2, 0), (M, 3, 2, 0), (X, 3, 0, 0), (Y, 2, 1, 1), (M, 0, 2, 1), (M, 3, 2, 1),
        (D, 2, 0, 1), (Y, 3, 0, 0), (M, 2, 2, 0), (X, 3, 0, 1), (Y, 3, 0, 1), (NATIVE, M, 2, 0, 2), (M, 2, 2, 1),
        (SERVE, 0), (X, 0, 1, 0), (Y, 0, 1, 0), (NATIVE, M, 2, 1, 2), (D, 3, 1, 0), (X, 0, 1, 1), (Y, 0, 1, 1),
        (NATIVE, D, 1, 0, 2), (D, 3, 1, 1), (SERVE, 1), (Y, 3, 1, 0), (X, 3, 1, 0), (NATIVE, D, 1, 1, 2),
        (D, 2, 1, 0), (X, 3, 1, 1), (Y, 3, 1, 1), (NATIVE, D, 2, 0, 2), (D, 2, 1, 1), (SERVE, 2), (Y, 0, 2, 0),
        (X, 0, 2, 0), (ACT, 2), (D, 0, 0, 0), (D, 2, 2, 0), (X, 3, 2, 0), (Y, 3, 2, 0), (NATIVE, D, 2, 1, 2),
        (D, 0, 0, 1), (D, 2, 2, 1), (X, 0, 2, 1), (D, 3, 0, 0), (D, 0, 1, 0), (X, 3, 2, 1), (Y, 0, 2, 1),
        (D, 0, 1, 1), (X, 2, 2, 0), (Y, 3, 2, 1), (ACT, 0), (D, 0, 2, 0), (D, 3, 0, 1), (Y, 2, 2, 0), (D, 0, 2, 1),
        (ACT, 3), (Y, 2, 2, 1), (X, 2, 2, 1), (DOWN, 0), (D, 3, 2, 1), (D, 3, 2, 0), (DOWN, 2), (DOWN, 3),
    ),
    (
        (NATIVE, M, 0, 0, 1), (LOCAL,), (NATIVE, M, 0, 1, 1), (INTRA, 0), (INTRA, 1), (NATIVE, M, 1, 0, 1),
        (NATIVE, M, 1, 1, 1), (M, 1, 0, 0), (M, 3, 0, 0), (M, 1, 0, 1), (M, 3, 0, 1), (M, 1, 1, 0), (M, 3, 1, 0),
        (X, 1, 0, 0), (Y, 1, 0, 0), (M, 1, 1, 1), (M, 3, 1, 1), (X, 3, 0, 0), (Y, 3, 0, 0), (M, 0, 0, 0),
        (M, 3, 2, 0), (X, 1, 0, 1), (Y, 1, 0, 1), (M, 0, 0, 1), (M, 3, 2, 1), (X, 3, 0, 1), (Y, 3, 0, 1), (STATE, 0),
        (D, 3, 0, 0), (X, 1, 1, 0), (Y, 1, 1, 0), (NATIVE, M, 2, 0, 1), (STATE, 1), (D, 3, 0, 1), (X, 3, 1, 0),
        (Y, 3, 1, 0), (NATIVE, M, 2, 1, 1), (STATE, 2), (D, 3, 1, 0), (X, 1, 1, 1), (D, 1, 0, 0), (STATE, 3),
        (FINISH,), (D, 3, 1, 1), (X, 3, 1, 1), (Y, 1, 1, 1), (M, 0, 1, 0), (X, 0, 0, 0), (Y, 3, 1, 1),
        (NATIVE, D, 1, 0, 1), (M, 0, 1, 1), (ACT, 3), (Y, 0, 0, 0), (X, 3, 2, 0), (NATIVE, D, 1, 1, 1), (M, 0, 2, 0),
        (D, 1, 0, 1), (Y, 3, 2, 0), (D, 3, 2, 0), (NATIVE, D, 2, 0, 1), (M, 0, 2, 1), (X, 0, 0, 1), (Y, 0, 0, 1),
        (D, 3, 2, 1), (NATIVE, D, 2, 1, 1), (M, 1, 2, 0), (X, 3, 2, 1), (Y, 3, 2, 1), (M, 1, 2, 1), (DOWN, 3),
        (X, 0, 1, 0), (Y, 0, 1, 0), (SERVE, 0), (X, 0, 1, 1), (D, 0, 0, 0), (D, 1, 1, 0), (OWN,), (Y, 0, 1, 1),
        (D, 1, 1, 1), (X, 0, 2, 0), (SERVE, 1), (D, 1, 2, 0), (Y, 0, 2, 0), (X, 0, 2, 1), (ACT, 1), (D, 1, 2, 1),
        (D, 0, 0, 1), (Y, 0, 2, 1), (SERVE, 2), (X, 1, 2, 0), (D, 0, 1, 0), (Y, 1, 2, 0), (D, 0, 1, 1), (X, 1, 2, 1),
        (Y, 1, 2, 1), (ACT, 0), (D, 0, 2, 1), (D, 0, 2, 0), (DOWN, 1), (DOWN, 0),
    ),
    (
        (NATIVE, M, 0, 0, 2), (NATIVE, M, 0, 1, 2), (NATIVE, M, 1, 0, 2), (NATIVE, M, 1, 1, 2), (LOCAL,), (INTRA, 0),
        (INTRA, 1), (NATIVE, M, 2, 0, 2), (NATIVE, M, 2, 1, 2), (M, 1, 0, 0), (NATIVE, D, 0, 0, 2), (M, 1, 0, 1),
        (NATIVE, D, 0, 1, 2), (M, 1, 1, 0), (X, 1, 0, 0), (Y, 1, 0, 0), (NATIVE, D, 1, 0, 2), (M, 1, 1, 1),
        (X, 1, 0, 1), (Y, 1, 0, 1), (NATIVE, D, 1, 1, 2), (M, 0, 0, 0), (X, 1, 1, 0), (Y, 1, 1, 0), (M, 0, 0, 1),
        (X, 1, 1, 1), (D, 1, 0, 0), (STATE, 0), (D, 1, 0, 1), (Y, 1, 1, 1), (STATE, 1), (X, 0, 0, 0), (Y, 0, 0, 0),
        (STATE, 2), (NATIVE, D, 2, 0, 2), (X, 0, 0, 1), (D, 1, 1, 0), (NATIVE, D, 2, 1, 2), (STATE, 3), (FINISH,),
        (Y, 0, 0, 1), (D, 1, 1, 1), (COMPACT,), (M, 0, 1, 0), (D, 0, 0, 0), (OWN,), (M, 0, 1, 1), (ACT, 1),
        (M, 0, 2, 0), (D, 0, 0, 1), (Y, 0, 1, 0), (M, 0, 2, 1), (X, 0, 1, 0), (Y, 0, 1, 1), (M, 1, 2, 0),
        (X, 0, 1, 1), (Y, 0, 2, 0), (M, 1, 2, 1), (X, 0, 2, 0), (Y, 0, 2, 1), (X, 0, 2, 1), (D, 0, 1, 0),
        (D, 0, 1, 1), (Y, 1, 2, 0), (ACT, 0), (X, 1, 2, 0), (Y, 1, 2, 1), (X, 1, 2, 1), (D, 0, 2, 0), (D, 0, 2, 1),
        (D, 1, 2, 0), (DOWN, 0), (D, 1, 2, 1), (SERVED,), (DOWN, 1),
    ),
)


def fused_kernel(
    n,
    q_hbm,
    k_hbm,
    v_hbm,
    s_hbm,
    attn_gain_hbm,
    moe_gain_hbm,
    ids_hbm,
    gw_hbm,
    wg_hbm,
    wu_hbm,
    wd_hbm,
    out_ref,
    qb,
    kb,
    vb,
    sb,
    attn_gain_ref,
    moe_gain_ref,
    ids,
    gw,
    wg,
    wu,
    wd,
    local,
    prefix,
    passed,
    attended,
    hidden,
    moe_in,
    total,
    active,
    pick,
    rows_out,
    rows_in,
    load_sem,
    send_sem,
    piece_sem,
    sib_sem,
    state_send,
    state_recv,
    row_send,
    row_recv,
):
    g, z, r = lax.axis_index("group"), lax.axis_index("seq"), lax.axis_index("rep")
    x, c = r // 2, r % 2
    r_x, r_s = 2 * (1 - x) + c, 2 * x + (1 - c)
    piece_of = {
        M: g * 4 + r,
        X: g * 4 + r_x,
        Y: (1 - g) * 4 + r,
        D: (1 - g) * 4 + r_x,
    }
    to_x, to_y, to_s = {"rep": r_x}, {"group": 1 - g}, {"rep": r_s}
    rows = qb.shape[0]
    cap = rows_in.shape[0]
    group = cap // 3
    hbm = (wg_hbm, wu_hbm, wd_hbm)
    held = (wg, wu, wd)

    def span(t, piece, half):
        size = held[t].shape[1] // 16
        return pl.ds(pl.multiple_of(piece * 2 * size + half * size, size), size)

    barrier = pltpu.get_barrier_semaphore()
    for to in (to_x, to_y, to_s):
        pl.semaphore_signal(barrier, inc=1, device_id=to, device_id_type=MESH)

    @pl.when(z < n - 1)
    def _():
        pl.semaphore_signal(barrier, inc=1, device_id={"seq": z + 1}, device_id_type=MESH)

    @pl.when(z > 0)
    def _():
        pl.semaphore_signal(barrier, inc=1, device_id={"seq": z - 1}, device_id_type=MESH)

    loads = [
        pltpu.make_async_copy(src, dst, load_sem.at[i])
        for i, (src, dst) in enumerate(
            [
                (k_hbm.at[0], kb),
                (v_hbm.at[0], vb),
                (q_hbm.at[0], qb),
                (s_hbm.at[0], sb),
                (attn_gain_hbm, attn_gain_ref),
                (moe_gain_hbm, moe_gain_ref),
                (ids_hbm.at[0], ids),
                (gw_hbm.at[0], gw),
                (wg_hbm.at[0], wg.at[z]),
                (wu_hbm.at[0], wu.at[z]),
                (wd_hbm.at[0], wd.at[z]),
            ]
        )
    ]
    for load in loads[:4]:
        load.start()
    pl.semaphore_wait(barrier, 3 + (z < n - 1).astype(jnp.int32) + (z > 0).astype(jnp.int32))

    def head(h):
        return pl.ds(h * DH, DH)

    def local_state():
        loads[0].wait()
        loads[1].wait()
        for h in range(H):
            local[h] = lax.dot_general(
                kb[:, head(h)],
                vb[:, head(h)],
                (((0,), (0,)), ((), ())),
                preferred_element_type=jnp.float32,
            )

    def intra(part):
        if part == 0:
            loads[2].wait()
        causal = lax.broadcasted_iota(jnp.int32, (rows, rows), 0) >= lax.broadcasted_iota(
            jnp.int32, (rows, rows), 1
        )
        for h in range(part * H // 2, (part + 1) * H // 2):
            scores = lax.dot_general(
                qb[:, head(h)],
                kb[:, head(h)],
                (((1,), (1,)), ((), ())),
                preferred_element_type=jnp.float32,
            )
            weights = jnp.where(causal, scores, 0.0).astype(jnp.bfloat16)
            attended[:, head(h)] = jnp.dot(
                weights, vb[:, head(h)], preferred_element_type=jnp.float32
            )

    def finish():
        for load in loads[3:8]:
            load.wait()
        square = jnp.zeros((rows, DH), jnp.float32)
        for h in range(H):
            both = attended[:, head(h)] + jnp.dot(
                qb[:, head(h)], prefix[h], preferred_element_type=jnp.float32
            )
            scale = lax.rsqrt(jnp.mean(both * both, axis=-1, keepdims=True) + 1e-06)
            wide = sb[:, head(h)].astype(jnp.float32) + both * scale * attn_gain_ref[:, head(h)]
            rounded = wide.astype(jnp.bfloat16)
            hidden[:, head(h)] = rounded
            wide = rounded.astype(jnp.float32)
            square = square + wide * wide
        scale = lax.rsqrt(jnp.sum(square, axis=-1, keepdims=True) / (H * DH) + 1e-06)
        for h in range(H):
            wide = hidden[:, head(h)].astype(jnp.float32)
            moe_in[:, head(h)] = (wide * scale * moe_gain_ref[:, head(h)]).astype(jnp.bfloat16)

    def activate(inputs, e):
        gate = jnp.dot(inputs, wg[e], preferred_element_type=jnp.float32)
        upper = jnp.dot(inputs, wu[e], preferred_element_type=jnp.float32)
        return (gate / (1.0 + jnp.exp(-gate)) * upper).astype(jnp.bfloat16)

    def down(acts, e):
        return jnp.dot(acts, wd[e], preferred_element_type=jnp.float32).astype(jnp.bfloat16)

    def weigh(made, e):
        chosen = jnp.sum(jnp.where(ids[...] == e, gw[...], 0.0), axis=0, keepdims=True)
        return made.astype(jnp.float32) * jnp.broadcast_to(chosen, (8, rows)).T[:, :1]

    def program(at):
        end = at in (0, n - 1)
        near = 1 if at == 0 else at - 1 if at == n - 1 else n - 1 - at
        outer = None if end else (0 if at < n - 1 - at else n - 1)
        sent = {}

        def push(sem, copy):
            sent[sem] = sent.get(sem, 0) + 1
            copy.start()

        def piece(kind, landed, e, t, half, sem, to, source=None):
            where = span(t, piece_of[kind], half)
            dst = held[t].at[e, where, :]
            return pltpu.make_async_remote_copy(
                src_ref=dst if source is None else source.at[0, where, :],
                dst_ref=dst,
                send_sem=send_sem.at[sem],
                recv_sem=landed,
                device_id=to,
                device_id_type=MESH,
            )

        def landing(kind, e, t, half):
            return piece_sem.at[kind, e, t, half]

        def doubled(e, t):
            origin = 0 if e == outer else 1 if e == near else 2
            return not end and t in DOUBLED[origin]

        def native(kind, t, half, to):
            landed = landing(kind, at, t, half)
            sem = 0 if to > at else 1
            push(sem, piece(kind, landed, at, t, half, sem, {"seq": to}, hbm[t]))

        def pass_on(kind, e, t, half):
            piece(kind, landing(kind, e, t, half), e, t, half, 0, to_x).wait_recv()
            if kind == M:
                if not end:
                    to = near if e == outer else outer
                    sem = 0 if to > at else 1
                    push(sem, piece(M, landing(M, e, t, half), e, t, half, sem, {"seq": to}))
                push(2, piece(M, landing(X, e, t, half), e, t, half, 2, to_x))
                push(3, piece(M, landing(Y, e, t, half), e, t, half, 3, to_y))
            if kind == D and not end and e == outer and t in DOUBLED[2]:
                sem = 0 if near > at else 1
                push(sem, piece(D, landing(D, e, t, half), e, t, half, sem, {"seq": near}))
            if kind == X and half == 0 and not doubled(e, t):
                push(3, piece(X, landing(D, e, t, half), e, t, half, 3, to_y))
            if kind == Y and half == 1 and not doubled(e, t):
                push(2, piece(Y, landing(D, e, t, half), e, t, half, 2, to_x))
            sem = 4 + kind
            push(sem, piece(kind, sib_sem.at[e, t], e, t, half, sem, to_s))

        def from_sibling(e, t):
            half = held[t].at[e, pl.ds(0, held[t].shape[1] // 2), :]
            pltpu.make_async_copy(half, half, sib_sem.at[e, t]).wait()

        def state_copy(part):
            heads = pl.ds(part * (H // 4), H // 4)
            return pltpu.make_async_remote_copy(
                src_ref=passed.at[heads],
                dst_ref=prefix.at[heads],
                send_sem=state_send.at[part],
                recv_sem=state_recv.at[part],
                device_id={"seq": at + 1 if at < n - 1 else at - 1},
                device_id_type=MESH,
            )

        def first_state():
            prefix[...] = jnp.zeros_like(prefix)
            passed[...] = local[...].astype(passed.dtype)
            for part in range(4):
                state_copy(part).start()

        def next_state(part):
            state_copy(part).wait_recv()
            if at < n - 1:
                heads = pl.ds(part * (H // 4), H // 4)
                passed[heads] = (prefix[heads].astype(jnp.float32) + local[heads]).astype(
                    passed.dtype
                )
                state_copy(part).start()

        def row_copy(part):
            some = pl.ds(part * group, group)
            return pltpu.make_async_remote_copy(
                src_ref=rows_out.at[some],
                dst_ref=rows_in.at[some],
                send_sem=row_send.at[part],
                recv_sem=row_recv.at[part],
                device_id={"seq": near if end else outer},
                device_id_type=MESH,
            )

        def compact():
            named = jnp.max((ids[...] == near).astype(jnp.float32), axis=0, keepdims=True)
            earlier = lax.broadcasted_iota(jnp.int32, (rows, rows), 0) < lax.broadcasted_iota(
                jnp.int32, (rows, rows), 1
            )
            place = jnp.dot(
                jnp.broadcast_to(named, (8, rows)).astype(jnp.bfloat16),
                earlier.astype(jnp.bfloat16),
                preferred_element_type=jnp.float32,
            )[:1]
            slots = lax.broadcasted_iota(jnp.int32, (cap, rows), 0).astype(jnp.float32)
            pick[...] = jnp.where(slots == place, named, 0.0).astype(jnp.bfloat16)
            rows_out[...] = jnp.dot(
                pick[...], moe_in[...], preferred_element_type=jnp.float32
            ).astype(jnp.bfloat16)
            for part in range(3):
                row_copy(part).start()

        def serve(part):
            row_copy(part).wait_recv()
            some = pl.ds(part * group, group)
            rows_out[some] = down(activate(rows_in[some], at), at)
            row_copy(part).start()

        def served():
            for part in range(3):
                row_copy(part).wait_recv()
            made = lax.dot_general(
                pick[...],
                rows_in[...],
                (((0,), (0,)), ((), ())),
                preferred_element_type=jnp.float32,
            )
            return weigh(made, near)

        def own():
            return weigh(down(activate(moe_in[...], at), at), at)

        def act(e):
            from_sibling(e, 0)
            from_sibling(e, 1)
            active[e] = activate(moe_in[...], e)

        def expert_out(e):
            from_sibling(e, 2)
            return weigh(down(active[e], e), e)

        def settle():
            for sem, count in sent.items():
                some = wg.at[:, pl.ds(0, wg.shape[1] // 64 * count), :]
                pltpu.make_async_copy(some, some, send_sem.at[sem]).wait()
            if at < n - 1:
                for part in range(4):
                    state_copy(part).wait_send()
            for part in range(3):
                row_copy(part).wait_send()

        items = PROGRAMS[at]
        started = ready = begun = False
        for index, item in enumerate(items):
            name, *rest = item
            if name in (OWN, SERVE) and not ready:
                ready = True
                for load in loads[8:]:
                    load.wait()
            if name <= D:
                pass_on(name, *rest)
            elif name == NATIVE:
                native(*rest)
            elif name == STATE:
                next_state(*rest)
            elif name == FIRST:
                first_state()
            elif name == LOCAL:
                local_state()
            elif name == INTRA:
                intra(*rest)
            elif name == FINISH:
                finish()
            elif name == COMPACT:
                compact()
            elif name == SERVE:
                serve(*rest)
            elif name == ACT:
                act(*rest)
            else:
                last = index == len(items) - 1
                if last:
                    settle()
                if name == OWN:
                    added = own()
                else:
                    added = served() if name == SERVED else expert_out(*rest)
                if begun:
                    added = total[...] + added
                begun = True
                if last:
                    out_ref[0] = (hidden[...].astype(jnp.float32) + added).astype(out_ref.dtype)
                else:
                    total[...] = added
            if name == LOCAL and not started:
                started = True
                for load in loads[4:]:
                    load.start()

    for at in range(n):

        @pl.when(z == at)
        def _():
            program(at)


def gathered_weights(
    n,
    queries,
    keys,
    values,
    stream,
    attn_gain,
    moe_gain,
    expert_ids,
    gate_weights,
    w_gate,
    w_up,
    w_down,
):
    rows, width = queries.shape[1:]
    units = w_gate.shape[2]
    cap = 3 * rows // n
    half = jnp.bfloat16
    anywhere = pl.BlockSpec(memory_space=pl.ANY)
    vmem = pl.BlockSpec(memory_space=pltpu.VMEM)
    dma = pltpu.SemaphoreType.DMA
    return pl.pallas_call(
        functools.partial(fused_kernel, n),
        out_shape=pltpu.VMEM((1, rows, width), half),
        in_specs=[anywhere] * 11,
        out_specs=vmem,
        scratch_shapes=[
            pltpu.VMEM((rows, width), half),
            pltpu.VMEM((rows, width), half),
            pltpu.VMEM((rows, width), half),
            pltpu.VMEM((rows, width), half),
            pltpu.VMEM((1, width), jnp.float32),
            pltpu.VMEM((1, width), jnp.float32),
            pltpu.VMEM((2, rows), jnp.int32),
            pltpu.VMEM((2, rows), jnp.float32),
            pltpu.VMEM((n, width, units), half),
            pltpu.VMEM((n, width, units), half),
            pltpu.VMEM((n, units, width), half),
            pltpu.VMEM((H, DH, DH), jnp.float32),
            pltpu.VMEM((H, DH, DH), half),
            pltpu.VMEM((H, DH, DH), half),
            pltpu.VMEM((rows, width), jnp.float32),
            pltpu.VMEM((rows, width), half),
            pltpu.VMEM((rows, width), half),
            pltpu.VMEM((rows, width), jnp.float32),
            pltpu.VMEM((n, rows, units), half),
            pltpu.VMEM((cap, rows), half),
            pltpu.VMEM((cap, width), half),
            pltpu.VMEM((cap, width), half),
            dma((11,)),
            dma((8,)),
            dma((4, n, 3, 2)),
            dma((n, 3)),
            dma((4,)),
            dma((4,)),
            dma((3,)),
            dma((3,)),
        ],
        compiler_params=pltpu.CompilerParams(
            collective_id=0, has_side_effects=True, vmem_limit_bytes=(64 << 20) - (600 << 10)
        ),
    )(
        queries,
        keys,
        values,
        stream,
        attn_gain[None],
        moe_gain[None],
        jnp.swapaxes(expert_ids, 1, 2),
        jnp.swapaxes(gate_weights, 1, 2),
        w_gate,
        w_up,
        w_down,
    )


def prefix_2(value, axis, join, neutral):
    count, mine = (lax.axis_size(axis), lax.axis_index(axis))
    pieces = lax.all_gather(value, axis)
    total = jnp.full_like(value, 0) + jnp.asarray(neutral, value.dtype)

    def lap(position, total):
        longer = join(total, pieces[position])
        return jnp.where(position < mine, longer, total)

    return lax.fori_loop(0, count - 1, lap, total)


def add_states(earlier, later):
    return earlier + later


def per_device(
    queries,
    keys,
    values,
    stream,
    attn_gain,
    moe_gain,
    expert_ids,
    gate_weights,
    w_gate,
    w_up,
    w_down,
):
    row_count = queries.shape[1]
    width = queries.shape[2]
    query_heads = queries[0].reshape(row_count, H, DH)
    key_heads = keys[0].reshape(row_count, H, DH)
    value_heads = values[0].reshape(row_count, H, DH)
    own_state = jnp.einsum(
        "shd,she->hde", key_heads, value_heads, preferred_element_type=jnp.float32
    )
    scores = jnp.einsum("thd,shd->hts", query_heads, key_heads, preferred_element_type=jnp.float32)
    causal = jnp.arange(row_count)[:, None] >= jnp.arange(row_count)[None, :]
    weights = jnp.where(causal[None], scores, jnp.zeros((), jnp.float32)).astype(jnp.bfloat16)
    intra = jnp.einsum("hts,shd->thd", weights, value_heads, preferred_element_type=jnp.float32)
    prefix = prefix_2(own_state, "seq", add_states, jnp.zeros_like(own_state))
    inter = jnp.einsum(
        "thd,hde->the", query_heads, prefix.astype(jnp.bfloat16), preferred_element_type=jnp.float32
    )
    attended = intra + inter
    normed = attended * lax.rsqrt(jnp.mean(attended * attended, axis=-1, keepdims=True) + 1e-06)
    hidden = (stream[0].astype(jnp.float32) + normed.reshape(row_count, width) * attn_gain).astype(
        jnp.bfloat16
    )
    hidden_wide = hidden.astype(jnp.float32)
    moe_in = (
        hidden_wide
        * lax.rsqrt(jnp.mean(hidden_wide * hidden_wide, axis=-1, keepdims=True) + 1e-06)
        * moe_gain
    ).astype(jnp.bfloat16)
    dest_count = lax.axis_size("seq")
    capacity = 3 * row_count // dest_count
    choice_ids = expert_ids[0].reshape(-1)
    place = jnp.arange(2 * row_count, dtype=jnp.int32)
    earlier = (choice_ids[:, None] == choice_ids[None, :]) & (place[:, None] > place[None, :])
    slot_rank = jnp.sum(earlier.astype(jnp.int32), axis=1)
    slot_index = choice_ids * capacity + slot_rank
    token_index = jnp.arange(2 * row_count, dtype=jnp.int32) // 2
    outgoing = (
        jnp.zeros((dest_count * capacity, width), jnp.bfloat16)
        .at[slot_index]
        .set(moe_in[token_index])
    )
    outgoing = outgoing.reshape(dest_count, capacity, width)
    received = lax.all_to_all(outgoing, "seq", split_axis=0, concat_axis=0, tiled=True)
    flat_rows = received.reshape(-1, width)
    gate = jnp.dot(flat_rows, w_gate[0], preferred_element_type=jnp.float32)
    upper = jnp.dot(flat_rows, w_up[0], preferred_element_type=jnp.float32)
    active = (jax.nn.silu(gate) * upper).astype(jnp.bfloat16)
    produced = jnp.dot(active, w_down[0], preferred_element_type=jnp.float32).astype(jnp.bfloat16)
    returned = lax.all_to_all(
        produced.reshape(received.shape), "seq", split_axis=0, concat_axis=0, tiled=True
    )
    picked = returned.reshape(-1, width)[slot_index].astype(jnp.float32)
    weighted = (gate_weights[0].reshape(-1)[:, None] * picked).reshape(row_count, 2, width)
    mixed = hidden_wide + (weighted[:, 0] + weighted[:, 1])
    return mixed.astype(jnp.bfloat16)[None]


def solution(mesh):
    placed = (
        P(("group", "rep"), "seq", None),
        P(("group", "rep"), "seq", None),
        P(("group", "rep"), "seq", None),
        P(("group", "rep"), "seq", None),
        P(),
        P(),
        P(("group", "rep"), "seq", None),
        P(("group", "rep"), "seq", None),
        P("seq", None, None),
        P("seq", None, None),
        P("seq", None, None),
    )
    ways = dict(mesh.shape)

    def plan(*args):
        n = ways["seq"]
        held = n * sum(w.size // w.shape[0] * w.dtype.itemsize for w in args[-3:])
        whole = args[-1].shape[1] % 256 == 0 and args[0].shape[1] % 64 == 0
        if ways["group"] == 2 and ways["rep"] == 4 and n == len(PROGRAMS) and whole and held <= GATHER_LIMIT:
            return gathered_weights(n, *args)
        return per_device(*args)

    return jax.shard_map(
        plan,
        mesh=mesh,
        in_specs=placed,
        out_specs=P(("group", "rep"), "seq", None),
        check_vma=False,
    )
```

```python
import functools

import jax
import jax.numpy as jnp
from jax import lax
from jax.experimental import pallas as pl
from jax.experimental.pallas import tpu as pltpu
from jax.sharding import PartitionSpec as P

H = 8
DH = 128
MESH = pl.DeviceIdType.MESH
GATHER_LIMIT = 24 << 20


ASKED = 2
ROW_PARTS = 3
STATE_PARTS = 4
DOUBLED = ((0, 1, 2), (1,), (1, 2), (1,))
M, X, Y, D, NATIVE, STATE, FIRST, LOCAL, INTRA, FINISH, COMPACT, OWN, ACT, DOWN, SERVE, SERVED = range(16)
PROGRAMS = (
    (
        (LOCAL,), (FIRST,), (INTRA, 0), (NATIVE, M, 0, 0, 1), (NATIVE, M, 0, 1, 1), (NATIVE, M, 1, 0, 1),
        (NATIVE, M, 1, 1, 1), (NATIVE, M, 2, 0, 1), (NATIVE, M, 2, 1, 1), (INTRA, 1), (FINISH,), (COMPACT,),
        (M, 1, 2, 0), (M, 1, 2, 1), (M, 1, 0, 0), (X, 1, 2, 0), (Y, 1, 2, 0), (M, 1, 0, 1), (X, 1, 2, 1),
        (Y, 1, 2, 1), (OWN,), (Y, 1, 0, 0), (M, 1, 1, 0), (X, 1, 0, 0), (M, 1, 1, 1), (X, 1, 0, 1), (D, 1, 2, 0),
        (D, 1, 1, 0), (D, 1, 2, 1), (Y, 1, 0, 1), (D, 1, 1, 1), (X, 1, 1, 0), (Y, 1, 1, 0), (M, 3, 1, 0),
        (X, 1, 1, 1), (D, 1, 0, 0), (M, 3, 1, 1), (D, 1, 0, 1), (Y, 1, 1, 1), (M, 3, 0, 0), (ACT, 1), (Y, 3, 1, 0),
        (X, 3, 1, 0), (NATIVE, D, 2, 0, 1), (DOWN, 1), (M, 3, 0, 1), (X, 3, 1, 1), (Y, 3, 1, 1), (NATIVE, D, 2, 1, 1),
        (M, 3, 2, 0), (X, 3, 0, 0), (Y, 3, 0, 0), (M, 3, 2, 1), (D, 3, 1, 0), (X, 3, 0, 1), (NATIVE, D, 1, 0, 1),
        (NATIVE, D, 1, 1, 1), (Y, 3, 0, 1), (D, 3, 1, 1), (NATIVE, D, 0, 0, 1), (Y, 3, 2, 0), (NATIVE, D, 0, 1, 1),
        (X, 3, 2, 0), (D, 3, 0, 0), (X, 3, 2, 1), (Y, 3, 2, 1), (D, 3, 0, 1), (ACT, 3), (D, 3, 2, 0), (D, 3, 2, 1),
        (DOWN, 3), (SERVED,),
    ),
    (
        (NATIVE, M, 1, 0, 2), (NATIVE, M, 1, 1, 2), (NATIVE, M, 2, 0, 0), (NATIVE, M, 2, 1, 0), (LOCAL,), (INTRA, 0),
        (NATIVE, M, 0, 0, 2), (NATIVE, M, 0, 1, 2), (NATIVE, M, 0, 0, 0), (NATIVE, M, 0, 1, 0), (NATIVE, M, 2, 0, 2),
        (INTRA, 1), (NATIVE, M, 1, 0, 0), (NATIVE, M, 2, 1, 2), (NATIVE, M, 1, 1, 0), (M, 2, 0, 0), (STATE, 0),
        (NATIVE, D, 1, 0, 0), (M, 2, 0, 1), (STATE, 1), (NATIVE, D, 1, 1, 0), (M, 2, 2, 0), (STATE, 2), (X, 2, 0, 0),
        (Y, 2, 0, 0), (M, 2, 2, 1), (STATE, 3), (X, 2, 0, 1), (Y, 2, 0, 1), (FINISH,), (M, 2, 1, 0), (M, 0, 0, 0),
        (X, 2, 2, 0), (Y, 2, 2, 0), (M, 2, 1, 1), (M, 0, 0, 1), (D, 2, 0, 0), (X, 2, 2, 1), (M, 3, 1, 0),
        (M, 0, 1, 0), (D, 2, 0, 1), (Y, 2, 2, 1), (M, 3, 1, 1), (M, 0, 1, 1), (Y, 2, 1, 0), (X, 2, 1, 0),
        (M, 3, 0, 0), (M, 0, 2, 0), (X, 0, 0, 0), (Y, 0, 0, 0), (M, 3, 0, 1), (M, 0, 2, 1), (D, 2, 2, 0),
        (X, 2, 1, 1), (M, 3, 2, 0), (X, 0, 0, 1), (Y, 2, 1, 1), (NATIVE, D, 1, 0, 2), (M, 3, 2, 1), (OWN,),
        (D, 2, 1, 0), (X, 3, 1, 0), (Y, 0, 0, 1), (NATIVE, D, 1, 1, 2), (X, 0, 1, 0), (Y, 3, 1, 0), (D, 2, 1, 1),
        (D, 2, 2, 1), (Y, 0, 1, 0), (ACT, 2), (D, 3, 2, 0), (DOWN, 2), (X, 3, 1, 1), (Y, 3, 1, 1), (SERVE, 0),
        (D, 3, 2, 1), (Y, 0, 1, 1), (X, 0, 1, 1), (SERVE, 1), (D, 3, 1, 0), (SERVE, 2), (D, 0, 2, 0), (X, 3, 0, 0),
        (Y, 3, 0, 0), (D, 3, 1, 1), (D, 0, 2, 1), (X, 0, 2, 0), (Y, 0, 2, 0), (D, 0, 1, 0), (X, 3, 0, 1),
        (Y, 3, 0, 1), (D, 0, 1, 1), (X, 0, 2, 1), (Y, 0, 2, 1), (D, 0, 0, 0), (X, 3, 2, 0), (Y, 3, 2, 0),
        (D, 0, 0, 1), (X, 3, 2, 1), (Y, 3, 2, 1), (ACT, 0), (D, 3, 0, 1), (D, 3, 0, 0), (DOWN, 0), (ACT, 3),
        (DOWN, 3),
    ),
    (
        (NATIVE, M, 0, 0, 1), (NATIVE, M, 0, 1, 1), (LOCAL,), (INTRA, 0), (NATIVE, M, 2, 0, 1), (NATIVE, M, 2, 1, 1),
        (INTRA, 1), (NATIVE, M, 1, 0, 1), (NATIVE, M, 1, 1, 1), (M, 1, 1, 0), (M, 3, 1, 0), (M, 1, 1, 1),
        (M, 3, 1, 1), (M, 1, 0, 0), (M, 3, 0, 0), (X, 1, 1, 0), (Y, 1, 1, 0), (M, 1, 0, 1), (M, 3, 0, 1),
        (X, 3, 1, 0), (Y, 3, 1, 0), (M, 1, 2, 0), (M, 3, 2, 0), (X, 1, 1, 1), (Y, 1, 1, 1), (M, 1, 2, 1),
        (M, 3, 2, 1), (X, 3, 1, 1), (Y, 3, 1, 1), (STATE, 0), (D, 3, 0, 0), (X, 1, 0, 0), (Y, 1, 0, 0),
        (NATIVE, D, 1, 0, 1), (STATE, 1), (D, 3, 0, 1), (X, 3, 0, 0), (Y, 3, 0, 0), (NATIVE, D, 1, 1, 1), (STATE, 2),
        (D, 3, 2, 0), (X, 1, 0, 1), (Y, 1, 0, 1), (STATE, 3), (D, 3, 2, 1), (FINISH,), (Y, 3, 0, 1), (X, 3, 0, 1),
        (D, 3, 1, 0), (M, 0, 0, 0), (X, 1, 2, 0), (Y, 1, 2, 0), (D, 3, 1, 1), (M, 0, 0, 1), (X, 3, 2, 0),
        (Y, 3, 2, 0), (M, 0, 1, 0), (X, 1, 2, 1), (Y, 1, 2, 1), (M, 0, 1, 1), (X, 3, 2, 1), (Y, 3, 2, 1),
        (M, 0, 2, 0), (D, 1, 0, 1), (D, 1, 0, 0), (M, 0, 2, 1), (OWN,), (Y, 0, 0, 0), (X, 0, 0, 0), (D, 1, 1, 0),
        (X, 0, 0, 1), (D, 1, 2, 0), (SERVE, 0), (D, 1, 1, 1), (X, 0, 1, 0), (Y, 0, 0, 1), (SERVE, 1), (D, 1, 2, 1),
        (Y, 0, 1, 0), (D, 0, 2, 0), (ACT, 3), (X, 0, 1, 1), (Y, 0, 1, 1), (DOWN, 3), (D, 0, 2, 1), (X, 0, 2, 0),
        (Y, 0, 2, 0), (SERVE, 2), (D, 0, 1, 0), (ACT, 1), (X, 0, 2, 1), (Y, 0, 2, 1), (DOWN, 1), (D, 0, 1, 1),
        (D, 0, 0, 1), (D, 0, 0, 0), (ACT, 0), (DOWN, 0),
    ),
    (
        (NATIVE, M, 1, 0, 2), (NATIVE, M, 1, 1, 2), (LOCAL,), (INTRA, 0), (NATIVE, M, 0, 0, 2), (NATIVE, M, 0, 1, 2),
        (NATIVE, M, 2, 0, 2), (NATIVE, M, 2, 1, 2), (INTRA, 1), (NATIVE, D, 0, 0, 2), (NATIVE, D, 0, 1, 2),
        (M, 1, 1, 0), (NATIVE, D, 2, 0, 2), (M, 1, 1, 1), (NATIVE, D, 2, 1, 2), (M, 1, 0, 0), (NATIVE, D, 1, 0, 2),
        (X, 1, 1, 0), (Y, 1, 1, 0), (M, 1, 0, 1), (NATIVE, D, 1, 1, 2), (X, 1, 1, 1), (Y, 1, 1, 1), (M, 1, 2, 0),
        (X, 1, 0, 0), (Y, 1, 0, 0), (M, 1, 2, 1), (X, 1, 0, 1), (D, 1, 1, 0), (STATE, 0), (D, 1, 1, 1), (Y, 1, 0, 1),
        (STATE, 1), (X, 1, 2, 0), (Y, 1, 2, 0), (STATE, 2), (X, 1, 2, 1), (D, 1, 0, 0), (STATE, 3), (FINISH,),
        (Y, 1, 2, 1), (D, 1, 0, 1), (COMPACT,), (M, 0, 0, 0), (D, 1, 2, 0), (OWN,), (M, 0, 0, 1), (ACT, 1),
        (M, 0, 1, 0), (D, 1, 2, 1), (Y, 0, 0, 0), (DOWN, 1), (X, 0, 0, 0), (M, 0, 1, 1), (Y, 0, 0, 1), (M, 0, 2, 0),
        (X, 0, 0, 1), (Y, 0, 1, 0), (M, 0, 2, 1), (X, 0, 1, 0), (D, 0, 0, 0), (X, 0, 1, 1), (Y, 0, 1, 1),
        (D, 0, 0, 1), (Y, 0, 2, 0), (X, 0, 2, 0), (Y, 0, 2, 1), (X, 0, 2, 1), (D, 0, 1, 0), (D, 0, 1, 1),
        (D, 0, 2, 0), (ACT, 0), (D, 0, 2, 1), (SERVED,), (DOWN, 0),
    ),
)


def fused_kernel(
    n,
    q_hbm,
    k_hbm,
    v_hbm,
    s_hbm,
    attn_gain_hbm,
    moe_gain_hbm,
    ids_hbm,
    gw_hbm,
    wg_hbm,
    wu_hbm,
    wd_hbm,
    out_ref,
    qb,
    kb,
    vb,
    sb,
    attn_gain_ref,
    moe_gain_ref,
    ids,
    gw,
    wg,
    wu,
    wd,
    local,
    prefix,
    passed,
    attended,
    hidden,
    moe_in,
    total,
    active,
    pick,
    rows_out,
    rows_in,
    load_sem,
    send_sem,
    piece_sem,
    sib_sem,
    state_send,
    state_recv,
    row_send,
    row_recv,
):
    g, z, r = lax.axis_index("group"), lax.axis_index("seq"), lax.axis_index("rep")
    x, c = r // 2, r % 2
    r_x, r_s = 2 * (1 - x) + c, 2 * x + (1 - c)
    piece_of = {
        M: g * 4 + r,
        X: g * 4 + r_x,
        Y: (1 - g) * 4 + r,
        D: (1 - g) * 4 + r_x,
    }
    to_x, to_y, to_s = {"rep": r_x}, {"group": 1 - g}, {"rep": r_s}
    rows = qb.shape[0]
    cap = rows_in.shape[0]
    group = cap // ROW_PARTS
    hbm = (wg_hbm, wu_hbm, wd_hbm)
    held = (wg, wu, wd)

    def span(t, piece, half):
        size = held[t].shape[1] // 16
        return pl.ds(pl.multiple_of(piece * 2 * size + half * size, size), size)

    barrier = pltpu.get_barrier_semaphore()
    for to in (to_x, to_y, to_s):
        pl.semaphore_signal(barrier, inc=1, device_id=to, device_id_type=MESH)

    @pl.when(z < n - 1)
    def _():
        pl.semaphore_signal(barrier, inc=1, device_id={"seq": z + 1}, device_id_type=MESH)

    @pl.when(z > 0)
    def _():
        pl.semaphore_signal(barrier, inc=1, device_id={"seq": z - 1}, device_id_type=MESH)

    loads = [
        pltpu.make_async_copy(src, dst, load_sem.at[i])
        for i, (src, dst) in enumerate(
            [
                (k_hbm.at[0], kb),
                (v_hbm.at[0], vb),
                (q_hbm.at[0], qb),
                (s_hbm.at[0], sb),
                (attn_gain_hbm, attn_gain_ref),
                (moe_gain_hbm, moe_gain_ref),
                (ids_hbm.at[0], ids),
                (gw_hbm.at[0], gw),
                (wg_hbm.at[0], wg.at[z]),
                (wu_hbm.at[0], wu.at[z]),
                (wd_hbm.at[0], wd.at[z]),
            ]
        )
    ]
    for load in loads[:4]:
        load.start()
    pl.semaphore_wait(barrier, 3 + (z < n - 1).astype(jnp.int32) + (z > 0).astype(jnp.int32))

    def head(h):
        return pl.ds(h * DH, DH)

    def local_state():
        loads[0].wait()
        loads[1].wait()
        for h in range(H):
            local[h] = lax.dot_general(
                kb[:, head(h)],
                vb[:, head(h)],
                (((0,), (0,)), ((), ())),
                preferred_element_type=jnp.float32,
            )

    def intra(part):
        if part == 0:
            loads[2].wait()
        causal = lax.broadcasted_iota(jnp.int32, (rows, rows), 0) >= lax.broadcasted_iota(
            jnp.int32, (rows, rows), 1
        )
        for h in range(part * H // 2, (part + 1) * H // 2):
            scores = lax.dot_general(
                qb[:, head(h)],
                kb[:, head(h)],
                (((1,), (1,)), ((), ())),
                preferred_element_type=jnp.float32,
            )
            weights = jnp.where(causal, scores, 0.0).astype(jnp.bfloat16)
            attended[:, head(h)] = jnp.dot(
                weights, vb[:, head(h)], preferred_element_type=jnp.float32
            )

    def finish():
        for load in loads[3:8]:
            load.wait()
        square = jnp.zeros((rows, DH), jnp.float32)
        for h in range(H):
            both = attended[:, head(h)] + jnp.dot(
                qb[:, head(h)], prefix[h], preferred_element_type=jnp.float32
            )
            scale = lax.rsqrt(jnp.mean(both * both, axis=-1, keepdims=True) + 1e-06)
            wide = sb[:, head(h)].astype(jnp.float32) + both * scale * attn_gain_ref[:, head(h)]
            rounded = wide.astype(jnp.bfloat16)
            hidden[:, head(h)] = rounded
            wide = rounded.astype(jnp.float32)
            square = square + wide * wide
        scale = lax.rsqrt(jnp.sum(square, axis=-1, keepdims=True) / (H * DH) + 1e-06)
        for h in range(H):
            wide = hidden[:, head(h)].astype(jnp.float32)
            moe_in[:, head(h)] = (wide * scale * moe_gain_ref[:, head(h)]).astype(jnp.bfloat16)

    def activate(inputs, e):
        gate = jnp.dot(inputs, wg[e], preferred_element_type=jnp.float32)
        upper = jnp.dot(inputs, wu[e], preferred_element_type=jnp.float32)
        return (gate / (1.0 + jnp.exp(-gate)) * upper).astype(jnp.bfloat16)

    def down(acts, e):
        return jnp.dot(acts, wd[e], preferred_element_type=jnp.float32).astype(jnp.bfloat16)

    def weigh(made, e):
        chosen = jnp.sum(jnp.where(ids[...] == e, gw[...], 0.0), axis=0, keepdims=True)
        return made.astype(jnp.float32) * jnp.broadcast_to(chosen, (8, rows)).T[:, :1]

    def program(at):
        end = at in (0, n - 1)
        near = 1 if at == 0 else at - 1 if at == n - 1 else n - 1 - at
        outer = None if end else (0 if at < n - 1 - at else n - 1)
        sent = {}

        def push(sem, copy):
            sent[sem] = sent.get(sem, 0) + 1
            copy.start()

        def piece(kind, landed, e, t, half, sem, to, source=None):
            where = span(t, piece_of[kind], half)
            dst = held[t].at[e, where, :]
            return pltpu.make_async_remote_copy(
                src_ref=dst if source is None else source.at[0, where, :],
                dst_ref=dst,
                send_sem=send_sem.at[sem],
                recv_sem=landed,
                device_id=to,
                device_id_type=MESH,
            )

        def landing(kind, e, t, half):
            return piece_sem.at[kind, e, t, half]

        def doubled(e, t):
            if end:
                return at == 0 and e == near and t in DOUBLED[3]
            return t in DOUBLED[0 if e == outer else 1 if e == near else 2]

        def native(kind, t, half, to):
            landed = landing(kind, at, t, half)
            sem = 0 if to > at else 1
            push(sem, piece(kind, landed, at, t, half, sem, {"seq": to}, hbm[t]))

        def pass_on(kind, e, t, half):
            piece(kind, landing(kind, e, t, half), e, t, half, 0, to_x).wait_recv()
            if kind == M:
                if not end and not (outer == 0 and e == ASKED):
                    to = near if e == outer else outer
                    sem = 0 if to > at else 1
                    push(sem, piece(M, landing(M, e, t, half), e, t, half, sem, {"seq": to}))
                push(2, piece(M, landing(X, e, t, half), e, t, half, 2, to_x))
                push(3, piece(M, landing(Y, e, t, half), e, t, half, 3, to_y))
            if kind == D and not end and e == outer and t in DOUBLED[2]:
                sem = 0 if near > at else 1
                push(sem, piece(D, landing(D, e, t, half), e, t, half, sem, {"seq": near}))
            if kind == X and half == 0 and not doubled(e, t):
                push(3, piece(X, landing(D, e, t, half), e, t, half, 3, to_y))
            if kind == Y and half == 1 and not doubled(e, t):
                push(2, piece(Y, landing(D, e, t, half), e, t, half, 2, to_x))
            sem = 4 + kind
            push(sem, piece(kind, sib_sem.at[e, t], e, t, half, sem, to_s))

        def from_sibling(e, t):
            half = held[t].at[e, pl.ds(0, held[t].shape[1] // 2), :]
            pltpu.make_async_copy(half, half, sib_sem.at[e, t]).wait()

        def state_copy(part):
            heads = pl.ds(part * (H // STATE_PARTS), H // STATE_PARTS)
            return pltpu.make_async_remote_copy(
                src_ref=passed.at[heads],
                dst_ref=prefix.at[heads],
                send_sem=state_send.at[part],
                recv_sem=state_recv.at[part],
                device_id={"seq": at + 1 if at < n - 1 else at - 1},
                device_id_type=MESH,
            )

        def first_state():
            prefix[...] = jnp.zeros_like(prefix)
            passed[...] = local[...].astype(passed.dtype)
            for part in range(STATE_PARTS):
                state_copy(part).start()

        def next_state(part):
            state_copy(part).wait_recv()
            if at < n - 1:
                heads = pl.ds(part * (H // STATE_PARTS), H // STATE_PARTS)
                passed[heads] = (prefix[heads].astype(jnp.float32) + local[heads]).astype(
                    passed.dtype
                )
                state_copy(part).start()

        def row_copy(part):
            some = pl.ds(part * group, group)
            return pltpu.make_async_remote_copy(
                src_ref=rows_out.at[some],
                dst_ref=rows_in.at[some],
                send_sem=row_send.at[part],
                recv_sem=row_recv.at[part],
                device_id={"seq": near if end else outer},
                device_id_type=MESH,
            )

        def compact():
            named = jnp.max((ids[...] == ASKED).astype(jnp.float32), axis=0, keepdims=True)
            earlier = lax.broadcasted_iota(jnp.int32, (rows, rows), 0) < lax.broadcasted_iota(
                jnp.int32, (rows, rows), 1
            )
            place = jnp.dot(
                jnp.broadcast_to(named, (8, rows)).astype(jnp.bfloat16),
                earlier.astype(jnp.bfloat16),
                preferred_element_type=jnp.float32,
            )[:1]
            slots = lax.broadcasted_iota(jnp.int32, (cap, rows), 0).astype(jnp.float32)
            pick[...] = jnp.where(slots == place, named, 0.0).astype(jnp.bfloat16)
            rows_out[...] = jnp.dot(
                pick[...], moe_in[...], preferred_element_type=jnp.float32
            ).astype(jnp.bfloat16)
            for part in range(ROW_PARTS):
                row_copy(part).start()

        def serve(part):
            row_copy(part).wait_recv()
            some = pl.ds(part * group, group)
            rows_out[some] = down(activate(rows_in[some], ASKED), ASKED)
            row_copy(part).start()

        def served():
            for part in range(ROW_PARTS):
                row_copy(part).wait_recv()
            made = lax.dot_general(
                pick[...],
                rows_in[...],
                (((0,), (0,)), ((), ())),
                preferred_element_type=jnp.float32,
            )
            return weigh(made, ASKED)

        def own():
            return weigh(down(activate(moe_in[...], at), at), at)

        def act(e):
            from_sibling(e, 0)
            from_sibling(e, 1)
            active[e] = activate(moe_in[...], e)

        def expert_out(e):
            from_sibling(e, 2)
            return weigh(down(active[e], e), e)

        def settle():
            for sem, count in sent.items():
                some = wg.at[:, pl.ds(0, wg.shape[1] // 64 * count), :]
                pltpu.make_async_copy(some, some, send_sem.at[sem]).wait()
            if at < n - 1:
                for part in range(STATE_PARTS):
                    state_copy(part).wait_send()
            for part in range(ROW_PARTS):
                row_copy(part).wait_send()

        items = PROGRAMS[at]
        started = ready = begun = False
        for index, item in enumerate(items):
            name, *rest = item
            if (name == OWN or name == SERVE and at == ASKED) and not ready:
                ready = True
                for load in loads[8:]:
                    load.wait()
            if name <= D:
                pass_on(name, *rest)
            elif name == NATIVE:
                native(*rest)
            elif name == STATE:
                next_state(*rest)
            elif name == FIRST:
                first_state()
            elif name == LOCAL:
                local_state()
            elif name == INTRA:
                intra(*rest)
            elif name == FINISH:
                finish()
            elif name == COMPACT:
                compact()
            elif name == SERVE:
                serve(*rest)
            elif name == ACT:
                act(*rest)
            else:
                last = index == len(items) - 1
                if last:
                    settle()
                if name == OWN:
                    added = own()
                else:
                    added = served() if name == SERVED else expert_out(*rest)
                if begun:
                    added = total[...] + added
                begun = True
                if last:
                    out_ref[0] = (hidden[...].astype(jnp.float32) + added).astype(out_ref.dtype)
                else:
                    total[...] = added
            if name == LOCAL and not started:
                started = True
                for load in loads[4:]:
                    load.start()

    for at in range(n):

        @pl.when(z == at)
        def _():
            program(at)


def gathered_weights(
    n,
    queries,
    keys,
    values,
    stream,
    attn_gain,
    moe_gain,
    expert_ids,
    gate_weights,
    w_gate,
    w_up,
    w_down,
):
    rows, width = queries.shape[1:]
    units = w_gate.shape[2]
    cap = 3 * rows // n
    half = jnp.bfloat16
    anywhere = pl.BlockSpec(memory_space=pl.ANY)
    vmem = pl.BlockSpec(memory_space=pltpu.VMEM)
    dma = pltpu.SemaphoreType.DMA
    return pl.pallas_call(
        functools.partial(fused_kernel, n),
        out_shape=pltpu.VMEM((1, rows, width), half),
        in_specs=[anywhere] * 11,
        out_specs=vmem,
        scratch_shapes=[
            pltpu.VMEM((rows, width), half),
            pltpu.VMEM((rows, width), half),
            pltpu.VMEM((rows, width), half),
            pltpu.VMEM((rows, width), half),
            pltpu.VMEM((1, width), jnp.float32),
            pltpu.VMEM((1, width), jnp.float32),
            pltpu.VMEM((2, rows), jnp.int32),
            pltpu.VMEM((2, rows), jnp.float32),
            pltpu.VMEM((n, width, units), half),
            pltpu.VMEM((n, width, units), half),
            pltpu.VMEM((n, units, width), half),
            pltpu.VMEM((H, DH, DH), jnp.float32),
            pltpu.VMEM((H, DH, DH), half),
            pltpu.VMEM((H, DH, DH), half),
            pltpu.VMEM((rows, width), jnp.float32),
            pltpu.VMEM((rows, width), half),
            pltpu.VMEM((rows, width), half),
            pltpu.VMEM((rows, width), jnp.float32),
            pltpu.VMEM((n, rows, units), half),
            pltpu.VMEM((cap, rows), half),
            pltpu.VMEM((cap, width), half),
            pltpu.VMEM((cap, width), half),
            dma((11,)),
            dma((8,)),
            dma((4, n, 3, 2)),
            dma((n, 3)),
            dma((STATE_PARTS,)),
            dma((STATE_PARTS,)),
            dma((ROW_PARTS,)),
            dma((ROW_PARTS,)),
        ],
        compiler_params=pltpu.CompilerParams(
            collective_id=0, has_side_effects=True, vmem_limit_bytes=(64 << 20) - (600 << 10)
        ),
    )(
        queries,
        keys,
        values,
        stream,
        attn_gain[None],
        moe_gain[None],
        jnp.swapaxes(expert_ids, 1, 2),
        jnp.swapaxes(gate_weights, 1, 2),
        w_gate,
        w_up,
        w_down,
    )


def prefix_2(value, axis, join, neutral):
    count, mine = (lax.axis_size(axis), lax.axis_index(axis))
    pieces = lax.all_gather(value, axis)
    total = jnp.full_like(value, 0) + jnp.asarray(neutral, value.dtype)

    def lap(position, total):
        longer = join(total, pieces[position])
        return jnp.where(position < mine, longer, total)

    return lax.fori_loop(0, count - 1, lap, total)


def add_states(earlier, later):
    return earlier + later


def per_device(
    queries,
    keys,
    values,
    stream,
    attn_gain,
    moe_gain,
    expert_ids,
    gate_weights,
    w_gate,
    w_up,
    w_down,
):
    row_count = queries.shape[1]
    width = queries.shape[2]
    query_heads = queries[0].reshape(row_count, H, DH)
    key_heads = keys[0].reshape(row_count, H, DH)
    value_heads = values[0].reshape(row_count, H, DH)
    own_state = jnp.einsum(
        "shd,she->hde", key_heads, value_heads, preferred_element_type=jnp.float32
    )
    scores = jnp.einsum("thd,shd->hts", query_heads, key_heads, preferred_element_type=jnp.float32)
    causal = jnp.arange(row_count)[:, None] >= jnp.arange(row_count)[None, :]
    weights = jnp.where(causal[None], scores, jnp.zeros((), jnp.float32)).astype(jnp.bfloat16)
    intra = jnp.einsum("hts,shd->thd", weights, value_heads, preferred_element_type=jnp.float32)
    prefix = prefix_2(own_state, "seq", add_states, jnp.zeros_like(own_state))
    inter = jnp.einsum(
        "thd,hde->the", query_heads, prefix.astype(jnp.bfloat16), preferred_element_type=jnp.float32
    )
    attended = intra + inter
    normed = attended * lax.rsqrt(jnp.mean(attended * attended, axis=-1, keepdims=True) + 1e-06)
    hidden = (stream[0].astype(jnp.float32) + normed.reshape(row_count, width) * attn_gain).astype(
        jnp.bfloat16
    )
    hidden_wide = hidden.astype(jnp.float32)
    moe_in = (
        hidden_wide
        * lax.rsqrt(jnp.mean(hidden_wide * hidden_wide, axis=-1, keepdims=True) + 1e-06)
        * moe_gain
    ).astype(jnp.bfloat16)
    dest_count = lax.axis_size("seq")
    capacity = 3 * row_count // dest_count
    choice_ids = expert_ids[0].reshape(-1)
    place = jnp.arange(2 * row_count, dtype=jnp.int32)
    earlier = (choice_ids[:, None] == choice_ids[None, :]) & (place[:, None] > place[None, :])
    slot_rank = jnp.sum(earlier.astype(jnp.int32), axis=1)
    slot_index = choice_ids * capacity + slot_rank
    token_index = jnp.arange(2 * row_count, dtype=jnp.int32) // 2
    outgoing = (
        jnp.zeros((dest_count * capacity, width), jnp.bfloat16)
        .at[slot_index]
        .set(moe_in[token_index])
    )
    outgoing = outgoing.reshape(dest_count, capacity, width)
    received = lax.all_to_all(outgoing, "seq", split_axis=0, concat_axis=0, tiled=True)
    flat_rows = received.reshape(-1, width)
    gate = jnp.dot(flat_rows, w_gate[0], preferred_element_type=jnp.float32)
    upper = jnp.dot(flat_rows, w_up[0], preferred_element_type=jnp.float32)
    active = (jax.nn.silu(gate) * upper).astype(jnp.bfloat16)
    produced = jnp.dot(active, w_down[0], preferred_element_type=jnp.float32).astype(jnp.bfloat16)
    returned = lax.all_to_all(
        produced.reshape(received.shape), "seq", split_axis=0, concat_axis=0, tiled=True
    )
    picked = returned.reshape(-1, width)[slot_index].astype(jnp.float32)
    weighted = (gate_weights[0].reshape(-1)[:, None] * picked).reshape(row_count, 2, width)
    mixed = hidden_wide + (weighted[:, 0] + weighted[:, 1])
    return mixed.astype(jnp.bfloat16)[None]


def solution(mesh):
    placed = (
        P(("group", "rep"), "seq", None),
        P(("group", "rep"), "seq", None),
        P(("group", "rep"), "seq", None),
        P(("group", "rep"), "seq", None),
        P(),
        P(),
        P(("group", "rep"), "seq", None),
        P(("group", "rep"), "seq", None),
        P("seq", None, None),
        P("seq", None, None),
        P("seq", None, None),
    )
    ways = dict(mesh.shape)

    def plan(*args):
        n = ways["seq"]
        held = n * sum(w.size // w.shape[0] * w.dtype.itemsize for w in args[-3:])
        whole = args[-1].shape[1] % 256 == 0 and 3 * args[0].shape[1] // n % (16 * ROW_PARTS) == 0
        if ways["group"] == 2 and ways["rep"] == 4 and n == len(PROGRAMS) and whole and held <= GATHER_LIMIT:
            return gathered_weights(n, *args)
        return per_device(*args)

    return jax.shard_map(
        plan,
        mesh=mesh,
        in_specs=placed,
        out_specs=P(("group", "rep"), "seq", None),
        check_vma=False,
    )
```

```python
import functools

import jax
import jax.numpy as jnp
from jax import lax
from jax.experimental import pallas as pl
from jax.experimental.pallas import tpu as pltpu
from jax.sharding import PartitionSpec as P

H = 8
DH = 128
MESH = pl.DeviceIdType.MESH
GATHER_LIMIT = 24 << 20


ASKED = 2
ROW_PARTS = 6
STATE_PARTS = 8
DOUBLED = ((0, 1, 2), (1,), (1, 2), (2,))
M, X, Y, D, NATIVE, STATE, FIRST, LOCAL, INTRA, FINISH, COMPACT, OWN, ACT, DOWN, SERVE, SERVED = range(16)
PROGRAMS = (
    (
        (LOCAL,), (FIRST,), (NATIVE, M, 0, 0, 1), (NATIVE, M, 0, 1, 1), (NATIVE, M, 1, 0, 1), (NATIVE, M, 1, 1, 1),
        (NATIVE, M, 2, 0, 1), (NATIVE, M, 2, 1, 1), (INTRA, 0), (INTRA, 1), (FINISH,), (COMPACT,), (M, 1, 0, 0),
        (OWN,), (M, 1, 0, 1), (M, 1, 1, 0), (X, 1, 0, 0), (Y, 1, 0, 0), (M, 1, 1, 1), (X, 1, 0, 1), (Y, 1, 0, 1),
        (D, 1, 2, 0), (X, 1, 1, 0), (Y, 1, 1, 0), (D, 1, 2, 1), (X, 1, 1, 1), (D, 1, 0, 0), (M, 1, 2, 0),
        (D, 1, 0, 1), (Y, 1, 1, 1), (M, 1, 2, 1), (D, 1, 1, 0), (M, 3, 0, 0), (X, 1, 2, 0), (Y, 1, 2, 0),
        (D, 1, 1, 1), (Y, 1, 2, 1), (M, 3, 0, 1), (ACT, 1), (X, 1, 2, 1), (Y, 3, 0, 0), (NATIVE, D, 1, 0, 1),
        (M, 3, 1, 0), (X, 3, 0, 0), (DOWN, 1), (NATIVE, D, 1, 1, 1), (M, 3, 1, 1), (Y, 3, 0, 1), (X, 3, 0, 1),
        (NATIVE, D, 2, 0, 1), (Y, 3, 1, 0), (X, 3, 1, 0), (NATIVE, D, 2, 1, 1), (D, 3, 0, 0), (X, 3, 1, 1),
        (M, 3, 2, 0), (NATIVE, D, 0, 0, 1), (Y, 3, 1, 1), (D, 3, 0, 1), (M, 3, 2, 1), (NATIVE, D, 0, 1, 1),
        (D, 3, 1, 0), (X, 3, 2, 0), (Y, 3, 2, 0), (D, 3, 1, 1), (Y, 3, 2, 1), (ACT, 3), (X, 3, 2, 1), (D, 3, 2, 0),
        (D, 3, 2, 1), (DOWN, 3), (SERVED,),
    ),
    (
        (NATIVE, M, 0, 0, 2), (NATIVE, M, 0, 1, 2), (NATIVE, M, 1, 0, 2), (NATIVE, M, 1, 1, 2), (NATIVE, M, 0, 0, 0),
        (NATIVE, M, 0, 1, 0), (NATIVE, M, 1, 0, 0), (NATIVE, M, 1, 1, 0), (LOCAL,), (INTRA, 0), (NATIVE, M, 2, 0, 2),
        (INTRA, 1), (NATIVE, D, 2, 0, 0), (NATIVE, M, 2, 1, 2), (NATIVE, D, 2, 1, 0), (STATE, 0), (M, 2, 0, 0),
        (STATE, 1), (NATIVE, M, 2, 0, 0), (STATE, 2), (M, 2, 0, 1), (STATE, 3), (NATIVE, M, 2, 1, 0), (STATE, 4),
        (M, 2, 2, 0), (STATE, 5), (X, 2, 0, 0), (Y, 2, 0, 0), (STATE, 6), (M, 2, 2, 1), (STATE, 7), (X, 2, 0, 1),
        (Y, 2, 0, 1), (FINISH,), (M, 2, 1, 0), (M, 0, 0, 0), (X, 2, 2, 0), (Y, 2, 2, 0), (M, 2, 1, 1), (M, 0, 0, 1),
        (X, 2, 2, 1), (D, 2, 0, 0), (M, 3, 0, 0), (OWN,), (D, 2, 0, 1), (Y, 2, 2, 1), (M, 0, 1, 0), (X, 2, 1, 0),
        (Y, 2, 1, 0), (M, 3, 0, 1), (M, 0, 1, 1), (M, 3, 1, 0), (M, 0, 2, 0), (Y, 0, 0, 0), (X, 0, 0, 0),
        (M, 3, 1, 1), (M, 0, 2, 1), (X, 2, 1, 1), (D, 2, 2, 0), (D, 2, 1, 0), (X, 0, 0, 1), (Y, 2, 1, 1),
        (NATIVE, D, 1, 0, 2), (D, 2, 1, 1), (X, 3, 0, 0), (Y, 0, 0, 1), (NATIVE, D, 1, 1, 2), (ACT, 2), (M, 3, 2, 0),
        (Y, 3, 0, 0), (D, 2, 2, 1), (M, 3, 2, 1), (X, 0, 1, 0), (Y, 0, 1, 0), (DOWN, 2), (SERVE, 0), (X, 3, 0, 1),
        (Y, 3, 0, 1), (D, 3, 1, 0), (SERVE, 1), (D, 3, 1, 1), (SERVE, 2), (X, 0, 1, 1), (Y, 0, 1, 1), (SERVE, 3),
        (D, 0, 1, 0), (X, 3, 1, 0), (Y, 3, 1, 0), (D, 3, 2, 0), (SERVE, 4), (D, 3, 2, 1), (SERVE, 5), (Y, 0, 2, 0),
        (D, 0, 1, 1), (X, 0, 2, 0), (D, 0, 2, 0), (X, 3, 1, 1), (Y, 3, 1, 1), (D, 0, 2, 1), (X, 0, 2, 1),
        (Y, 0, 2, 1), (D, 0, 0, 0), (X, 3, 2, 0), (D, 3, 0, 0), (D, 0, 0, 1), (X, 3, 2, 1), (Y, 3, 2, 0), (ACT, 0),
        (D, 3, 0, 1), (Y, 3, 2, 1), (DOWN, 0), (ACT, 3), (DOWN, 3),
    ),
    (
        (NATIVE, M, 0, 0, 1), (NATIVE, M, 0, 1, 1), (NATIVE, M, 2, 0, 1), (NATIVE, M, 2, 1, 1), (LOCAL,), (INTRA, 0),
        (INTRA, 1), (NATIVE, M, 1, 0, 1), (NATIVE, M, 1, 1, 1), (M, 1, 0, 0), (D, 3, 0, 0), (M, 1, 0, 1),
        (D, 3, 0, 1), (M, 1, 1, 0), (M, 3, 0, 0), (X, 1, 0, 0), (Y, 1, 0, 0), (M, 1, 1, 1), (M, 3, 0, 1),
        (X, 1, 0, 1), (Y, 1, 0, 1), (M, 3, 1, 0), (M, 1, 2, 0), (X, 1, 1, 0), (Y, 1, 1, 0), (M, 3, 1, 1),
        (M, 1, 2, 1), (X, 3, 0, 0), (Y, 3, 0, 0), (NATIVE, D, 1, 0, 1), (STATE, 0), (NATIVE, D, 1, 1, 1),
        (M, 3, 2, 0), (STATE, 1), (X, 1, 1, 1), (D, 1, 0, 0), (STATE, 2), (M, 3, 2, 1), (STATE, 3), (X, 3, 0, 1),
        (Y, 1, 1, 1), (STATE, 4), (D, 3, 1, 0), (STATE, 5), (D, 1, 0, 1), (Y, 3, 0, 1), (STATE, 6), (D, 3, 1, 1),
        (STATE, 7), (FINISH,), (X, 3, 1, 0), (Y, 3, 1, 0), (D, 3, 2, 0), (M, 0, 0, 0), (X, 1, 2, 0), (Y, 1, 2, 0),
        (D, 3, 2, 1), (M, 0, 0, 1), (X, 3, 1, 1), (Y, 3, 1, 1), (M, 0, 1, 0), (ACT, 3), (X, 1, 2, 1), (Y, 1, 2, 1),
        (M, 0, 1, 1), (X, 3, 2, 0), (Y, 3, 2, 0), (M, 0, 2, 0), (X, 3, 2, 1), (Y, 3, 2, 1), (M, 0, 2, 1), (SERVE, 0),
        (Y, 0, 0, 0), (X, 0, 0, 0), (DOWN, 3), (D, 1, 1, 0), (OWN,), (X, 0, 0, 1), (D, 1, 2, 0), (D, 1, 1, 1),
        (SERVE, 1), (Y, 0, 0, 1), (X, 0, 1, 0), (SERVE, 2), (D, 1, 2, 1), (Y, 0, 1, 0), (SERVE, 3), (D, 0, 1, 0),
        (ACT, 1), (Y, 0, 1, 1), (X, 0, 1, 1), (SERVE, 4), (D, 0, 1, 1), (X, 0, 2, 0), (Y, 0, 2, 0), (DOWN, 1),
        (SERVE, 5), (D, 0, 2, 0), (X, 0, 2, 1), (Y, 0, 2, 1), (D, 0, 2, 1), (D, 0, 0, 1), (D, 0, 0, 0), (ACT, 0),
        (DOWN, 0),
    ),
    (
        (NATIVE, D, 0, 0, 2), (NATIVE, D, 0, 1, 2), (NATIVE, M, 0, 0, 2), (NATIVE, M, 0, 1, 2), (LOCAL,), (INTRA, 0),
        (NATIVE, M, 1, 0, 2), (NATIVE, M, 1, 1, 2), (NATIVE, M, 2, 0, 2), (NATIVE, M, 2, 1, 2), (INTRA, 1),
        (M, 1, 0, 0), (NATIVE, D, 1, 0, 2), (M, 1, 0, 1), (NATIVE, D, 1, 1, 2), (M, 1, 1, 0), (NATIVE, D, 2, 0, 2),
        (X, 1, 0, 0), (Y, 1, 0, 0), (M, 1, 1, 1), (NATIVE, D, 2, 1, 2), (X, 1, 0, 1), (Y, 1, 0, 1), (M, 1, 2, 0),
        (X, 1, 1, 0), (Y, 1, 1, 0), (M, 1, 2, 1), (X, 1, 1, 1), (D, 1, 0, 0), (STATE, 0), (STATE, 1), (D, 1, 0, 1),
        (Y, 1, 1, 1), (STATE, 2), (STATE, 3), (X, 1, 2, 0), (Y, 1, 2, 0), (STATE, 4), (STATE, 5), (X, 1, 2, 1),
        (D, 1, 1, 0), (STATE, 6), (STATE, 7), (FINISH,), (D, 1, 1, 1), (Y, 1, 2, 1), (COMPACT,), (M, 0, 0, 0),
        (D, 1, 2, 0), (ACT, 1), (M, 0, 0, 1), (OWN,), (M, 0, 1, 0), (D, 1, 2, 1), (Y, 0, 0, 0), (M, 0, 1, 1),
        (X, 0, 0, 0), (DOWN, 1), (Y, 0, 0, 1), (M, 0, 2, 0), (X, 0, 0, 1), (Y, 0, 1, 0), (M, 0, 2, 1), (X, 0, 1, 0),
        (Y, 0, 1, 1), (X, 0, 1, 1), (D, 0, 0, 0), (D, 0, 0, 1), (Y, 0, 2, 0), (X, 0, 2, 0), (Y, 0, 2, 1),
        (X, 0, 2, 1), (D, 0, 1, 0), (D, 0, 1, 1), (D, 0, 2, 0), (ACT, 0), (D, 0, 2, 1), (SERVED,), (DOWN, 0),
    ),
)


def fused_kernel(
    n,
    q_hbm,
    k_hbm,
    v_hbm,
    s_hbm,
    attn_gain_hbm,
    moe_gain_hbm,
    ids_hbm,
    gw_hbm,
    wg_hbm,
    wu_hbm,
    wd_hbm,
    out_ref,
    qb,
    kb,
    vb,
    sb,
    attn_gain_ref,
    moe_gain_ref,
    ids,
    gw,
    wg,
    wu,
    wd,
    local,
    prefix,
    passed,
    attended,
    hidden,
    moe_in,
    total,
    active,
    pick,
    rows_out,
    rows_in,
    load_sem,
    send_sem,
    piece_sem,
    sib_sem,
    state_send,
    state_recv,
    row_send,
    row_recv,
):
    g, z, r = lax.axis_index("group"), lax.axis_index("seq"), lax.axis_index("rep")
    x, c = r // 2, r % 2
    r_x, r_s = 2 * (1 - x) + c, 2 * x + (1 - c)
    piece_of = {
        M: g * 4 + r,
        X: g * 4 + r_x,
        Y: (1 - g) * 4 + r,
        D: (1 - g) * 4 + r_x,
    }
    to_x, to_y, to_s = {"rep": r_x}, {"group": 1 - g}, {"rep": r_s}
    rows = qb.shape[0]
    cap = rows_in.shape[0]
    group = cap // ROW_PARTS
    hbm = (wg_hbm, wu_hbm, wd_hbm)
    held = (wg, wu, wd)

    def span(t, piece, half):
        size = held[t].shape[1] // 16
        return pl.ds(pl.multiple_of(piece * 2 * size + half * size, size), size)

    barrier = pltpu.get_barrier_semaphore()
    for to in (to_x, to_y, to_s):
        pl.semaphore_signal(barrier, inc=1, device_id=to, device_id_type=MESH)

    @pl.when(z < n - 1)
    def _():
        pl.semaphore_signal(barrier, inc=1, device_id={"seq": z + 1}, device_id_type=MESH)

    @pl.when(z > 0)
    def _():
        pl.semaphore_signal(barrier, inc=1, device_id={"seq": z - 1}, device_id_type=MESH)

    loads = [
        pltpu.make_async_copy(src, dst, load_sem.at[i])
        for i, (src, dst) in enumerate(
            [
                (k_hbm.at[0], kb),
                (v_hbm.at[0], vb),
                (q_hbm.at[0], qb),
                (s_hbm.at[0], sb),
                (attn_gain_hbm, attn_gain_ref),
                (moe_gain_hbm, moe_gain_ref),
                (ids_hbm.at[0], ids),
                (gw_hbm.at[0], gw),
                (wg_hbm.at[0], wg.at[z]),
                (wu_hbm.at[0], wu.at[z]),
                (wd_hbm.at[0], wd.at[z]),
            ]
        )
    ]
    for load in loads[:4]:
        load.start()
    pl.semaphore_wait(barrier, 3 + (z < n - 1).astype(jnp.int32) + (z > 0).astype(jnp.int32))

    def head(h):
        return pl.ds(h * DH, DH)

    def local_state():
        loads[0].wait()
        loads[1].wait()
        for h in range(H):
            local[h] = lax.dot_general(
                kb[:, head(h)],
                vb[:, head(h)],
                (((0,), (0,)), ((), ())),
                preferred_element_type=jnp.float32,
            )

    def intra(part):
        if part == 0:
            loads[2].wait()
        causal = lax.broadcasted_iota(jnp.int32, (rows, rows), 0) >= lax.broadcasted_iota(
            jnp.int32, (rows, rows), 1
        )
        for h in range(part * H // 2, (part + 1) * H // 2):
            scores = lax.dot_general(
                qb[:, head(h)],
                kb[:, head(h)],
                (((1,), (1,)), ((), ())),
                preferred_element_type=jnp.float32,
            )
            weights = jnp.where(causal, scores, 0.0).astype(jnp.bfloat16)
            attended[:, head(h)] = jnp.dot(
                weights, vb[:, head(h)], preferred_element_type=jnp.float32
            )

    def finish():
        for load in loads[3:8]:
            load.wait()
        square = jnp.zeros((rows, DH), jnp.float32)
        for h in range(H):
            both = attended[:, head(h)] + jnp.dot(
                qb[:, head(h)], prefix[h], preferred_element_type=jnp.float32
            )
            scale = lax.rsqrt(jnp.mean(both * both, axis=-1, keepdims=True) + 1e-06)
            wide = sb[:, head(h)].astype(jnp.float32) + both * scale * attn_gain_ref[:, head(h)]
            rounded = wide.astype(jnp.bfloat16)
            hidden[:, head(h)] = rounded
            wide = rounded.astype(jnp.float32)
            square = square + wide * wide
        scale = lax.rsqrt(jnp.sum(square, axis=-1, keepdims=True) / (H * DH) + 1e-06)
        for h in range(H):
            wide = hidden[:, head(h)].astype(jnp.float32)
            moe_in[:, head(h)] = (wide * scale * moe_gain_ref[:, head(h)]).astype(jnp.bfloat16)

    def activate(inputs, e):
        gate = jnp.dot(inputs, wg[e], preferred_element_type=jnp.float32)
        upper = jnp.dot(inputs, wu[e], preferred_element_type=jnp.float32)
        return (gate / (1.0 + jnp.exp(-gate)) * upper).astype(jnp.bfloat16)

    def down(acts, e):
        return jnp.dot(acts, wd[e], preferred_element_type=jnp.float32).astype(jnp.bfloat16)

    def weigh(made, e):
        chosen = jnp.sum(jnp.where(ids[...] == e, gw[...], 0.0), axis=0, keepdims=True)
        return made.astype(jnp.float32) * jnp.broadcast_to(chosen, (8, rows)).T[:, :1]

    def program(at):
        end = at in (0, n - 1)
        near = 1 if at == 0 else at - 1 if at == n - 1 else n - 1 - at
        outer = None if end else (0 if at < n - 1 - at else n - 1)
        sent = {}

        def push(sem, copy):
            sent[sem] = sent.get(sem, 0) + 1
            copy.start()

        def piece(kind, landed, e, t, half, sem, to, source=None):
            where = span(t, piece_of[kind], half)
            dst = held[t].at[e, where, :]
            return pltpu.make_async_remote_copy(
                src_ref=dst if source is None else source.at[0, where, :],
                dst_ref=dst,
                send_sem=send_sem.at[sem],
                recv_sem=landed,
                device_id=to,
                device_id_type=MESH,
            )

        def landing(kind, e, t, half):
            return piece_sem.at[kind, e, t, half]

        def doubled(e, t):
            if end:
                return at == 0 and e == near and t in DOUBLED[3]
            return t in DOUBLED[0 if e == outer else 1 if e == near else 2]

        def native(kind, t, half, to):
            landed = landing(kind, at, t, half)
            sem = 0 if to > at else 1
            push(sem, piece(kind, landed, at, t, half, sem, {"seq": to}, hbm[t]))

        def pass_on(kind, e, t, half):
            piece(kind, landing(kind, e, t, half), e, t, half, 0, to_x).wait_recv()
            if kind == M:
                if not end and not (outer == 0 and e == ASKED):
                    to = near if e == outer else outer
                    sem = 0 if to > at else 1
                    push(sem, piece(M, landing(M, e, t, half), e, t, half, sem, {"seq": to}))
                push(2, piece(M, landing(X, e, t, half), e, t, half, 2, to_x))
                push(3, piece(M, landing(Y, e, t, half), e, t, half, 3, to_y))
            if kind == D and not end and e == outer and t in DOUBLED[2]:
                sem = 0 if near > at else 1
                push(sem, piece(D, landing(D, e, t, half), e, t, half, sem, {"seq": near}))
            if kind == X and half == 0 and not doubled(e, t):
                push(3, piece(X, landing(D, e, t, half), e, t, half, 3, to_y))
            if kind == Y and half == 1 and not doubled(e, t):
                push(2, piece(Y, landing(D, e, t, half), e, t, half, 2, to_x))
            sem = 4 + kind
            push(sem, piece(kind, sib_sem.at[e, t], e, t, half, sem, to_s))

        def from_sibling(e, t):
            half = held[t].at[e, pl.ds(0, held[t].shape[1] // 2), :]
            pltpu.make_async_copy(half, half, sib_sem.at[e, t]).wait()

        def state_copy(part):
            heads = pl.ds(part * (H // STATE_PARTS), H // STATE_PARTS)
            return pltpu.make_async_remote_copy(
                src_ref=passed.at[heads],
                dst_ref=prefix.at[heads],
                send_sem=state_send.at[part],
                recv_sem=state_recv.at[part],
                device_id={"seq": at + 1 if at < n - 1 else at - 1},
                device_id_type=MESH,
            )

        def first_state():
            prefix[...] = jnp.zeros_like(prefix)
            passed[...] = local[...].astype(passed.dtype)
            for part in range(STATE_PARTS):
                state_copy(part).start()

        def next_state(part):
            state_copy(part).wait_recv()
            if at < n - 1:
                heads = pl.ds(part * (H // STATE_PARTS), H // STATE_PARTS)
                passed[heads] = (prefix[heads].astype(jnp.float32) + local[heads]).astype(
                    passed.dtype
                )
                state_copy(part).start()

        def row_copy(part):
            some = pl.ds(part * group, group)
            return pltpu.make_async_remote_copy(
                src_ref=rows_out.at[some],
                dst_ref=rows_in.at[some],
                send_sem=row_send.at[part],
                recv_sem=row_recv.at[part],
                device_id={"seq": near if end else outer},
                device_id_type=MESH,
            )

        def compact():
            named = jnp.max((ids[...] == ASKED).astype(jnp.float32), axis=0, keepdims=True)
            earlier = lax.broadcasted_iota(jnp.int32, (rows, rows), 0) < lax.broadcasted_iota(
                jnp.int32, (rows, rows), 1
            )
            place = jnp.dot(
                jnp.broadcast_to(named, (8, rows)).astype(jnp.bfloat16),
                earlier.astype(jnp.bfloat16),
                preferred_element_type=jnp.float32,
            )[:1]
            slots = lax.broadcasted_iota(jnp.int32, (cap, rows), 0).astype(jnp.float32)
            pick[...] = jnp.where(slots == place, named, 0.0).astype(jnp.bfloat16)
            rows_out[...] = jnp.dot(
                pick[...], moe_in[...], preferred_element_type=jnp.float32
            ).astype(jnp.bfloat16)
            for part in range(ROW_PARTS):
                row_copy(part).start()

        def serve(part):
            row_copy(part).wait_recv()
            some = pl.ds(part * group, group)
            rows_out[some] = down(activate(rows_in[some], ASKED), ASKED)
            row_copy(part).start()

        def served():
            for part in range(ROW_PARTS):
                row_copy(part).wait_recv()
            made = lax.dot_general(
                pick[...],
                rows_in[...],
                (((0,), (0,)), ((), ())),
                preferred_element_type=jnp.float32,
            )
            return weigh(made, ASKED)

        def own():
            return weigh(down(activate(moe_in[...], at), at), at)

        def act(e):
            from_sibling(e, 0)
            from_sibling(e, 1)
            active[e] = activate(moe_in[...], e)

        def expert_out(e):
            from_sibling(e, 2)
            return weigh(down(active[e], e), e)

        def settle():
            for sem, count in sent.items():
                some = wg.at[:, pl.ds(0, wg.shape[1] // 64 * count), :]
                pltpu.make_async_copy(some, some, send_sem.at[sem]).wait()
            if at < n - 1:
                for part in range(STATE_PARTS):
                    state_copy(part).wait_send()
            for part in range(ROW_PARTS):
                row_copy(part).wait_send()

        items = PROGRAMS[at]
        started = ready = begun = False
        for index, item in enumerate(items):
            name, *rest = item
            if (name == OWN or name == SERVE and at == ASKED) and not ready:
                ready = True
                for load in loads[8:]:
                    load.wait()
            if name <= D:
                pass_on(name, *rest)
            elif name == NATIVE:
                native(*rest)
            elif name == STATE:
                next_state(*rest)
            elif name == FIRST:
                first_state()
            elif name == LOCAL:
                local_state()
            elif name == INTRA:
                intra(*rest)
            elif name == FINISH:
                finish()
            elif name == COMPACT:
                compact()
            elif name == SERVE:
                serve(*rest)
            elif name == ACT:
                act(*rest)
            else:
                last = index == len(items) - 1
                if last:
                    settle()
                if name == OWN:
                    added = own()
                else:
                    added = served() if name == SERVED else expert_out(*rest)
                if begun:
                    added = total[...] + added
                begun = True
                if last:
                    out_ref[0] = (hidden[...].astype(jnp.float32) + added).astype(out_ref.dtype)
                else:
                    total[...] = added
            if name == LOCAL and not started:
                started = True
                for load in loads[4:]:
                    load.start()

    for at in range(n):

        @pl.when(z == at)
        def _():
            program(at)


def gathered_weights(
    n,
    queries,
    keys,
    values,
    stream,
    attn_gain,
    moe_gain,
    expert_ids,
    gate_weights,
    w_gate,
    w_up,
    w_down,
):
    rows, width = queries.shape[1:]
    units = w_gate.shape[2]
    cap = 3 * rows // n
    half = jnp.bfloat16
    anywhere = pl.BlockSpec(memory_space=pl.ANY)
    vmem = pl.BlockSpec(memory_space=pltpu.VMEM)
    dma = pltpu.SemaphoreType.DMA
    return pl.pallas_call(
        functools.partial(fused_kernel, n),
        out_shape=pltpu.VMEM((1, rows, width), half),
        in_specs=[anywhere] * 11,
        out_specs=vmem,
        scratch_shapes=[
            pltpu.VMEM((rows, width), half),
            pltpu.VMEM((rows, width), half),
            pltpu.VMEM((rows, width), half),
            pltpu.VMEM((rows, width), half),
            pltpu.VMEM((1, width), jnp.float32),
            pltpu.VMEM((1, width), jnp.float32),
            pltpu.VMEM((2, rows), jnp.int32),
            pltpu.VMEM((2, rows), jnp.float32),
            pltpu.VMEM((n, width, units), half),
            pltpu.VMEM((n, width, units), half),
            pltpu.VMEM((n, units, width), half),
            pltpu.VMEM((H, DH, DH), jnp.float32),
            pltpu.VMEM((H, DH, DH), half),
            pltpu.VMEM((H, DH, DH), half),
            pltpu.VMEM((rows, width), jnp.float32),
            pltpu.VMEM((rows, width), half),
            pltpu.VMEM((rows, width), half),
            pltpu.VMEM((rows, width), jnp.float32),
            pltpu.VMEM((n, rows, units), half),
            pltpu.VMEM((cap, rows), half),
            pltpu.VMEM((cap, width), half),
            pltpu.VMEM((cap, width), half),
            dma((11,)),
            dma((8,)),
            dma((4, n, 3, 2)),
            dma((n, 3)),
            dma((STATE_PARTS,)),
            dma((STATE_PARTS,)),
            dma((ROW_PARTS,)),
            dma((ROW_PARTS,)),
        ],
        compiler_params=pltpu.CompilerParams(
            collective_id=0, has_side_effects=True, vmem_limit_bytes=(64 << 20) - (600 << 10)
        ),
    )(
        queries,
        keys,
        values,
        stream,
        attn_gain[None],
        moe_gain[None],
        jnp.swapaxes(expert_ids, 1, 2),
        jnp.swapaxes(gate_weights, 1, 2),
        w_gate,
        w_up,
        w_down,
    )


def prefix_2(value, axis, join, neutral):
    count, mine = (lax.axis_size(axis), lax.axis_index(axis))
    pieces = lax.all_gather(value, axis)
    total = jnp.full_like(value, 0) + jnp.asarray(neutral, value.dtype)

    def lap(position, total):
        longer = join(total, pieces[position])
        return jnp.where(position < mine, longer, total)

    return lax.fori_loop(0, count - 1, lap, total)


def add_states(earlier, later):
    return earlier + later


def per_device(
    queries,
    keys,
    values,
    stream,
    attn_gain,
    moe_gain,
    expert_ids,
    gate_weights,
    w_gate,
    w_up,
    w_down,
):
    row_count = queries.shape[1]
    width = queries.shape[2]
    query_heads = queries[0].reshape(row_count, H, DH)
    key_heads = keys[0].reshape(row_count, H, DH)
    value_heads = values[0].reshape(row_count, H, DH)
    own_state = jnp.einsum(
        "shd,she->hde", key_heads, value_heads, preferred_element_type=jnp.float32
    )
    scores = jnp.einsum("thd,shd->hts", query_heads, key_heads, preferred_element_type=jnp.float32)
    causal = jnp.arange(row_count)[:, None] >= jnp.arange(row_count)[None, :]
    weights = jnp.where(causal[None], scores, jnp.zeros((), jnp.float32)).astype(jnp.bfloat16)
    intra = jnp.einsum("hts,shd->thd", weights, value_heads, preferred_element_type=jnp.float32)
    prefix = prefix_2(own_state, "seq", add_states, jnp.zeros_like(own_state))
    inter = jnp.einsum(
        "thd,hde->the", query_heads, prefix.astype(jnp.bfloat16), preferred_element_type=jnp.float32
    )
    attended = intra + inter
    normed = attended * lax.rsqrt(jnp.mean(attended * attended, axis=-1, keepdims=True) + 1e-06)
    hidden = (stream[0].astype(jnp.float32) + normed.reshape(row_count, width) * attn_gain).astype(
        jnp.bfloat16
    )
    hidden_wide = hidden.astype(jnp.float32)
    moe_in = (
        hidden_wide
        * lax.rsqrt(jnp.mean(hidden_wide * hidden_wide, axis=-1, keepdims=True) + 1e-06)
        * moe_gain
    ).astype(jnp.bfloat16)
    dest_count = lax.axis_size("seq")
    capacity = 3 * row_count // dest_count
    choice_ids = expert_ids[0].reshape(-1)
    place = jnp.arange(2 * row_count, dtype=jnp.int32)
    earlier = (choice_ids[:, None] == choice_ids[None, :]) & (place[:, None] > place[None, :])
    slot_rank = jnp.sum(earlier.astype(jnp.int32), axis=1)
    slot_index = choice_ids * capacity + slot_rank
    token_index = jnp.arange(2 * row_count, dtype=jnp.int32) // 2
    outgoing = (
        jnp.zeros((dest_count * capacity, width), jnp.bfloat16)
        .at[slot_index]
        .set(moe_in[token_index])
    )
    outgoing = outgoing.reshape(dest_count, capacity, width)
    received = lax.all_to_all(outgoing, "seq", split_axis=0, concat_axis=0, tiled=True)
    flat_rows = received.reshape(-1, width)
    gate = jnp.dot(flat_rows, w_gate[0], preferred_element_type=jnp.float32)
    upper = jnp.dot(flat_rows, w_up[0], preferred_element_type=jnp.float32)
    active = (jax.nn.silu(gate) * upper).astype(jnp.bfloat16)
    produced = jnp.dot(active, w_down[0], preferred_element_type=jnp.float32).astype(jnp.bfloat16)
    returned = lax.all_to_all(
        produced.reshape(received.shape), "seq", split_axis=0, concat_axis=0, tiled=True
    )
    picked = returned.reshape(-1, width)[slot_index].astype(jnp.float32)
    weighted = (gate_weights[0].reshape(-1)[:, None] * picked).reshape(row_count, 2, width)
    mixed = hidden_wide + (weighted[:, 0] + weighted[:, 1])
    return mixed.astype(jnp.bfloat16)[None]


def solution(mesh):
    placed = (
        P(("group", "rep"), "seq", None),
        P(("group", "rep"), "seq", None),
        P(("group", "rep"), "seq", None),
        P(("group", "rep"), "seq", None),
        P(),
        P(),
        P(("group", "rep"), "seq", None),
        P(("group", "rep"), "seq", None),
        P("seq", None, None),
        P("seq", None, None),
        P("seq", None, None),
    )
    ways = dict(mesh.shape)

    def plan(*args):
        n = ways["seq"]
        held = n * sum(w.size // w.shape[0] * w.dtype.itemsize for w in args[-3:])
        whole = args[-1].shape[1] % 256 == 0 and 3 * args[0].shape[1] // n % (16 * ROW_PARTS) == 0
        if ways["group"] == 2 and ways["rep"] == 4 and n == len(PROGRAMS) and whole and held <= GATHER_LIMIT:
            return gathered_weights(n, *args)
        return per_device(*args)

    return jax.shard_map(
        plan,
        mesh=mesh,
        in_specs=placed,
        out_specs=P(("group", "rep"), "seq", None),
        check_vma=False,
    )
```

```python
import functools

import jax
import jax.numpy as jnp
from jax import lax
from jax.experimental import pallas as pl
from jax.experimental.pallas import tpu as pltpu
from jax.sharding import PartitionSpec as P

H = 8
DH = 128
MESH = pl.DeviceIdType.MESH
GATHER_LIMIT = 24 << 20


ASKED = 2
ROW_PARTS = 6
STATE_PARTS = 8
DOUBLED = ((0, 1, 2), (1,), (1, 2), (2,))
M, X, Y, D, NATIVE, STATE, FIRST, LOCAL, INTRA, FINISH, COMPACT, OWN, ACT, DOWN, SERVE, SERVED = range(16)
PROGRAMS = (
    (
        (LOCAL,), (FIRST,), (NATIVE, M, 0, 0, 1), (NATIVE, M, 0, 1, 1), (NATIVE, M, 1, 0, 1), (NATIVE, M, 1, 1, 1),
        (NATIVE, M, 2, 0, 1), (NATIVE, M, 2, 1, 1), (INTRA, 0), (INTRA, 1), (FINISH,), (COMPACT,), (M, 1, 0, 0),
        (OWN,), (M, 1, 0, 1), (M, 1, 1, 0), (X, 1, 0, 0), (Y, 1, 0, 0), (M, 1, 1, 1), (X, 1, 0, 1), (Y, 1, 0, 1),
        (D, 1, 2, 0), (X, 1, 1, 0), (Y, 1, 1, 0), (D, 1, 2, 1), (X, 1, 1, 1), (D, 1, 0, 0), (M, 1, 2, 0),
        (D, 1, 0, 1), (Y, 1, 1, 1), (M, 1, 2, 1), (D, 1, 1, 0), (M, 3, 0, 0), (X, 1, 2, 0), (Y, 1, 2, 0),
        (D, 1, 1, 1), (Y, 1, 2, 1), (M, 3, 0, 1), (ACT, 1), (X, 1, 2, 1), (Y, 3, 0, 0), (NATIVE, D, 1, 0, 1),
        (M, 3, 1, 0), (X, 3, 0, 0), (DOWN, 1), (NATIVE, D, 1, 1, 1), (M, 3, 1, 1), (Y, 3, 0, 1), (X, 3, 0, 1),
        (NATIVE, D, 2, 0, 1), (Y, 3, 1, 0), (X, 3, 1, 0), (NATIVE, D, 2, 1, 1), (D, 3, 0, 0), (X, 3, 1, 1),
        (M, 3, 2, 0), (NATIVE, D, 0, 0, 1), (Y, 3, 1, 1), (D, 3, 0, 1), (M, 3, 2, 1), (NATIVE, D, 0, 1, 1),
        (D, 3, 1, 0), (X, 3, 2, 0), (Y, 3, 2, 0), (D, 3, 1, 1), (Y, 3, 2, 1), (ACT, 3), (X, 3, 2, 1), (D, 3, 2, 0),
        (D, 3, 2, 1), (DOWN, 3), (SERVED,),
    ),
    (
        (NATIVE, M, 0, 0, 2), (NATIVE, M, 0, 1, 2), (NATIVE, M, 1, 0, 2), (NATIVE, M, 1, 1, 2), (NATIVE, M, 0, 0, 0),
        (NATIVE, M, 0, 1, 0), (NATIVE, M, 1, 0, 0), (NATIVE, M, 1, 1, 0), (LOCAL,), (INTRA, 0), (NATIVE, M, 2, 0, 2),
        (INTRA, 1), (NATIVE, D, 2, 0, 0), (NATIVE, M, 2, 1, 2), (NATIVE, D, 2, 1, 0), (STATE, 0), (M, 2, 0, 0),
        (STATE, 1), (NATIVE, M, 2, 0, 0), (STATE, 2), (M, 2, 0, 1), (STATE, 3), (NATIVE, M, 2, 1, 0), (STATE, 4),
        (M, 2, 2, 0), (STATE, 5), (X, 2, 0, 0), (Y, 2, 0, 0), (STATE, 6), (M, 2, 2, 1), (STATE, 7), (X, 2, 0, 1),
        (Y, 2, 0, 1), (FINISH,), (M, 2, 1, 0), (M, 0, 0, 0), (X, 2, 2, 0), (Y, 2, 2, 0), (M, 2, 1, 1), (M, 0, 0, 1),
        (X, 2, 2, 1), (D, 2, 0, 0), (M, 3, 0, 0), (OWN,), (D, 2, 0, 1), (Y, 2, 2, 1), (M, 0, 1, 0), (X, 2, 1, 0),
        (Y, 2, 1, 0), (M, 3, 0, 1), (M, 0, 1, 1), (M, 3, 1, 0), (M, 0, 2, 0), (Y, 0, 0, 0), (X, 0, 0, 0),
        (M, 3, 1, 1), (M, 0, 2, 1), (X, 2, 1, 1), (D, 2, 2, 0), (D, 2, 1, 0), (X, 0, 0, 1), (Y, 2, 1, 1),
        (NATIVE, D, 1, 0, 2), (D, 2, 1, 1), (X, 3, 0, 0), (Y, 0, 0, 1), (NATIVE, D, 1, 1, 2), (ACT, 2), (M, 3, 2, 0),
        (Y, 3, 0, 0), (D, 2, 2, 1), (M, 3, 2, 1), (X, 0, 1, 0), (Y, 0, 1, 0), (DOWN, 2), (SERVE, 0), (X, 3, 0, 1),
        (Y, 3, 0, 1), (D, 3, 1, 0), (SERVE, 1), (D, 3, 1, 1), (SERVE, 2), (X, 0, 1, 1), (Y, 0, 1, 1), (SERVE, 3),
        (D, 0, 1, 0), (X, 3, 1, 0), (Y, 3, 1, 0), (D, 3, 2, 0), (SERVE, 4), (D, 3, 2, 1), (SERVE, 5), (Y, 0, 2, 0),
        (D, 0, 1, 1), (X, 0, 2, 0), (D, 0, 2, 0), (X, 3, 1, 1), (Y, 3, 1, 1), (D, 0, 2, 1), (X, 0, 2, 1),
        (Y, 0, 2, 1), (D, 0, 0, 0), (X, 3, 2, 0), (D, 3, 0, 0), (D, 0, 0, 1), (X, 3, 2, 1), (Y, 3, 2, 0), (ACT, 0),
        (D, 3, 0, 1), (Y, 3, 2, 1), (DOWN, 0), (ACT, 3), (DOWN, 3),
    ),
    (
        (NATIVE, M, 0, 0, 1), (NATIVE, M, 0, 1, 1), (NATIVE, M, 2, 0, 1), (NATIVE, M, 2, 1, 1), (LOCAL,), (INTRA, 0),
        (INTRA, 1), (NATIVE, M, 1, 0, 1), (NATIVE, M, 1, 1, 1), (M, 1, 0, 0), (D, 3, 0, 0), (M, 1, 0, 1),
        (D, 3, 0, 1), (M, 1, 1, 0), (M, 3, 0, 0), (X, 1, 0, 0), (Y, 1, 0, 0), (M, 1, 1, 1), (M, 3, 0, 1),
        (X, 1, 0, 1), (Y, 1, 0, 1), (M, 3, 1, 0), (M, 1, 2, 0), (X, 1, 1, 0), (Y, 1, 1, 0), (M, 3, 1, 1),
        (M, 1, 2, 1), (X, 3, 0, 0), (Y, 3, 0, 0), (NATIVE, D, 1, 0, 1), (STATE, 0), (NATIVE, D, 1, 1, 1),
        (M, 3, 2, 0), (STATE, 1), (X, 1, 1, 1), (D, 1, 0, 0), (STATE, 2), (M, 3, 2, 1), (STATE, 3), (X, 3, 0, 1),
        (Y, 1, 1, 1), (STATE, 4), (D, 3, 1, 0), (STATE, 5), (D, 1, 0, 1), (Y, 3, 0, 1), (STATE, 6), (D, 3, 1, 1),
        (STATE, 7), (FINISH,), (X, 3, 1, 0), (Y, 3, 1, 0), (D, 3, 2, 0), (M, 0, 0, 0), (X, 1, 2, 0), (Y, 1, 2, 0),
        (D, 3, 2, 1), (M, 0, 0, 1), (X, 3, 1, 1), (Y, 3, 1, 1), (M, 0, 1, 0), (ACT, 3), (X, 1, 2, 1), (Y, 1, 2, 1),
        (M, 0, 1, 1), (X, 3, 2, 0), (Y, 3, 2, 0), (M, 0, 2, 0), (X, 3, 2, 1), (Y, 3, 2, 1), (M, 0, 2, 1), (SERVE, 0),
        (Y, 0, 0, 0), (X, 0, 0, 0), (DOWN, 3), (D, 1, 1, 0), (OWN,), (X, 0, 0, 1), (D, 1, 2, 0), (D, 1, 1, 1),
        (SERVE, 1), (Y, 0, 0, 1), (X, 0, 1, 0), (SERVE, 2), (D, 1, 2, 1), (Y, 0, 1, 0), (SERVE, 3), (D, 0, 1, 0),
        (ACT, 1), (Y, 0, 1, 1), (X, 0, 1, 1), (SERVE, 4), (D, 0, 1, 1), (X, 0, 2, 0), (Y, 0, 2, 0), (DOWN, 1),
        (SERVE, 5), (D, 0, 2, 0), (X, 0, 2, 1), (Y, 0, 2, 1), (D, 0, 2, 1), (D, 0, 0, 1), (D, 0, 0, 0), (ACT, 0),
        (DOWN, 0),
    ),
    (
        (NATIVE, D, 0, 0, 2), (NATIVE, D, 0, 1, 2), (NATIVE, M, 0, 0, 2), (NATIVE, M, 0, 1, 2), (LOCAL,), (INTRA, 0),
        (NATIVE, M, 1, 0, 2), (NATIVE, M, 1, 1, 2), (NATIVE, M, 2, 0, 2), (NATIVE, M, 2, 1, 2), (INTRA, 1),
        (M, 1, 0, 0), (NATIVE, D, 1, 0, 2), (M, 1, 0, 1), (NATIVE, D, 1, 1, 2), (M, 1, 1, 0), (NATIVE, D, 2, 0, 2),
        (X, 1, 0, 0), (Y, 1, 0, 0), (M, 1, 1, 1), (NATIVE, D, 2, 1, 2), (X, 1, 0, 1), (Y, 1, 0, 1), (M, 1, 2, 0),
        (X, 1, 1, 0), (Y, 1, 1, 0), (M, 1, 2, 1), (X, 1, 1, 1), (D, 1, 0, 0), (STATE, 0), (STATE, 1), (D, 1, 0, 1),
        (Y, 1, 1, 1), (STATE, 2), (STATE, 3), (X, 1, 2, 0), (Y, 1, 2, 0), (STATE, 4), (STATE, 5), (X, 1, 2, 1),
        (D, 1, 1, 0), (STATE, 6), (STATE, 7), (FINISH,), (D, 1, 1, 1), (Y, 1, 2, 1), (COMPACT,), (M, 0, 0, 0),
        (D, 1, 2, 0), (ACT, 1), (M, 0, 0, 1), (OWN,), (M, 0, 1, 0), (D, 1, 2, 1), (Y, 0, 0, 0), (M, 0, 1, 1),
        (X, 0, 0, 0), (DOWN, 1), (Y, 0, 0, 1), (M, 0, 2, 0), (X, 0, 0, 1), (Y, 0, 1, 0), (M, 0, 2, 1), (X, 0, 1, 0),
        (Y, 0, 1, 1), (X, 0, 1, 1), (D, 0, 0, 0), (D, 0, 0, 1), (Y, 0, 2, 0), (X, 0, 2, 0), (Y, 0, 2, 1),
        (X, 0, 2, 1), (D, 0, 1, 0), (D, 0, 1, 1), (D, 0, 2, 0), (ACT, 0), (D, 0, 2, 1), (SERVED,), (DOWN, 0),
    ),
)


def fused_kernel(
    n,
    q_hbm,
    k_hbm,
    v_hbm,
    s_hbm,
    attn_gain_hbm,
    moe_gain_hbm,
    ids_hbm,
    gw_hbm,
    wg_hbm,
    wu_hbm,
    wd_hbm,
    out_ref,
    qb,
    kb,
    vb,
    sb,
    attn_gain_ref,
    moe_gain_ref,
    ids,
    gw,
    wg,
    wu,
    wd,
    local,
    prefix,
    passed,
    attended,
    hidden,
    moe_in,
    total,
    active,
    pick,
    rows_out,
    rows_in,
    load_sem,
    send_sem,
    piece_sem,
    sib_sem,
    state_send,
    state_recv,
    row_send,
    row_recv,
):
    g, z, r = lax.axis_index("group"), lax.axis_index("seq"), lax.axis_index("rep")
    x, c = r // 2, r % 2
    r_x, r_s = 2 * (1 - x) + c, 2 * x + (1 - c)
    piece_of = {
        M: g * 4 + r,
        X: g * 4 + r_x,
        Y: (1 - g) * 4 + r,
        D: (1 - g) * 4 + r_x,
    }
    to_x, to_y, to_s = {"rep": r_x}, {"group": 1 - g}, {"rep": r_s}
    rows = qb.shape[0]
    cap = rows_in.shape[0]
    group = cap // ROW_PARTS
    hbm = (wg_hbm, wu_hbm, wd_hbm)
    held = (wg, wu, wd)

    def span(t, piece, half):
        size = held[t].shape[1] // 16
        return pl.ds(pl.multiple_of((half * 8 + piece) * size, size), size)

    barrier = pltpu.get_barrier_semaphore()
    for to in (to_x, to_y, to_s):
        pl.semaphore_signal(barrier, inc=1, device_id=to, device_id_type=MESH)

    @pl.when(z < n - 1)
    def _():
        pl.semaphore_signal(barrier, inc=1, device_id={"seq": z + 1}, device_id_type=MESH)

    @pl.when(z > 0)
    def _():
        pl.semaphore_signal(barrier, inc=1, device_id={"seq": z - 1}, device_id_type=MESH)

    loads = [
        pltpu.make_async_copy(src, dst, load_sem.at[i])
        for i, (src, dst) in enumerate(
            [
                (k_hbm.at[0], kb),
                (v_hbm.at[0], vb),
                (q_hbm.at[0], qb),
                (s_hbm.at[0], sb),
                (attn_gain_hbm, attn_gain_ref),
                (moe_gain_hbm, moe_gain_ref),
                (ids_hbm.at[0], ids),
                (gw_hbm.at[0], gw),
                (wg_hbm.at[0], wg.at[z]),
                (wu_hbm.at[0], wu.at[z]),
                (wd_hbm.at[0], wd.at[z]),
            ]
        )
    ]
    for load in loads[:4]:
        load.start()
    pl.semaphore_wait(barrier, 3 + (z < n - 1).astype(jnp.int32) + (z > 0).astype(jnp.int32))

    def head(h):
        return pl.ds(h * DH, DH)

    def local_state():
        loads[0].wait()
        loads[1].wait()
        for h in range(H):
            local[h] = lax.dot_general(
                kb[:, head(h)],
                vb[:, head(h)],
                (((0,), (0,)), ((), ())),
                preferred_element_type=jnp.float32,
            )

    def intra(part):
        if part == 0:
            loads[2].wait()
        causal = lax.broadcasted_iota(jnp.int32, (rows, rows), 0) >= lax.broadcasted_iota(
            jnp.int32, (rows, rows), 1
        )
        for h in range(part * H // 2, (part + 1) * H // 2):
            scores = lax.dot_general(
                qb[:, head(h)],
                kb[:, head(h)],
                (((1,), (1,)), ((), ())),
                preferred_element_type=jnp.float32,
            )
            weights = jnp.where(causal, scores, 0.0).astype(jnp.bfloat16)
            attended[:, head(h)] = jnp.dot(
                weights, vb[:, head(h)], preferred_element_type=jnp.float32
            )

    def finish():
        for load in loads[3:8]:
            load.wait()
        square = jnp.zeros((rows, DH), jnp.float32)
        for h in range(H):
            both = attended[:, head(h)] + jnp.dot(
                qb[:, head(h)], prefix[h], preferred_element_type=jnp.float32
            )
            scale = lax.rsqrt(jnp.mean(both * both, axis=-1, keepdims=True) + 1e-06)
            wide = sb[:, head(h)].astype(jnp.float32) + both * scale * attn_gain_ref[:, head(h)]
            rounded = wide.astype(jnp.bfloat16)
            hidden[:, head(h)] = rounded
            wide = rounded.astype(jnp.float32)
            square = square + wide * wide
        scale = lax.rsqrt(jnp.sum(square, axis=-1, keepdims=True) / (H * DH) + 1e-06)
        for h in range(H):
            wide = hidden[:, head(h)].astype(jnp.float32)
            moe_in[:, head(h)] = (wide * scale * moe_gain_ref[:, head(h)]).astype(jnp.bfloat16)

    def activate(inputs, e):
        gate = jnp.dot(inputs, wg[e], preferred_element_type=jnp.float32)
        upper = jnp.dot(inputs, wu[e], preferred_element_type=jnp.float32)
        return (gate / (1.0 + jnp.exp(-gate)) * upper).astype(jnp.bfloat16)

    def down(acts, e):
        return jnp.dot(acts, wd[e], preferred_element_type=jnp.float32).astype(jnp.bfloat16)

    def weight_of(e):
        chosen = jnp.sum(jnp.where(ids[...] == e, gw[...], 0.0), axis=0, keepdims=True)
        return jnp.broadcast_to(chosen, (8, rows)).T[:, :1]

    def weigh(made, e):
        return made.astype(jnp.float32) * weight_of(e)

    def program(at):
        end = at in (0, n - 1)
        near = 1 if at == 0 else at - 1 if at == n - 1 else n - 1 - at
        outer = None if end else (0 if at < n - 1 - at else n - 1)
        sent = {}

        def push(sem, copy):
            sent[sem] = sent.get(sem, 0) + 1
            copy.start()

        def piece(kind, landed, e, t, half, sem, to, source=None):
            where = span(t, piece_of[kind], half)
            dst = held[t].at[e, where, :]
            return pltpu.make_async_remote_copy(
                src_ref=dst if source is None else source.at[0, where, :],
                dst_ref=dst,
                send_sem=send_sem.at[sem],
                recv_sem=landed,
                device_id=to,
                device_id_type=MESH,
            )

        def landing(kind, e, t, half):
            return piece_sem.at[kind, e, t, half]

        def doubled(e, t):
            if end:
                return at == 0 and e == near and t in DOUBLED[3]
            return t in DOUBLED[0 if e == outer else 1 if e == near else 2]

        def native(kind, t, half, to):
            landed = landing(kind, at, t, half)
            sem = 0 if to > at else 1
            push(sem, piece(kind, landed, at, t, half, sem, {"seq": to}, hbm[t]))

        def pass_on(kind, e, t, half):
            piece(kind, landing(kind, e, t, half), e, t, half, 0, to_x).wait_recv()
            if kind == M:
                if not end and not (outer == 0 and e == ASKED):
                    to = near if e == outer else outer
                    sem = 0 if to > at else 1
                    push(sem, piece(M, landing(M, e, t, half), e, t, half, sem, {"seq": to}))
                push(2, piece(M, landing(X, e, t, half), e, t, half, 2, to_x))
                push(3, piece(M, landing(Y, e, t, half), e, t, half, 3, to_y))
            if kind == D and not end and e == outer and t in DOUBLED[2]:
                sem = 0 if near > at else 1
                push(sem, piece(D, landing(D, e, t, half), e, t, half, sem, {"seq": near}))
            if kind == X and half == 0 and not doubled(e, t):
                push(3, piece(X, landing(D, e, t, half), e, t, half, 3, to_y))
            if kind == Y and half == 1 and not doubled(e, t):
                push(2, piece(Y, landing(D, e, t, half), e, t, half, 2, to_x))
            sem = 4 + kind
            push(sem, piece(kind, sib_sem.at[e, t, half], e, t, half, sem, to_s))

        def from_sibling(e, t, half):
            some = held[t].at[e, pl.ds(0, held[t].shape[1] // 4), :]
            pltpu.make_async_copy(some, some, sib_sem.at[e, t, half]).wait()

        def state_copy(part):
            heads = pl.ds(part * (H // STATE_PARTS), H // STATE_PARTS)
            return pltpu.make_async_remote_copy(
                src_ref=passed.at[heads],
                dst_ref=prefix.at[heads],
                send_sem=state_send.at[part],
                recv_sem=state_recv.at[part],
                device_id={"seq": at + 1 if at < n - 1 else at - 1},
                device_id_type=MESH,
            )

        def first_state():
            prefix[...] = jnp.zeros_like(prefix)
            passed[...] = local[...].astype(passed.dtype)
            for part in range(STATE_PARTS):
                state_copy(part).start()

        def next_state(part):
            state_copy(part).wait_recv()
            if at < n - 1:
                heads = pl.ds(part * (H // STATE_PARTS), H // STATE_PARTS)
                passed[heads] = (prefix[heads].astype(jnp.float32) + local[heads]).astype(
                    passed.dtype
                )
                state_copy(part).start()

        def row_copy(part):
            some = pl.ds(part * group, group)
            return pltpu.make_async_remote_copy(
                src_ref=rows_out.at[some],
                dst_ref=rows_in.at[some],
                send_sem=row_send.at[part],
                recv_sem=row_recv.at[part],
                device_id={"seq": near if end else outer},
                device_id_type=MESH,
            )

        def compact():
            named = jnp.max((ids[...] == ASKED).astype(jnp.float32), axis=0, keepdims=True)
            earlier = lax.broadcasted_iota(jnp.int32, (rows, rows), 0) < lax.broadcasted_iota(
                jnp.int32, (rows, rows), 1
            )
            place = jnp.dot(
                jnp.broadcast_to(named, (8, rows)).astype(jnp.bfloat16),
                earlier.astype(jnp.bfloat16),
                preferred_element_type=jnp.float32,
            )[:1]
            slots = lax.broadcasted_iota(jnp.int32, (cap, rows), 0).astype(jnp.float32)
            pick[...] = jnp.where(slots == place, named, 0.0).astype(jnp.bfloat16)
            rows_out[...] = jnp.dot(
                pick[...], moe_in[...], preferred_element_type=jnp.float32
            ).astype(jnp.bfloat16)
            for part in range(ROW_PARTS):
                row_copy(part).start()

        def serve(part):
            row_copy(part).wait_recv()
            some = pl.ds(part * group, group)
            rows_out[some] = down(activate(rows_in[some], ASKED), ASKED)
            row_copy(part).start()

        def served():
            for part in range(ROW_PARTS):
                row_copy(part).wait_recv()
            made = lax.dot_general(
                pick[...],
                rows_in[...],
                (((0,), (0,)), ((), ())),
                preferred_element_type=jnp.float32,
            )
            return weigh(made, ASKED)

        def own():
            return weigh(down(activate(moe_in[...], at), at), at)

        def act(e):
            for t in range(2):
                for half in range(2):
                    from_sibling(e, t, half)
            active[e] = activate(moe_in[...], e)

        def expert_out(e):
            weight = weight_of(e)
            from_sibling(e, 2, 0)
            from_sibling(e, 2, 1)
            return down(active[e], e).astype(jnp.float32) * weight

        def expert_out_by_halves(e):
            weight = weight_of(e)
            depth = wd.shape[1] // 2
            from_sibling(e, 2, 0)
            attended[...] = jnp.dot(
                active[e, :, :depth], wd[e, :depth], preferred_element_type=jnp.float32
            )
            from_sibling(e, 2, 1)
            made = attended[...] + jnp.dot(
                active[e, :, depth:], wd[e, depth:], preferred_element_type=jnp.float32
            )
            return made.astype(jnp.bfloat16).astype(jnp.float32) * weight

        def settle():
            for sem, count in sent.items():
                some = wg.at[:, pl.ds(0, wg.shape[1] // 64 * count), :]
                pltpu.make_async_copy(some, some, send_sem.at[sem]).wait()
            if at < n - 1:
                for part in range(STATE_PARTS):
                    state_copy(part).wait_send()
            for part in range(ROW_PARTS):
                row_copy(part).wait_send()

        items = PROGRAMS[at]
        started = ready = begun = False
        for index, item in enumerate(items):
            name, *rest = item
            if (name == OWN or name == SERVE and at == ASKED) and not ready:
                ready = True
                for load in loads[8:]:
                    load.wait()
            if name <= D:
                pass_on(name, *rest)
            elif name == NATIVE:
                native(*rest)
            elif name == STATE:
                next_state(*rest)
            elif name == FIRST:
                first_state()
            elif name == LOCAL:
                local_state()
            elif name == INTRA:
                intra(*rest)
            elif name == FINISH:
                finish()
            elif name == COMPACT:
                compact()
            elif name == SERVE:
                serve(*rest)
            elif name == ACT:
                act(*rest)
            else:
                last = index == len(items) - 1
                if last:
                    settle()
                    total[...] += hidden[...].astype(jnp.float32)
                if name == OWN:
                    added = own()
                elif name == SERVED:
                    added = served()
                else:
                    added = (expert_out_by_halves if last else expert_out)(*rest)
                if begun:
                    added = total[...] + added
                begun = True
                if last:
                    out_ref[0] = added.astype(out_ref.dtype)
                else:
                    total[...] = added
            if name == LOCAL and not started:
                started = True
                for load in loads[4:]:
                    load.start()

    for at in range(n):

        @pl.when(z == at)
        def _():
            program(at)


def gathered_weights(
    n,
    queries,
    keys,
    values,
    stream,
    attn_gain,
    moe_gain,
    expert_ids,
    gate_weights,
    w_gate,
    w_up,
    w_down,
):
    rows, width = queries.shape[1:]
    units = w_gate.shape[2]
    cap = 3 * rows // n
    half = jnp.bfloat16
    anywhere = pl.BlockSpec(memory_space=pl.ANY)
    vmem = pl.BlockSpec(memory_space=pltpu.VMEM)
    dma = pltpu.SemaphoreType.DMA
    return pl.pallas_call(
        functools.partial(fused_kernel, n),
        out_shape=pltpu.VMEM((1, rows, width), half),
        in_specs=[anywhere] * 11,
        out_specs=vmem,
        scratch_shapes=[
            pltpu.VMEM((rows, width), half),
            pltpu.VMEM((rows, width), half),
            pltpu.VMEM((rows, width), half),
            pltpu.VMEM((rows, width), half),
            pltpu.VMEM((1, width), jnp.float32),
            pltpu.VMEM((1, width), jnp.float32),
            pltpu.VMEM((2, rows), jnp.int32),
            pltpu.VMEM((2, rows), jnp.float32),
            pltpu.VMEM((n, width, units), half),
            pltpu.VMEM((n, width, units), half),
            pltpu.VMEM((n, units, width), half),
            pltpu.VMEM((H, DH, DH), jnp.float32),
            pltpu.VMEM((H, DH, DH), half),
            pltpu.VMEM((H, DH, DH), half),
            pltpu.VMEM((rows, width), jnp.float32),
            pltpu.VMEM((rows, width), half),
            pltpu.VMEM((rows, width), half),
            pltpu.VMEM((rows, width), jnp.float32),
            pltpu.VMEM((n, rows, units), half),
            pltpu.VMEM((cap, rows), half),
            pltpu.VMEM((cap, width), half),
            pltpu.VMEM((cap, width), half),
            dma((11,)),
            dma((8,)),
            dma((4, n, 3, 2)),
            dma((n, 3, 2)),
            dma((STATE_PARTS,)),
            dma((STATE_PARTS,)),
            dma((ROW_PARTS,)),
            dma((ROW_PARTS,)),
        ],
        compiler_params=pltpu.CompilerParams(
            collective_id=0, has_side_effects=True, vmem_limit_bytes=(64 << 20) - (600 << 10)
        ),
    )(
        queries,
        keys,
        values,
        stream,
        attn_gain[None],
        moe_gain[None],
        jnp.swapaxes(expert_ids, 1, 2),
        jnp.swapaxes(gate_weights, 1, 2),
        w_gate,
        w_up,
        w_down,
    )


def prefix_2(value, axis, join, neutral):
    count, mine = (lax.axis_size(axis), lax.axis_index(axis))
    pieces = lax.all_gather(value, axis)
    total = jnp.full_like(value, 0) + jnp.asarray(neutral, value.dtype)

    def lap(position, total):
        longer = join(total, pieces[position])
        return jnp.where(position < mine, longer, total)

    return lax.fori_loop(0, count - 1, lap, total)


def add_states(earlier, later):
    return earlier + later


def per_device(
    queries,
    keys,
    values,
    stream,
    attn_gain,
    moe_gain,
    expert_ids,
    gate_weights,
    w_gate,
    w_up,
    w_down,
):
    row_count = queries.shape[1]
    width = queries.shape[2]
    query_heads = queries[0].reshape(row_count, H, DH)
    key_heads = keys[0].reshape(row_count, H, DH)
    value_heads = values[0].reshape(row_count, H, DH)
    own_state = jnp.einsum(
        "shd,she->hde", key_heads, value_heads, preferred_element_type=jnp.float32
    )
    scores = jnp.einsum("thd,shd->hts", query_heads, key_heads, preferred_element_type=jnp.float32)
    causal = jnp.arange(row_count)[:, None] >= jnp.arange(row_count)[None, :]
    weights = jnp.where(causal[None], scores, jnp.zeros((), jnp.float32)).astype(jnp.bfloat16)
    intra = jnp.einsum("hts,shd->thd", weights, value_heads, preferred_element_type=jnp.float32)
    prefix = prefix_2(own_state, "seq", add_states, jnp.zeros_like(own_state))
    inter = jnp.einsum(
        "thd,hde->the", query_heads, prefix.astype(jnp.bfloat16), preferred_element_type=jnp.float32
    )
    attended = intra + inter
    normed = attended * lax.rsqrt(jnp.mean(attended * attended, axis=-1, keepdims=True) + 1e-06)
    hidden = (stream[0].astype(jnp.float32) + normed.reshape(row_count, width) * attn_gain).astype(
        jnp.bfloat16
    )
    hidden_wide = hidden.astype(jnp.float32)
    moe_in = (
        hidden_wide
        * lax.rsqrt(jnp.mean(hidden_wide * hidden_wide, axis=-1, keepdims=True) + 1e-06)
        * moe_gain
    ).astype(jnp.bfloat16)
    dest_count = lax.axis_size("seq")
    capacity = 3 * row_count // dest_count
    choice_ids = expert_ids[0].reshape(-1)
    place = jnp.arange(2 * row_count, dtype=jnp.int32)
    earlier = (choice_ids[:, None] == choice_ids[None, :]) & (place[:, None] > place[None, :])
    slot_rank = jnp.sum(earlier.astype(jnp.int32), axis=1)
    slot_index = choice_ids * capacity + slot_rank
    token_index = jnp.arange(2 * row_count, dtype=jnp.int32) // 2
    outgoing = (
        jnp.zeros((dest_count * capacity, width), jnp.bfloat16)
        .at[slot_index]
        .set(moe_in[token_index])
    )
    outgoing = outgoing.reshape(dest_count, capacity, width)
    received = lax.all_to_all(outgoing, "seq", split_axis=0, concat_axis=0, tiled=True)
    flat_rows = received.reshape(-1, width)
    gate = jnp.dot(flat_rows, w_gate[0], preferred_element_type=jnp.float32)
    upper = jnp.dot(flat_rows, w_up[0], preferred_element_type=jnp.float32)
    active = (jax.nn.silu(gate) * upper).astype(jnp.bfloat16)
    produced = jnp.dot(active, w_down[0], preferred_element_type=jnp.float32).astype(jnp.bfloat16)
    returned = lax.all_to_all(
        produced.reshape(received.shape), "seq", split_axis=0, concat_axis=0, tiled=True
    )
    picked = returned.reshape(-1, width)[slot_index].astype(jnp.float32)
    weighted = (gate_weights[0].reshape(-1)[:, None] * picked).reshape(row_count, 2, width)
    mixed = hidden_wide + (weighted[:, 0] + weighted[:, 1])
    return mixed.astype(jnp.bfloat16)[None]


def solution(mesh):
    placed = (
        P(("group", "rep"), "seq", None),
        P(("group", "rep"), "seq", None),
        P(("group", "rep"), "seq", None),
        P(("group", "rep"), "seq", None),
        P(),
        P(),
        P(("group", "rep"), "seq", None),
        P(("group", "rep"), "seq", None),
        P("seq", None, None),
        P("seq", None, None),
        P("seq", None, None),
    )
    ways = dict(mesh.shape)

    def plan(*args):
        n = ways["seq"]
        held = n * sum(w.size // w.shape[0] * w.dtype.itemsize for w in args[-3:])
        whole = args[-1].shape[1] % 256 == 0 and 3 * args[0].shape[1] // n % (16 * ROW_PARTS) == 0
        if ways["group"] == 2 and ways["rep"] == 4 and n == len(PROGRAMS) and whole and held <= GATHER_LIMIT:
            return gathered_weights(n, *args)
        return per_device(*args)

    return jax.shard_map(
        plan,
        mesh=mesh,
        in_specs=placed,
        out_specs=P(("group", "rep"), "seq", None),
        check_vma=False,
    )
```

```python
import functools

import jax
import jax.numpy as jnp
from jax import lax
from jax.experimental import pallas as pl
from jax.experimental.pallas import tpu as pltpu
from jax.sharding import PartitionSpec as P

H = 8
DH = 128
MESH = pl.DeviceIdType.MESH
GATHER_LIMIT = 24 << 20


ASKED = 2
ROW_PARTS = 6
STATE_PARTS = 8
CUT = (2, 2, 2)
DOUBLED = (((), (1,), ()), ((0, 1, 2), (1,), (1, 2)), ((0, 1, 2), (0, 1), (1, 2)), ((), (), ()))
M, X, Y, D, NATIVE, STATE, FIRST, LOCAL, INTRA, FINISH, COMPACT, OWN, ACT, DOWN, SERVE, SERVED = range(16)
PROGRAMS = (
    (
        (LOCAL,), (FIRST,), (NATIVE, M, 0, 0, 1), (NATIVE, M, 0, 1, 1), (NATIVE, M, 1, 0, 1), (NATIVE, M, 1, 1, 1),
        (NATIVE, M, 2, 0, 1), (NATIVE, M, 2, 1, 1), (INTRA, 0), (INTRA, 1), (FINISH,), (COMPACT,), (M, 1, 2, 0),
        (OWN,), (M, 1, 2, 1), (M, 1, 0, 0), (X, 1, 2, 0), (Y, 1, 2, 0), (M, 1, 0, 1), (X, 1, 2, 1), (Y, 1, 2, 1),
        (M, 1, 1, 0), (X, 1, 0, 0), (Y, 1, 0, 0), (M, 1, 1, 1), (X, 1, 0, 1), (D, 1, 2, 0), (D, 1, 2, 1),
        (Y, 1, 0, 1), (X, 1, 1, 0), (Y, 1, 1, 0), (M, 3, 0, 0), (X, 1, 1, 1), (D, 1, 0, 0), (M, 3, 0, 1),
        (Y, 1, 1, 1), (D, 1, 0, 1), (M, 3, 1, 0), (X, 3, 0, 0), (Y, 3, 0, 0), (NATIVE, D, 1, 0, 1), (M, 3, 1, 1),
        (NATIVE, D, 1, 1, 1), (X, 3, 0, 1), (Y, 3, 0, 1), (D, 1, 1, 0), (NATIVE, D, 2, 0, 1), (X, 3, 1, 0),
        (Y, 3, 1, 0), (D, 1, 1, 1), (NATIVE, D, 2, 1, 1), (X, 3, 1, 1), (D, 3, 0, 0), (M, 3, 2, 0),
        (NATIVE, D, 0, 0, 1), (D, 3, 0, 1), (Y, 3, 1, 1), (M, 3, 2, 1), (NATIVE, D, 0, 1, 1), (D, 3, 1, 0), (ACT, 1),
        (DOWN, 1), (X, 3, 2, 0), (Y, 3, 2, 0), (D, 3, 1, 1), (Y, 3, 2, 1), (ACT, 3), (X, 3, 2, 1), (D, 3, 2, 0),
        (D, 3, 2, 1), (DOWN, 3), (SERVED,),
    ),
    (
        (NATIVE, M, 1, 0, 2), (NATIVE, M, 1, 1, 2), (NATIVE, M, 2, 0, 2), (NATIVE, M, 2, 1, 2), (NATIVE, M, 2, 0, 0),
        (NATIVE, M, 2, 1, 0), (LOCAL,), (NATIVE, M, 0, 0, 0), (NATIVE, M, 0, 1, 0), (INTRA, 0), (NATIVE, M, 0, 0, 2),
        (INTRA, 1), (NATIVE, M, 1, 0, 0), (NATIVE, M, 0, 1, 2), (NATIVE, M, 1, 1, 0), (STATE, 0), (M, 2, 0, 0),
        (STATE, 1), (STATE, 2), (M, 2, 0, 1), (STATE, 3), (STATE, 4), (M, 2, 2, 0), (STATE, 5), (Y, 2, 0, 0),
        (X, 2, 0, 0), (STATE, 6), (M, 2, 2, 1), (STATE, 7), (Y, 2, 0, 1), (X, 2, 0, 1), (FINISH,), (M, 2, 1, 0),
        (M, 0, 0, 0), (Y, 2, 2, 0), (X, 2, 2, 0), (M, 2, 1, 1), (M, 0, 0, 1), (X, 2, 2, 1), (D, 2, 0, 0),
        (M, 3, 0, 0), (OWN,), (Y, 2, 2, 1), (M, 0, 1, 0), (M, 3, 0, 1), (M, 0, 1, 1), (X, 2, 1, 0), (Y, 2, 1, 0),
        (D, 2, 0, 1), (M, 3, 1, 0), (M, 0, 2, 0), (Y, 0, 0, 0), (X, 0, 0, 0), (M, 3, 1, 1), (NATIVE, D, 1, 0, 0),
        (NATIVE, D, 1, 1, 0), (M, 0, 2, 1), (D, 2, 2, 0), (X, 2, 1, 1), (D, 2, 1, 0), (X, 0, 0, 1), (Y, 2, 1, 1),
        (NATIVE, D, 0, 0, 2), (D, 2, 1, 1), (X, 3, 0, 0), (Y, 0, 0, 1), (NATIVE, D, 0, 1, 2), (ACT, 2), (M, 3, 2, 0),
        (D, 2, 2, 1), (Y, 3, 0, 0), (M, 3, 2, 1), (DOWN, 2), (Y, 0, 1, 0), (X, 0, 1, 0), (SERVE, 0), (D, 3, 1, 0),
        (X, 3, 0, 1), (Y, 3, 0, 1), (NATIVE, D, 1, 0, 2), (NATIVE, D, 1, 1, 2), (SERVE, 1), (D, 3, 1, 1), (SERVE, 2),
        (Y, 0, 1, 1), (X, 0, 1, 1), (SERVE, 3), (D, 3, 2, 0), (X, 3, 1, 0), (Y, 3, 1, 0), (D, 0, 1, 0), (SERVE, 4),
        (D, 3, 2, 1), (SERVE, 5), (X, 0, 2, 0), (Y, 0, 2, 0), (D, 0, 1, 1), (D, 0, 2, 0), (X, 3, 1, 1), (Y, 3, 1, 1),
        (D, 0, 2, 1), (X, 0, 2, 1), (Y, 0, 2, 1), (D, 0, 0, 0), (X, 3, 2, 0), (D, 3, 0, 0), (D, 0, 0, 1),
        (X, 3, 2, 1), (Y, 3, 2, 0), (ACT, 0), (D, 3, 0, 1), (Y, 3, 2, 1), (DOWN, 0), (ACT, 3), (DOWN, 3),
    ),
    (
        (NATIVE, M, 0, 0, 1), (NATIVE, M, 0, 1, 1), (NATIVE, M, 2, 0, 1), (NATIVE, M, 2, 1, 1), (LOCAL,), (INTRA, 0),
        (INTRA, 1), (NATIVE, M, 1, 0, 1), (NATIVE, M, 1, 1, 1), (D, 3, 0, 0), (M, 1, 1, 0), (D, 3, 0, 1),
        (M, 1, 1, 1), (M, 3, 0, 0), (M, 1, 2, 0), (X, 1, 1, 0), (Y, 1, 1, 0), (M, 3, 0, 1), (M, 1, 2, 1),
        (X, 1, 1, 1), (Y, 1, 1, 1), (M, 1, 0, 0), (M, 3, 1, 0), (X, 3, 0, 0), (Y, 3, 0, 0), (M, 1, 0, 1),
        (M, 3, 1, 1), (X, 1, 2, 0), (STATE, 0), (NATIVE, D, 1, 0, 1), (NATIVE, D, 1, 1, 1), (Y, 1, 2, 0),
        (M, 3, 2, 0), (STATE, 1), (X, 3, 0, 1), (Y, 3, 0, 1), (STATE, 2), (M, 3, 2, 1), (STATE, 3), (X, 1, 2, 1),
        (Y, 1, 2, 1), (STATE, 4), (D, 3, 1, 0), (STATE, 5), (X, 1, 0, 0), (Y, 1, 0, 0), (STATE, 6), (D, 3, 1, 1),
        (STATE, 7), (FINISH,), (Y, 3, 1, 0), (X, 3, 1, 0), (M, 0, 0, 0), (X, 1, 0, 1), (Y, 1, 0, 1), (M, 0, 0, 1),
        (X, 3, 1, 1), (Y, 3, 1, 1), (D, 3, 2, 0), (M, 0, 1, 0), (ACT, 3), (D, 1, 2, 0), (X, 3, 2, 0), (D, 3, 2, 1),
        (M, 0, 1, 1), (OWN,), (X, 3, 2, 1), (Y, 3, 2, 0), (M, 0, 2, 0), (D, 1, 2, 1), (Y, 3, 2, 1), (M, 0, 2, 1),
        (SERVE, 0), (Y, 0, 0, 0), (X, 0, 0, 0), (DOWN, 3), (D, 1, 0, 0), (SERVE, 1), (Y, 0, 0, 1), (X, 0, 0, 1),
        (D, 1, 0, 1), (SERVE, 2), (X, 0, 1, 0), (Y, 0, 1, 0), (D, 1, 1, 0), (SERVE, 3), (X, 0, 1, 1), (Y, 0, 1, 1),
        (D, 1, 1, 1), (SERVE, 4), (X, 0, 2, 0), (Y, 0, 2, 0), (ACT, 1), (D, 0, 1, 0), (DOWN, 1), (X, 0, 2, 1),
        (Y, 0, 2, 1), (SERVE, 5), (D, 0, 1, 1), (D, 0, 0, 1), (D, 0, 0, 0), (D, 0, 2, 0), (ACT, 0), (D, 0, 2, 1),
        (DOWN, 0),
    ),
    (
        (NATIVE, D, 0, 0, 2), (NATIVE, D, 0, 1, 2), (LOCAL,), (INTRA, 0), (NATIVE, M, 0, 0, 2), (NATIVE, M, 0, 1, 2),
        (NATIVE, M, 1, 0, 2), (NATIVE, M, 1, 1, 2), (NATIVE, M, 2, 0, 2), (NATIVE, M, 2, 1, 2), (INTRA, 1),
        (M, 1, 1, 0), (NATIVE, D, 1, 0, 2), (M, 1, 1, 1), (NATIVE, D, 1, 1, 2), (M, 1, 2, 0), (X, 1, 1, 0),
        (Y, 1, 1, 0), (M, 1, 2, 1), (X, 1, 1, 1), (Y, 1, 1, 1), (M, 1, 0, 0), (X, 1, 2, 0), (Y, 1, 2, 0),
        (M, 1, 0, 1), (X, 1, 2, 1), (D, 1, 1, 0), (STATE, 0), (STATE, 1), (D, 1, 1, 1), (Y, 1, 2, 1), (STATE, 2),
        (NATIVE, D, 2, 0, 2), (NATIVE, D, 2, 1, 2), (STATE, 3), (X, 1, 0, 0), (Y, 1, 0, 0), (STATE, 4), (STATE, 5),
        (X, 1, 0, 1), (D, 1, 2, 0), (STATE, 6), (STATE, 7), (FINISH,), (Y, 1, 0, 1), (D, 1, 2, 1), (COMPACT,),
        (M, 0, 0, 0), (D, 1, 0, 0), (M, 0, 0, 1), (OWN,), (M, 0, 1, 0), (D, 1, 0, 1), (Y, 0, 0, 0), (M, 0, 1, 1),
        (X, 0, 0, 0), (ACT, 1), (DOWN, 1), (Y, 0, 0, 1), (M, 0, 2, 0), (X, 0, 0, 1), (Y, 0, 1, 0), (M, 0, 2, 1),
        (X, 0, 1, 0), (Y, 0, 1, 1), (X, 0, 1, 1), (D, 0, 0, 0), (D, 0, 0, 1), (Y, 0, 2, 0), (X, 0, 2, 0),
        (Y, 0, 2, 1), (X, 0, 2, 1), (D, 0, 1, 0), (D, 0, 1, 1), (D, 0, 2, 0), (ACT, 0), (D, 0, 2, 1), (SERVED,),
        (DOWN, 0),
    ),
)


def fused_kernel(
    n,
    q_hbm,
    k_hbm,
    v_hbm,
    s_hbm,
    attn_gain_hbm,
    moe_gain_hbm,
    ids_hbm,
    gw_hbm,
    wg_hbm,
    wu_hbm,
    wd_hbm,
    out_ref,
    qb,
    kb,
    vb,
    sb,
    attn_gain_ref,
    moe_gain_ref,
    ids,
    gw,
    wg,
    wu,
    wd,
    local,
    prefix,
    passed,
    attended,
    hidden,
    moe_in,
    total,
    active,
    pick,
    rows_out,
    rows_in,
    load_sem,
    send_sem,
    piece_sem,
    sib_sem,
    state_send,
    state_recv,
    row_send,
    row_recv,
):
    g, z, r = lax.axis_index("group"), lax.axis_index("seq"), lax.axis_index("rep")
    x, c = r // 2, r % 2
    r_x, r_s = 2 * (1 - x) + c, 2 * x + (1 - c)
    piece_of = {
        M: g * 4 + r,
        X: g * 4 + r_x,
        Y: (1 - g) * 4 + r,
        D: (1 - g) * 4 + r_x,
    }
    to_x, to_y, to_s = {"rep": r_x}, {"group": 1 - g}, {"rep": r_s}
    rows = qb.shape[0]
    cap = rows_in.shape[0]
    group = cap // ROW_PARTS
    hbm = (wg_hbm, wu_hbm, wd_hbm)
    held = (wg, wu, wd)

    def span(t, piece, half):
        size = held[t].shape[1] // 32
        first, length = ((0, CUT[t]), (CUT[t], 4 - CUT[t]))[half]
        return pl.ds(pl.multiple_of((piece * 4 + first) * size, size), length * size)

    barrier = pltpu.get_barrier_semaphore()
    for to in (to_x, to_y, to_s):
        pl.semaphore_signal(barrier, inc=1, device_id=to, device_id_type=MESH)

    @pl.when(z < n - 1)
    def _():
        pl.semaphore_signal(barrier, inc=1, device_id={"seq": z + 1}, device_id_type=MESH)

    @pl.when(z > 0)
    def _():
        pl.semaphore_signal(barrier, inc=1, device_id={"seq": z - 1}, device_id_type=MESH)

    loads = [
        pltpu.make_async_copy(src, dst, load_sem.at[i])
        for i, (src, dst) in enumerate(
            [
                (k_hbm.at[0], kb),
                (v_hbm.at[0], vb),
                (q_hbm.at[0], qb),
                (s_hbm.at[0], sb),
                (attn_gain_hbm, attn_gain_ref),
                (moe_gain_hbm, moe_gain_ref),
                (ids_hbm.at[0], ids),
                (gw_hbm.at[0], gw),
                (wg_hbm.at[0], wg.at[z]),
                (wu_hbm.at[0], wu.at[z]),
                (wd_hbm.at[0], wd.at[z]),
            ]
        )
    ]
    for load in loads[:4]:
        load.start()
    pl.semaphore_wait(barrier, 3 + (z < n - 1).astype(jnp.int32) + (z > 0).astype(jnp.int32))

    def head(h):
        return pl.ds(h * DH, DH)

    def local_state():
        loads[0].wait()
        loads[1].wait()
        for h in range(H):
            local[h] = lax.dot_general(
                kb[:, head(h)],
                vb[:, head(h)],
                (((0,), (0,)), ((), ())),
                preferred_element_type=jnp.float32,
            )

    def intra(part):
        if part == 0:
            loads[2].wait()
        causal = lax.broadcasted_iota(jnp.int32, (rows, rows), 0) >= lax.broadcasted_iota(
            jnp.int32, (rows, rows), 1
        )
        for h in range(part * H // 2, (part + 1) * H // 2):
            scores = lax.dot_general(
                qb[:, head(h)],
                kb[:, head(h)],
                (((1,), (1,)), ((), ())),
                preferred_element_type=jnp.float32,
            )
            weights = jnp.where(causal, scores, 0.0).astype(jnp.bfloat16)
            attended[:, head(h)] = jnp.dot(
                weights, vb[:, head(h)], preferred_element_type=jnp.float32
            )

    def finish():
        for load in loads[3:8]:
            load.wait()
        square = jnp.zeros((rows, DH), jnp.float32)
        for h in range(H):
            both = attended[:, head(h)] + jnp.dot(
                qb[:, head(h)], prefix[h], preferred_element_type=jnp.float32
            )
            scale = lax.rsqrt(jnp.mean(both * both, axis=-1, keepdims=True) + 1e-06)
            wide = sb[:, head(h)].astype(jnp.float32) + both * scale * attn_gain_ref[:, head(h)]
            rounded = wide.astype(jnp.bfloat16)
            hidden[:, head(h)] = rounded
            wide = rounded.astype(jnp.float32)
            square = square + wide * wide
        scale = lax.rsqrt(jnp.sum(square, axis=-1, keepdims=True) / (H * DH) + 1e-06)
        for h in range(H):
            wide = hidden[:, head(h)].astype(jnp.float32)
            moe_in[:, head(h)] = (wide * scale * moe_gain_ref[:, head(h)]).astype(jnp.bfloat16)

    def activate(inputs, e):
        gate = jnp.dot(inputs, wg[e], preferred_element_type=jnp.float32)
        upper = jnp.dot(inputs, wu[e], preferred_element_type=jnp.float32)
        return (gate / (1.0 + jnp.exp(-gate)) * upper).astype(jnp.bfloat16)

    def down(acts, e):
        return jnp.dot(acts, wd[e], preferred_element_type=jnp.float32).astype(jnp.bfloat16)

    def weigh(made, e):
        chosen = jnp.sum(jnp.where(ids[...] == e, gw[...], 0.0), axis=0, keepdims=True)
        return made.astype(jnp.float32) * jnp.broadcast_to(chosen, (8, rows)).T[:, :1]

    def program(at):
        end = at in (0, n - 1)
        near = 1 if at == 0 else at - 1 if at == n - 1 else n - 1 - at
        outer = None if end else (0 if at < n - 1 - at else n - 1)
        sent = {}

        def push(sem, t, half, copy):
            sent[sem] = sent.get(sem, 0) + (4 - CUT[t] if half else CUT[t])
            copy.start()

        def piece(kind, landed, e, t, half, sem, to, source=None):
            where = span(t, piece_of[kind], half)
            dst = held[t].at[e, where, :]
            return pltpu.make_async_remote_copy(
                src_ref=dst if source is None else source.at[0, where, :],
                dst_ref=dst,
                send_sem=send_sem.at[sem],
                recv_sem=landed,
                device_id=to,
                device_id_type=MESH,
            )

        def landing(kind, e, t, half):
            return piece_sem.at[kind, e, t, half]

        def doubled(e, t):
            return t in DOUBLED[at][0 if e == outer else 1 if e == near else 2]

        def native(kind, t, half, to):
            landed = landing(kind, at, t, half)
            sem = 0 if to > at else 1
            push(sem, t, half, piece(kind, landed, at, t, half, sem, {"seq": to}, hbm[t]))

        def pass_on(kind, e, t, half):
            piece(kind, landing(kind, e, t, half), e, t, half, 0, to_x).wait_recv()
            if kind == M:
                if not end and not (outer == 0 and e == ASKED):
                    to = near if e == outer else outer
                    sem = 0 if to > at else 1
                    push(sem, t, half, piece(M, landing(M, e, t, half), e, t, half, sem, {"seq": to}))
                push(2, t, half, piece(M, landing(X, e, t, half), e, t, half, 2, to_x))
                push(3, t, half, piece(M, landing(Y, e, t, half), e, t, half, 3, to_y))
            if kind == D and not end and e == outer and t in DOUBLED[near][2]:
                sem = 0 if near > at else 1
                push(sem, t, half, piece(D, landing(D, e, t, half), e, t, half, sem, {"seq": near}))
            if kind == X and half == 0 and not doubled(e, t):
                push(3, t, half, piece(X, landing(D, e, t, half), e, t, half, 3, to_y))
            if kind == Y and half == 1 and not doubled(e, t):
                push(2, t, half, piece(Y, landing(D, e, t, half), e, t, half, 2, to_x))
            sem = 4 + kind
            push(sem, t, half, piece(kind, sib_sem.at[e, t], e, t, half, sem, to_s))

        def from_sibling(e, t):
            half = held[t].at[e, pl.ds(0, held[t].shape[1] // 2), :]
            pltpu.make_async_copy(half, half, sib_sem.at[e, t]).wait()

        def state_copy(part):
            heads = pl.ds(part * (H // STATE_PARTS), H // STATE_PARTS)
            return pltpu.make_async_remote_copy(
                src_ref=passed.at[heads],
                dst_ref=prefix.at[heads],
                send_sem=state_send.at[part],
                recv_sem=state_recv.at[part],
                device_id={"seq": at + 1 if at < n - 1 else at - 1},
                device_id_type=MESH,
            )

        def first_state():
            prefix[...] = jnp.zeros_like(prefix)
            passed[...] = local[...].astype(passed.dtype)
            for part in range(STATE_PARTS):
                state_copy(part).start()

        def next_state(part):
            state_copy(part).wait_recv()
            if at < n - 1:
                heads = pl.ds(part * (H // STATE_PARTS), H // STATE_PARTS)
                passed[heads] = (prefix[heads].astype(jnp.float32) + local[heads]).astype(
                    passed.dtype
                )
                state_copy(part).start()

        def row_copy(part):
            some = pl.ds(part * group, group)
            return pltpu.make_async_remote_copy(
                src_ref=rows_out.at[some],
                dst_ref=rows_in.at[some],
                send_sem=row_send.at[part],
                recv_sem=row_recv.at[part],
                device_id={"seq": near if end else outer},
                device_id_type=MESH,
            )

        def compact():
            named = jnp.max((ids[...] == ASKED).astype(jnp.float32), axis=0, keepdims=True)
            earlier = lax.broadcasted_iota(jnp.int32, (rows, rows), 0) < lax.broadcasted_iota(
                jnp.int32, (rows, rows), 1
            )
            place = jnp.dot(
                jnp.broadcast_to(named, (8, rows)).astype(jnp.bfloat16),
                earlier.astype(jnp.bfloat16),
                preferred_element_type=jnp.float32,
            )[:1]
            slots = lax.broadcasted_iota(jnp.int32, (cap, rows), 0).astype(jnp.float32)
            pick[...] = jnp.where(slots == place, named, 0.0).astype(jnp.bfloat16)
            rows_out[...] = jnp.dot(
                pick[...], moe_in[...], preferred_element_type=jnp.float32
            ).astype(jnp.bfloat16)
            for part in range(ROW_PARTS):
                row_copy(part).start()

        def serve(part):
            row_copy(part).wait_recv()
            some = pl.ds(part * group, group)
            rows_out[some] = down(activate(rows_in[some], ASKED), ASKED)
            row_copy(part).start()

        def served():
            for part in range(ROW_PARTS):
                row_copy(part).wait_recv()
            made = lax.dot_general(
                pick[...],
                rows_in[...],
                (((0,), (0,)), ((), ())),
                preferred_element_type=jnp.float32,
            )
            return weigh(made, ASKED)

        def own():
            return weigh(down(activate(moe_in[...], at), at), at)

        def act(e):
            from_sibling(e, 0)
            from_sibling(e, 1)
            active[e] = activate(moe_in[...], e)

        def expert_out(e):
            from_sibling(e, 2)
            return weigh(down(active[e], e), e)

        def settle():
            for sem, count in sent.items():
                some = wg.at[pl.ds(0, 2), pl.ds(0, wg.shape[1] // 64 * count), :]
                pltpu.make_async_copy(some, some, send_sem.at[sem]).wait()
            if at < n - 1:
                for part in range(STATE_PARTS):
                    state_copy(part).wait_send()
            for part in range(ROW_PARTS):
                row_copy(part).wait_send()

        items = PROGRAMS[at]
        started = ready = begun = False
        for index, item in enumerate(items):
            name, *rest = item
            if (name == OWN or name == SERVE and at == ASKED) and not ready:
                ready = True
                for load in loads[8:]:
                    load.wait()
            if name <= D:
                pass_on(name, *rest)
            elif name == NATIVE:
                native(*rest)
            elif name == STATE:
                next_state(*rest)
            elif name == FIRST:
                first_state()
            elif name == LOCAL:
                local_state()
            elif name == INTRA:
                intra(*rest)
            elif name == FINISH:
                finish()
            elif name == COMPACT:
                compact()
            elif name == SERVE:
                serve(*rest)
            elif name == ACT:
                act(*rest)
            else:
                last = index == len(items) - 1
                if last:
                    settle()
                if name == OWN:
                    added = own()
                else:
                    added = served() if name == SERVED else expert_out(*rest)
                if begun:
                    added = total[...] + added
                begun = True
                if last:
                    out_ref[0] = (hidden[...].astype(jnp.float32) + added).astype(out_ref.dtype)
                else:
                    total[...] = added
            if name == LOCAL and not started:
                started = True
                for load in loads[4:]:
                    load.start()

    for at in range(n):

        @pl.when(z == at)
        def _():
            program(at)


def gathered_weights(
    n,
    queries,
    keys,
    values,
    stream,
    attn_gain,
    moe_gain,
    expert_ids,
    gate_weights,
    w_gate,
    w_up,
    w_down,
):
    rows, width = queries.shape[1:]
    units = w_gate.shape[2]
    cap = 3 * rows // n
    half = jnp.bfloat16
    anywhere = pl.BlockSpec(memory_space=pl.ANY)
    vmem = pl.BlockSpec(memory_space=pltpu.VMEM)
    dma = pltpu.SemaphoreType.DMA
    return pl.pallas_call(
        functools.partial(fused_kernel, n),
        out_shape=pltpu.VMEM((1, rows, width), half),
        in_specs=[anywhere] * 11,
        out_specs=vmem,
        scratch_shapes=[
            pltpu.VMEM((rows, width), half),
            pltpu.VMEM((rows, width), half),
            pltpu.VMEM((rows, width), half),
            pltpu.VMEM((rows, width), half),
            pltpu.VMEM((1, width), jnp.float32),
            pltpu.VMEM((1, width), jnp.float32),
            pltpu.VMEM((2, rows), jnp.int32),
            pltpu.VMEM((2, rows), jnp.float32),
            pltpu.VMEM((n, width, units), half),
            pltpu.VMEM((n, width, units), half),
            pltpu.VMEM((n, units, width), half),
            pltpu.VMEM((H, DH, DH), jnp.float32),
            pltpu.VMEM((H, DH, DH), half),
            pltpu.VMEM((H, DH, DH), half),
            pltpu.VMEM((rows, width), jnp.float32),
            pltpu.VMEM((rows, width), half),
            pltpu.VMEM((rows, width), half),
            pltpu.VMEM((rows, width), jnp.float32),
            pltpu.VMEM((n, rows, units), half),
            pltpu.VMEM((cap, rows), half),
            pltpu.VMEM((cap, width), half),
            pltpu.VMEM((cap, width), half),
            dma((11,)),
            dma((8,)),
            dma((4, n, 3, 2)),
            dma((n, 3)),
            dma((STATE_PARTS,)),
            dma((STATE_PARTS,)),
            dma((ROW_PARTS,)),
            dma((ROW_PARTS,)),
        ],
        compiler_params=pltpu.CompilerParams(
            collective_id=0, has_side_effects=True, vmem_limit_bytes=(64 << 20) - (600 << 10)
        ),
    )(
        queries,
        keys,
        values,
        stream,
        attn_gain[None],
        moe_gain[None],
        jnp.swapaxes(expert_ids, 1, 2),
        jnp.swapaxes(gate_weights, 1, 2),
        w_gate,
        w_up,
        w_down,
    )


def prefix_2(value, axis, join, neutral):
    count, mine = (lax.axis_size(axis), lax.axis_index(axis))
    pieces = lax.all_gather(value, axis)
    total = jnp.full_like(value, 0) + jnp.asarray(neutral, value.dtype)

    def lap(position, total):
        longer = join(total, pieces[position])
        return jnp.where(position < mine, longer, total)

    return lax.fori_loop(0, count - 1, lap, total)


def add_states(earlier, later):
    return earlier + later


def per_device(
    queries,
    keys,
    values,
    stream,
    attn_gain,
    moe_gain,
    expert_ids,
    gate_weights,
    w_gate,
    w_up,
    w_down,
):
    row_count = queries.shape[1]
    width = queries.shape[2]
    query_heads = queries[0].reshape(row_count, H, DH)
    key_heads = keys[0].reshape(row_count, H, DH)
    value_heads = values[0].reshape(row_count, H, DH)
    own_state = jnp.einsum(
        "shd,she->hde", key_heads, value_heads, preferred_element_type=jnp.float32
    )
    scores = jnp.einsum("thd,shd->hts", query_heads, key_heads, preferred_element_type=jnp.float32)
    causal = jnp.arange(row_count)[:, None] >= jnp.arange(row_count)[None, :]
    weights = jnp.where(causal[None], scores, jnp.zeros((), jnp.float32)).astype(jnp.bfloat16)
    intra = jnp.einsum("hts,shd->thd", weights, value_heads, preferred_element_type=jnp.float32)
    prefix = prefix_2(own_state, "seq", add_states, jnp.zeros_like(own_state))
    inter = jnp.einsum(
        "thd,hde->the", query_heads, prefix.astype(jnp.bfloat16), preferred_element_type=jnp.float32
    )
    attended = intra + inter
    normed = attended * lax.rsqrt(jnp.mean(attended * attended, axis=-1, keepdims=True) + 1e-06)
    hidden = (stream[0].astype(jnp.float32) + normed.reshape(row_count, width) * attn_gain).astype(
        jnp.bfloat16
    )
    hidden_wide = hidden.astype(jnp.float32)
    moe_in = (
        hidden_wide
        * lax.rsqrt(jnp.mean(hidden_wide * hidden_wide, axis=-1, keepdims=True) + 1e-06)
        * moe_gain
    ).astype(jnp.bfloat16)
    dest_count = lax.axis_size("seq")
    capacity = 3 * row_count // dest_count
    choice_ids = expert_ids[0].reshape(-1)
    place = jnp.arange(2 * row_count, dtype=jnp.int32)
    earlier = (choice_ids[:, None] == choice_ids[None, :]) & (place[:, None] > place[None, :])
    slot_rank = jnp.sum(earlier.astype(jnp.int32), axis=1)
    slot_index = choice_ids * capacity + slot_rank
    token_index = jnp.arange(2 * row_count, dtype=jnp.int32) // 2
    outgoing = (
        jnp.zeros((dest_count * capacity, width), jnp.bfloat16)
        .at[slot_index]
        .set(moe_in[token_index])
    )
    outgoing = outgoing.reshape(dest_count, capacity, width)
    received = lax.all_to_all(outgoing, "seq", split_axis=0, concat_axis=0, tiled=True)
    flat_rows = received.reshape(-1, width)
    gate = jnp.dot(flat_rows, w_gate[0], preferred_element_type=jnp.float32)
    upper = jnp.dot(flat_rows, w_up[0], preferred_element_type=jnp.float32)
    active = (jax.nn.silu(gate) * upper).astype(jnp.bfloat16)
    produced = jnp.dot(active, w_down[0], preferred_element_type=jnp.float32).astype(jnp.bfloat16)
    returned = lax.all_to_all(
        produced.reshape(received.shape), "seq", split_axis=0, concat_axis=0, tiled=True
    )
    picked = returned.reshape(-1, width)[slot_index].astype(jnp.float32)
    weighted = (gate_weights[0].reshape(-1)[:, None] * picked).reshape(row_count, 2, width)
    mixed = hidden_wide + (weighted[:, 0] + weighted[:, 1])
    return mixed.astype(jnp.bfloat16)[None]


def solution(mesh):
    placed = (
        P(("group", "rep"), "seq", None),
        P(("group", "rep"), "seq", None),
        P(("group", "rep"), "seq", None),
        P(("group", "rep"), "seq", None),
        P(),
        P(),
        P(("group", "rep"), "seq", None),
        P(("group", "rep"), "seq", None),
        P("seq", None, None),
        P("seq", None, None),
        P("seq", None, None),
    )
    ways = dict(mesh.shape)

    def plan(*args):
        n = ways["seq"]
        held = n * sum(w.size // w.shape[0] * w.dtype.itemsize for w in args[-3:])
        whole = args[-1].shape[1] % 512 == 0 and 3 * args[0].shape[1] // n % (16 * ROW_PARTS) == 0
        if ways["group"] == 2 and ways["rep"] == 4 and n == len(PROGRAMS) and whole and held <= GATHER_LIMIT:
            return gathered_weights(n, *args)
        return per_device(*args)

    return jax.shard_map(
        plan,
        mesh=mesh,
        in_specs=placed,
        out_specs=P(("group", "rep"), "seq", None),
        check_vma=False,
    )
```

```python
import functools

import jax
import jax.numpy as jnp
from jax import lax
from jax.experimental import pallas as pl
from jax.experimental.pallas import tpu as pltpu
from jax.sharding import PartitionSpec as P

H = 8
DH = 128
MESH = pl.DeviceIdType.MESH
GATHER_LIMIT = 24 << 20


ASKED = 2
ROW_PARTS = 6
STATE_PARTS = 8
DOUBLED = ((0, 1, 2), (1,), (1, 2), (2,))
M, X, Y, D, NATIVE, STATE, FIRST, LOCAL, INTRA, FINISH, COMPACT, OWN, ACT, DOWN, SERVE, SERVED = range(16)
PROGRAMS = (
    (
        (LOCAL,), (FIRST,), (NATIVE, M, 0, 0, 1), (NATIVE, M, 0, 1, 1), (NATIVE, M, 1, 0, 1), (NATIVE, M, 1, 1, 1),
        (NATIVE, M, 2, 0, 1), (NATIVE, M, 2, 1, 1), (INTRA, 0), (INTRA, 1), (FINISH,), (COMPACT,), (M, 1, 0, 0),
        (OWN,), (M, 1, 0, 1), (M, 1, 1, 0), (X, 1, 0, 0), (Y, 1, 0, 0), (M, 1, 1, 1), (X, 1, 0, 1), (Y, 1, 0, 1),
        (D, 1, 2, 0), (X, 1, 1, 0), (Y, 1, 1, 0), (D, 1, 2, 1), (X, 1, 1, 1), (D, 1, 0, 0), (M, 1, 2, 0),
        (D, 1, 0, 1), (Y, 1, 1, 1), (M, 1, 2, 1), (D, 1, 1, 0), (M, 3, 0, 0), (X, 1, 2, 0), (Y, 1, 2, 0),
        (D, 1, 1, 1), (Y, 1, 2, 1), (M, 3, 0, 1), (ACT, 1), (X, 1, 2, 1), (Y, 3, 0, 0), (NATIVE, D, 1, 0, 1),
        (M, 3, 1, 0), (X, 3, 0, 0), (DOWN, 1), (NATIVE, D, 1, 1, 1), (M, 3, 1, 1), (Y, 3, 0, 1), (X, 3, 0, 1),
        (NATIVE, D, 2, 0, 1), (Y, 3, 1, 0), (X, 3, 1, 0), (NATIVE, D, 2, 1, 1), (D, 3, 0, 0), (X, 3, 1, 1),
        (M, 3, 2, 0), (NATIVE, D, 0, 0, 1), (Y, 3, 1, 1), (D, 3, 0, 1), (M, 3, 2, 1), (NATIVE, D, 0, 1, 1),
        (D, 3, 1, 0), (X, 3, 2, 0), (Y, 3, 2, 0), (D, 3, 1, 1), (Y, 3, 2, 1), (ACT, 3), (X, 3, 2, 1), (D, 3, 2, 0),
        (D, 3, 2, 1), (DOWN, 3), (SERVED,),
    ),
    (
        (NATIVE, M, 0, 0, 2), (NATIVE, M, 0, 1, 2), (NATIVE, M, 1, 0, 2), (NATIVE, M, 1, 1, 2), (NATIVE, M, 0, 0, 0),
        (NATIVE, M, 0, 1, 0), (NATIVE, M, 1, 0, 0), (NATIVE, M, 1, 1, 0), (LOCAL,), (INTRA, 0), (NATIVE, M, 2, 0, 2),
        (INTRA, 1), (NATIVE, D, 2, 0, 0), (NATIVE, M, 2, 1, 2), (NATIVE, D, 2, 1, 0), (STATE, 0), (M, 2, 0, 0),
        (STATE, 1), (NATIVE, M, 2, 0, 0), (STATE, 2), (M, 2, 0, 1), (STATE, 3), (NATIVE, M, 2, 1, 0), (STATE, 4),
        (M, 2, 2, 0), (STATE, 5), (X, 2, 0, 0), (Y, 2, 0, 0), (STATE, 6), (M, 2, 2, 1), (STATE, 7), (X, 2, 0, 1),
        (Y, 2, 0, 1), (FINISH,), (M, 2, 1, 0), (M, 0, 0, 0), (X, 2, 2, 0), (Y, 2, 2, 0), (M, 2, 1, 1), (M, 0, 0, 1),
        (X, 2, 2, 1), (D, 2, 0, 0), (M, 3, 0, 0), (OWN,), (D, 2, 0, 1), (Y, 2, 2, 1), (M, 0, 1, 0), (X, 2, 1, 0),
        (Y, 2, 1, 0), (M, 3, 0, 1), (M, 0, 1, 1), (M, 3, 1, 0), (M, 0, 2, 0), (Y, 0, 0, 0), (X, 0, 0, 0),
        (M, 3, 1, 1), (M, 0, 2, 1), (X, 2, 1, 1), (D, 2, 2, 0), (D, 2, 1, 0), (X, 0, 0, 1), (Y, 2, 1, 1),
        (NATIVE, D, 1, 0, 2), (D, 2, 1, 1), (X, 3, 0, 0), (Y, 0, 0, 1), (NATIVE, D, 1, 1, 2), (ACT, 2), (M, 3, 2, 0),
        (Y, 3, 0, 0), (D, 2, 2, 1), (M, 3, 2, 1), (X, 0, 1, 0), (Y, 0, 1, 0), (DOWN, 2), (SERVE, 0), (X, 3, 0, 1),
        (Y, 3, 0, 1), (D, 3, 1, 0), (SERVE, 1), (D, 3, 1, 1), (SERVE, 2), (X, 0, 1, 1), (Y, 0, 1, 1), (SERVE, 3),
        (D, 0, 1, 0), (X, 3, 1, 0), (Y, 3, 1, 0), (D, 3, 2, 0), (SERVE, 4), (D, 3, 2, 1), (SERVE, 5), (Y, 0, 2, 0),
        (D, 0, 1, 1), (X, 0, 2, 0), (D, 0, 2, 0), (X, 3, 1, 1), (Y, 3, 1, 1), (D, 0, 2, 1), (X, 0, 2, 1),
        (Y, 0, 2, 1), (D, 0, 0, 0), (X, 3, 2, 0), (D, 3, 0, 0), (D, 0, 0, 1), (X, 3, 2, 1), (Y, 3, 2, 0), (ACT, 0),
        (D, 3, 0, 1), (Y, 3, 2, 1), (DOWN, 0), (ACT, 3), (DOWN, 3),
    ),
    (
        (NATIVE, M, 0, 0, 1), (NATIVE, M, 0, 1, 1), (NATIVE, M, 2, 0, 1), (NATIVE, M, 2, 1, 1), (LOCAL,), (INTRA, 0),
        (INTRA, 1), (NATIVE, M, 1, 0, 1), (NATIVE, M, 1, 1, 1), (M, 1, 0, 0), (D, 3, 0, 0), (M, 1, 0, 1),
        (D, 3, 0, 1), (M, 1, 1, 0), (M, 3, 0, 0), (X, 1, 0, 0), (Y, 1, 0, 0), (M, 1, 1, 1), (M, 3, 0, 1),
        (X, 1, 0, 1), (Y, 1, 0, 1), (M, 3, 1, 0), (M, 1, 2, 0), (X, 1, 1, 0), (Y, 1, 1, 0), (M, 3, 1, 1),
        (M, 1, 2, 1), (X, 3, 0, 0), (Y, 3, 0, 0), (NATIVE, D, 1, 0, 1), (STATE, 0), (NATIVE, D, 1, 1, 1),
        (M, 3, 2, 0), (STATE, 1), (X, 1, 1, 1), (D, 1, 0, 0), (STATE, 2), (M, 3, 2, 1), (STATE, 3), (X, 3, 0, 1),
        (Y, 1, 1, 1), (STATE, 4), (D, 3, 1, 0), (STATE, 5), (D, 1, 0, 1), (Y, 3, 0, 1), (STATE, 6), (D, 3, 1, 1),
        (STATE, 7), (FINISH,), (X, 3, 1, 0), (Y, 3, 1, 0), (D, 3, 2, 0), (M, 0, 0, 0), (X, 1, 2, 0), (Y, 1, 2, 0),
        (D, 3, 2, 1), (M, 0, 0, 1), (X, 3, 1, 1), (Y, 3, 1, 1), (M, 0, 1, 0), (ACT, 3), (X, 1, 2, 1), (Y, 1, 2, 1),
        (M, 0, 1, 1), (X, 3, 2, 0), (Y, 3, 2, 0), (M, 0, 2, 0), (X, 3, 2, 1), (Y, 3, 2, 1), (M, 0, 2, 1), (SERVE, 0),
        (Y, 0, 0, 0), (X, 0, 0, 0), (DOWN, 3), (D, 1, 1, 0), (OWN,), (X, 0, 0, 1), (D, 1, 2, 0), (D, 1, 1, 1),
        (SERVE, 1), (Y, 0, 0, 1), (X, 0, 1, 0), (SERVE, 2), (D, 1, 2, 1), (Y, 0, 1, 0), (SERVE, 3), (D, 0, 1, 0),
        (ACT, 1), (Y, 0, 1, 1), (X, 0, 1, 1), (SERVE, 4), (D, 0, 1, 1), (X, 0, 2, 0), (Y, 0, 2, 0), (DOWN, 1),
        (SERVE, 5), (D, 0, 2, 0), (X, 0, 2, 1), (Y, 0, 2, 1), (D, 0, 2, 1), (D, 0, 0, 1), (D, 0, 0, 0), (ACT, 0),
        (DOWN, 0),
    ),
    (
        (NATIVE, D, 0, 0, 2), (NATIVE, D, 0, 1, 2), (NATIVE, M, 0, 0, 2), (NATIVE, M, 0, 1, 2), (LOCAL,), (INTRA, 0),
        (NATIVE, M, 1, 0, 2), (NATIVE, M, 1, 1, 2), (NATIVE, M, 2, 0, 2), (NATIVE, M, 2, 1, 2), (INTRA, 1),
        (M, 1, 0, 0), (NATIVE, D, 1, 0, 2), (M, 1, 0, 1), (NATIVE, D, 1, 1, 2), (M, 1, 1, 0), (NATIVE, D, 2, 0, 2),
        (X, 1, 0, 0), (Y, 1, 0, 0), (M, 1, 1, 1), (NATIVE, D, 2, 1, 2), (X, 1, 0, 1), (Y, 1, 0, 1), (M, 1, 2, 0),
        (X, 1, 1, 0), (Y, 1, 1, 0), (M, 1, 2, 1), (X, 1, 1, 1), (D, 1, 0, 0), (STATE, 0), (STATE, 1), (D, 1, 0, 1),
        (Y, 1, 1, 1), (STATE, 2), (STATE, 3), (X, 1, 2, 0), (Y, 1, 2, 0), (STATE, 4), (STATE, 5), (X, 1, 2, 1),
        (D, 1, 1, 0), (STATE, 6), (STATE, 7), (FINISH,), (D, 1, 1, 1), (Y, 1, 2, 1), (COMPACT,), (M, 0, 0, 0),
        (D, 1, 2, 0), (M, 0, 0, 1), (M, 0, 1, 0), (D, 1, 2, 1), (Y, 0, 0, 0), (M, 0, 1, 1), (X, 0, 0, 0),
        (Y, 0, 0, 1), (M, 0, 2, 0), (X, 0, 0, 1), (Y, 0, 1, 0), (M, 0, 2, 1), (X, 0, 1, 0), (Y, 0, 1, 1),
        (X, 0, 1, 1), (ACT, 1), (OWN,), (DOWN, 1), (D, 0, 0, 0), (D, 0, 0, 1), (Y, 0, 2, 0), (X, 0, 2, 0),
        (Y, 0, 2, 1), (X, 0, 2, 1), (D, 0, 1, 0), (D, 0, 1, 1), (D, 0, 2, 0), (ACT, 0), (D, 0, 2, 1), (SERVED,),
        (DOWN, 0),
    ),
)


def fused_kernel(
    n,
    q_hbm,
    k_hbm,
    v_hbm,
    s_hbm,
    attn_gain_hbm,
    moe_gain_hbm,
    ids_hbm,
    gw_hbm,
    wg_hbm,
    wu_hbm,
    wd_hbm,
    out_ref,
    qb,
    kb,
    vb,
    sb,
    attn_gain_ref,
    moe_gain_ref,
    ids,
    gw,
    wg,
    wu,
    wd,
    local,
    prefix,
    passed,
    attended,
    hidden,
    moe_in,
    total,
    active,
    pick,
    rows_out,
    rows_in,
    load_sem,
    send_sem,
    piece_sem,
    sib_sem,
    state_send,
    state_recv,
    row_send,
    row_recv,
):
    g, z, r = lax.axis_index("group"), lax.axis_index("seq"), lax.axis_index("rep")
    x, c = r // 2, r % 2
    r_x, r_s = 2 * (1 - x) + c, 2 * x + (1 - c)
    piece_of = {
        M: g * 4 + r,
        X: g * 4 + r_x,
        Y: (1 - g) * 4 + r,
        D: (1 - g) * 4 + r_x,
    }
    to_x, to_y, to_s = {"rep": r_x}, {"group": 1 - g}, {"rep": r_s}
    rows = qb.shape[0]
    cap = rows_in.shape[0]
    group = cap // ROW_PARTS
    hbm = (wg_hbm, wu_hbm, wd_hbm)
    held = (wg, wu, wd)

    def span(t, piece, half):
        size = held[t].shape[1] // 16
        return pl.ds(pl.multiple_of(piece * 2 * size + half * size, size), size)

    barrier = pltpu.get_barrier_semaphore()
    for to in (to_x, to_y, to_s):
        pl.semaphore_signal(barrier, inc=1, device_id=to, device_id_type=MESH)

    @pl.when(z < n - 1)
    def _():
        pl.semaphore_signal(barrier, inc=1, device_id={"seq": z + 1}, device_id_type=MESH)

    @pl.when(z > 0)
    def _():
        pl.semaphore_signal(barrier, inc=1, device_id={"seq": z - 1}, device_id_type=MESH)

    loads = [
        pltpu.make_async_copy(src, dst, load_sem.at[i])
        for i, (src, dst) in enumerate(
            [
                (k_hbm.at[0], kb),
                (v_hbm.at[0], vb),
                (q_hbm.at[0], qb),
                (s_hbm.at[0], sb),
                (attn_gain_hbm, attn_gain_ref),
                (moe_gain_hbm, moe_gain_ref),
                (ids_hbm.at[0], ids),
                (gw_hbm.at[0], gw),
                (wg_hbm.at[0], wg.at[z]),
                (wu_hbm.at[0], wu.at[z]),
                (wd_hbm.at[0], wd.at[z]),
            ]
        )
    ]
    for load in loads[:4]:
        load.start()
    pl.semaphore_wait(barrier, 3 + (z < n - 1).astype(jnp.int32) + (z > 0).astype(jnp.int32))

    def head(h):
        return pl.ds(h * DH, DH)

    def local_state():
        loads[0].wait()
        loads[1].wait()
        for h in range(H):
            local[h] = lax.dot_general(
                kb[:, head(h)],
                vb[:, head(h)],
                (((0,), (0,)), ((), ())),
                preferred_element_type=jnp.float32,
            )

    def intra(part):
        if part == 0:
            loads[2].wait()
        causal = lax.broadcasted_iota(jnp.int32, (rows, rows), 0) >= lax.broadcasted_iota(
            jnp.int32, (rows, rows), 1
        )
        for h in range(part * H // 2, (part + 1) * H // 2):
            scores = lax.dot_general(
                qb[:, head(h)],
                kb[:, head(h)],
                (((1,), (1,)), ((), ())),
                preferred_element_type=jnp.float32,
            )
            weights = jnp.where(causal, scores, 0.0).astype(jnp.bfloat16)
            attended[:, head(h)] = jnp.dot(
                weights, vb[:, head(h)], preferred_element_type=jnp.float32
            )

    def finish():
        for load in loads[3:8]:
            load.wait()
        square = jnp.zeros((rows, DH), jnp.float32)
        for h in range(H):
            both = attended[:, head(h)] + jnp.dot(
                qb[:, head(h)], prefix[h], preferred_element_type=jnp.float32
            )
            scale = lax.rsqrt(jnp.mean(both * both, axis=-1, keepdims=True) + 1e-06)
            wide = sb[:, head(h)].astype(jnp.float32) + both * scale * attn_gain_ref[:, head(h)]
            rounded = wide.astype(jnp.bfloat16)
            hidden[:, head(h)] = rounded
            wide = rounded.astype(jnp.float32)
            square = square + wide * wide
        scale = lax.rsqrt(jnp.sum(square, axis=-1, keepdims=True) / (H * DH) + 1e-06)
        for h in range(H):
            wide = hidden[:, head(h)].astype(jnp.float32)
            moe_in[:, head(h)] = (wide * scale * moe_gain_ref[:, head(h)]).astype(jnp.bfloat16)

    def activate(inputs, e):
        gate = jnp.dot(inputs, wg[e], preferred_element_type=jnp.float32)
        upper = jnp.dot(inputs, wu[e], preferred_element_type=jnp.float32)
        return (gate / (1.0 + jnp.exp(-gate)) * upper).astype(jnp.bfloat16)

    def down(acts, e):
        return jnp.dot(acts, wd[e], preferred_element_type=jnp.float32).astype(jnp.bfloat16)

    def weigh(made, e):
        chosen = jnp.sum(jnp.where(ids[...] == e, gw[...], 0.0), axis=0, keepdims=True)
        return made.astype(jnp.float32) * jnp.broadcast_to(chosen, (8, rows)).T[:, :1]

    def program(at):
        end = at in (0, n - 1)
        near = 1 if at == 0 else at - 1 if at == n - 1 else n - 1 - at
        outer = None if end else (0 if at < n - 1 - at else n - 1)
        sent = {}

        def push(sem, copy):
            sent[sem] = sent.get(sem, 0) + 1
            copy.start()

        def piece(kind, landed, e, t, half, sem, to, source=None):
            where = span(t, piece_of[kind], half)
            dst = held[t].at[e, where, :]
            return pltpu.make_async_remote_copy(
                src_ref=dst if source is None else source.at[0, where, :],
                dst_ref=dst,
                send_sem=send_sem.at[sem],
                recv_sem=landed,
                device_id=to,
                device_id_type=MESH,
            )

        def landing(kind, e, t, half):
            return piece_sem.at[kind, e, t, half]

        def doubled(e, t):
            if end:
                return at == 0 and e == near and t in DOUBLED[3]
            return t in DOUBLED[0 if e == outer else 1 if e == near else 2]

        def native(kind, t, half, to):
            landed = landing(kind, at, t, half)
            sem = 0 if to > at else 1
            push(sem, piece(kind, landed, at, t, half, sem, {"seq": to}, hbm[t]))

        def pass_on(kind, e, t, half):
            piece(kind, landing(kind, e, t, half), e, t, half, 0, to_x).wait_recv()
            if kind == M:
                if not end and not (outer == 0 and e == ASKED):
                    to = near if e == outer else outer
                    sem = 0 if to > at else 1
                    push(sem, piece(M, landing(M, e, t, half), e, t, half, sem, {"seq": to}))
                push(2, piece(M, landing(X, e, t, half), e, t, half, 2, to_x))
                push(3, piece(M, landing(Y, e, t, half), e, t, half, 3, to_y))
            if kind == D and not end and e == outer and t in DOUBLED[2]:
                sem = 0 if near > at else 1
                push(sem, piece(D, landing(D, e, t, half), e, t, half, sem, {"seq": near}))
            if kind == X and half == 0 and not doubled(e, t):
                push(3, piece(X, landing(D, e, t, half), e, t, half, 3, to_y))
            if kind == Y and half == 1 and not doubled(e, t):
                push(2, piece(Y, landing(D, e, t, half), e, t, half, 2, to_x))
            sem = 4 + kind
            push(sem, piece(kind, sib_sem.at[e, t], e, t, half, sem, to_s))

        def from_sibling(e, t):
            half = held[t].at[e, pl.ds(0, held[t].shape[1] // 2), :]
            pltpu.make_async_copy(half, half, sib_sem.at[e, t]).wait()

        def state_copy(part):
            heads = pl.ds(part * (H // STATE_PARTS), H // STATE_PARTS)
            return pltpu.make_async_remote_copy(
                src_ref=passed.at[heads],
                dst_ref=prefix.at[heads],
                send_sem=state_send.at[part],
                recv_sem=state_recv.at[part],
                device_id={"seq": at + 1 if at < n - 1 else at - 1},
                device_id_type=MESH,
            )

        def first_state():
            prefix[...] = jnp.zeros_like(prefix)
            passed[...] = local[...].astype(passed.dtype)
            for part in range(STATE_PARTS):
                state_copy(part).start()

        def next_state(part):
            state_copy(part).wait_recv()
            if at < n - 1:
                heads = pl.ds(part * (H // STATE_PARTS), H // STATE_PARTS)
                passed[heads] = (prefix[heads].astype(jnp.float32) + local[heads]).astype(
                    passed.dtype
                )
                state_copy(part).start()

        def row_copy(part):
            some = pl.ds(part * group, group)
            return pltpu.make_async_remote_copy(
                src_ref=rows_out.at[some],
                dst_ref=rows_in.at[some],
                send_sem=row_send.at[part],
                recv_sem=row_recv.at[part],
                device_id={"seq": near if end else outer},
                device_id_type=MESH,
            )

        def compact():
            named = jnp.max((ids[...] == ASKED).astype(jnp.float32), axis=0, keepdims=True)
            earlier = lax.broadcasted_iota(jnp.int32, (rows, rows), 0) < lax.broadcasted_iota(
                jnp.int32, (rows, rows), 1
            )
            place = jnp.dot(
                jnp.broadcast_to(named, (8, rows)).astype(jnp.bfloat16),
                earlier.astype(jnp.bfloat16),
                preferred_element_type=jnp.float32,
            )[:1]
            slots = lax.broadcasted_iota(jnp.int32, (cap, rows), 0).astype(jnp.float32)
            pick[...] = jnp.where(slots == place, named, 0.0).astype(jnp.bfloat16)
            rows_out[...] = jnp.dot(
                pick[...], moe_in[...], preferred_element_type=jnp.float32
            ).astype(jnp.bfloat16)
            for part in range(ROW_PARTS):
                row_copy(part).start()

        def serve(part):
            row_copy(part).wait_recv()
            some = pl.ds(part * group, group)
            rows_out[some] = down(activate(rows_in[some], ASKED), ASKED)
            row_copy(part).start()

        def served():
            for part in range(ROW_PARTS):
                row_copy(part).wait_recv()
            made = lax.dot_general(
                pick[...],
                rows_in[...],
                (((0,), (0,)), ((), ())),
                preferred_element_type=jnp.float32,
            )
            return weigh(made, ASKED)

        def own():
            return weigh(down(activate(moe_in[...], at), at), at)

        def act(e):
            from_sibling(e, 0)
            from_sibling(e, 1)
            active[e] = activate(moe_in[...], e)

        def expert_out(e):
            from_sibling(e, 2)
            return weigh(down(active[e], e), e)

        def settle():
            for sem, count in sent.items():
                some = wg.at[:, pl.ds(0, wg.shape[1] // 64 * count), :]
                pltpu.make_async_copy(some, some, send_sem.at[sem]).wait()
            if at < n - 1:
                for part in range(STATE_PARTS):
                    state_copy(part).wait_send()
            for part in range(ROW_PARTS):
                row_copy(part).wait_send()

        items = PROGRAMS[at]
        started = ready = begun = False
        for index, item in enumerate(items):
            name, *rest = item
            if (name == OWN or name == SERVE and at == ASKED) and not ready:
                ready = True
                for load in loads[8:]:
                    load.wait()
            if name <= D:
                pass_on(name, *rest)
            elif name == NATIVE:
                native(*rest)
            elif name == STATE:
                next_state(*rest)
            elif name == FIRST:
                first_state()
            elif name == LOCAL:
                local_state()
            elif name == INTRA:
                intra(*rest)
            elif name == FINISH:
                finish()
            elif name == COMPACT:
                compact()
            elif name == SERVE:
                serve(*rest)
            elif name == ACT:
                act(*rest)
            else:
                last = index == len(items) - 1
                if last:
                    settle()
                if name == OWN:
                    added = own()
                else:
                    added = served() if name == SERVED else expert_out(*rest)
                if begun:
                    added = total[...] + added
                begun = True
                if last:
                    out_ref[0] = (hidden[...].astype(jnp.float32) + added).astype(out_ref.dtype)
                else:
                    total[...] = added
            if name == LOCAL and not started:
                started = True
                for load in loads[4:]:
                    load.start()

    for at in range(n):

        @pl.when(z == at)
        def _():
            program(at)


def gathered_weights(
    n,
    queries,
    keys,
    values,
    stream,
    attn_gain,
    moe_gain,
    expert_ids,
    gate_weights,
    w_gate,
    w_up,
    w_down,
):
    rows, width = queries.shape[1:]
    units = w_gate.shape[2]
    cap = 3 * rows // n
    half = jnp.bfloat16
    anywhere = pl.BlockSpec(memory_space=pl.ANY)
    vmem = pl.BlockSpec(memory_space=pltpu.VMEM)
    dma = pltpu.SemaphoreType.DMA
    return pl.pallas_call(
        functools.partial(fused_kernel, n),
        out_shape=pltpu.VMEM((1, rows, width), half),
        in_specs=[anywhere] * 11,
        out_specs=vmem,
        scratch_shapes=[
            pltpu.VMEM((rows, width), half),
            pltpu.VMEM((rows, width), half),
            pltpu.VMEM((rows, width), half),
            pltpu.VMEM((rows, width), half),
            pltpu.VMEM((1, width), jnp.float32),
            pltpu.VMEM((1, width), jnp.float32),
            pltpu.VMEM((2, rows), jnp.int32),
            pltpu.VMEM((2, rows), jnp.float32),
            pltpu.VMEM((n, width, units), half),
            pltpu.VMEM((n, width, units), half),
            pltpu.VMEM((n, units, width), half),
            pltpu.VMEM((H, DH, DH), jnp.float32),
            pltpu.VMEM((H, DH, DH), half),
            pltpu.VMEM((H, DH, DH), half),
            pltpu.VMEM((rows, width), jnp.float32),
            pltpu.VMEM((rows, width), half),
            pltpu.VMEM((rows, width), half),
            pltpu.VMEM((rows, width), jnp.float32),
            pltpu.VMEM((n, rows, units), half),
            pltpu.VMEM((cap, rows), half),
            pltpu.VMEM((cap, width), half),
            pltpu.VMEM((cap, width), half),
            dma((11,)),
            dma((8,)),
            dma((4, n, 3, 2)),
            dma((n, 3)),
            dma((STATE_PARTS,)),
            dma((STATE_PARTS,)),
            dma((ROW_PARTS,)),
            dma((ROW_PARTS,)),
        ],
        compiler_params=pltpu.CompilerParams(
            collective_id=0, has_side_effects=True, vmem_limit_bytes=(64 << 20) - (600 << 10)
        ),
    )(
        queries,
        keys,
        values,
        stream,
        attn_gain[None],
        moe_gain[None],
        jnp.swapaxes(expert_ids, 1, 2),
        jnp.swapaxes(gate_weights, 1, 2),
        w_gate,
        w_up,
        w_down,
    )


def prefix_2(value, axis, join, neutral):
    count, mine = (lax.axis_size(axis), lax.axis_index(axis))
    pieces = lax.all_gather(value, axis)
    total = jnp.full_like(value, 0) + jnp.asarray(neutral, value.dtype)

    def lap(position, total):
        longer = join(total, pieces[position])
        return jnp.where(position < mine, longer, total)

    return lax.fori_loop(0, count - 1, lap, total)


def add_states(earlier, later):
    return earlier + later


def per_device(
    queries,
    keys,
    values,
    stream,
    attn_gain,
    moe_gain,
    expert_ids,
    gate_weights,
    w_gate,
    w_up,
    w_down,
):
    row_count = queries.shape[1]
    width = queries.shape[2]
    query_heads = queries[0].reshape(row_count, H, DH)
    key_heads = keys[0].reshape(row_count, H, DH)
    value_heads = values[0].reshape(row_count, H, DH)
    own_state = jnp.einsum(
        "shd,she->hde", key_heads, value_heads, preferred_element_type=jnp.float32
    )
    scores = jnp.einsum("thd,shd->hts", query_heads, key_heads, preferred_element_type=jnp.float32)
    causal = jnp.arange(row_count)[:, None] >= jnp.arange(row_count)[None, :]
    weights = jnp.where(causal[None], scores, jnp.zeros((), jnp.float32)).astype(jnp.bfloat16)
    intra = jnp.einsum("hts,shd->thd", weights, value_heads, preferred_element_type=jnp.float32)
    prefix = prefix_2(own_state, "seq", add_states, jnp.zeros_like(own_state))
    inter = jnp.einsum(
        "thd,hde->the", query_heads, prefix.astype(jnp.bfloat16), preferred_element_type=jnp.float32
    )
    attended = intra + inter
    normed = attended * lax.rsqrt(jnp.mean(attended * attended, axis=-1, keepdims=True) + 1e-06)
    hidden = (stream[0].astype(jnp.float32) + normed.reshape(row_count, width) * attn_gain).astype(
        jnp.bfloat16
    )
    hidden_wide = hidden.astype(jnp.float32)
    moe_in = (
        hidden_wide
        * lax.rsqrt(jnp.mean(hidden_wide * hidden_wide, axis=-1, keepdims=True) + 1e-06)
        * moe_gain
    ).astype(jnp.bfloat16)
    dest_count = lax.axis_size("seq")
    capacity = 3 * row_count // dest_count
    choice_ids = expert_ids[0].reshape(-1)
    place = jnp.arange(2 * row_count, dtype=jnp.int32)
    earlier = (choice_ids[:, None] == choice_ids[None, :]) & (place[:, None] > place[None, :])
    slot_rank = jnp.sum(earlier.astype(jnp.int32), axis=1)
    slot_index = choice_ids * capacity + slot_rank
    token_index = jnp.arange(2 * row_count, dtype=jnp.int32) // 2
    outgoing = (
        jnp.zeros((dest_count * capacity, width), jnp.bfloat16)
        .at[slot_index]
        .set(moe_in[token_index])
    )
    outgoing = outgoing.reshape(dest_count, capacity, width)
    received = lax.all_to_all(outgoing, "seq", split_axis=0, concat_axis=0, tiled=True)
    flat_rows = received.reshape(-1, width)
    gate = jnp.dot(flat_rows, w_gate[0], preferred_element_type=jnp.float32)
    upper = jnp.dot(flat_rows, w_up[0], preferred_element_type=jnp.float32)
    active = (jax.nn.silu(gate) * upper).astype(jnp.bfloat16)
    produced = jnp.dot(active, w_down[0], preferred_element_type=jnp.float32).astype(jnp.bfloat16)
    returned = lax.all_to_all(
        produced.reshape(received.shape), "seq", split_axis=0, concat_axis=0, tiled=True
    )
    picked = returned.reshape(-1, width)[slot_index].astype(jnp.float32)
    weighted = (gate_weights[0].reshape(-1)[:, None] * picked).reshape(row_count, 2, width)
    mixed = hidden_wide + (weighted[:, 0] + weighted[:, 1])
    return mixed.astype(jnp.bfloat16)[None]


def solution(mesh):
    placed = (
        P(("group", "rep"), "seq", None),
        P(("group", "rep"), "seq", None),
        P(("group", "rep"), "seq", None),
        P(("group", "rep"), "seq", None),
        P(),
        P(),
        P(("group", "rep"), "seq", None),
        P(("group", "rep"), "seq", None),
        P("seq", None, None),
        P("seq", None, None),
        P("seq", None, None),
    )
    ways = dict(mesh.shape)

    def plan(*args):
        n = ways["seq"]
        held = n * sum(w.size // w.shape[0] * w.dtype.itemsize for w in args[-3:])
        whole = args[-1].shape[1] % 256 == 0 and 3 * args[0].shape[1] // n % (16 * ROW_PARTS) == 0
        if ways["group"] == 2 and ways["rep"] == 4 and n == len(PROGRAMS) and whole and held <= GATHER_LIMIT:
            return gathered_weights(n, *args)
        return per_device(*args)

    return jax.shard_map(
        plan,
        mesh=mesh,
        in_specs=placed,
        out_specs=P(("group", "rep"), "seq", None),
        check_vma=False,
    )
```
